32 devices in a mesh: fsdp: 32 (over z, y, x, core).
Axes of the slice: x: 2, y: 2, z: 4, core: 2. Of those that a mesh axis runs over, the one named last changes fastest.
Arguments:
- frames_in: bfloat16 [4096, 1024], P('fsdp'), may hold values from -6 to 6
- segment_ids: int32 [4096], P('fsdp'), may hold values from 0 to 1, as said below
- gain_attn: bfloat16 [8192], P('fsdp'), may hold values from 0.099609375 to 1.8984375
- w_qkv: bfloat16 [8192, 3072], P('fsdp'), may hold values from -0.1875 to 0.1875
- w_out: bfloat16 [8192, 1024], P('fsdp'), may hold values from -0.375 to 0.375
- gain_ffn: bfloat16 [8192], P('fsdp'), may hold values from 0.099609375 to 1.8984375
- w_gate_up: bfloat16 [8192, 5632], P('fsdp'), may hold values from -0.1875 to 0.1875
- w_down: bfloat16 [22528, 1024], P('fsdp'), may hold values from -0.109375 to 0.109375
- cotangent: bfloat16 [4096, 1024], P('fsdp'), may hold values from -6 to 6
Outputs:
- block_out: bfloat16 [4096, 1024], P('fsdp')
- grad_in: float32 [4096, 1024], P('fsdp')
- grad_gain_attn: float32 [8192], P('fsdp')
- grad_w_qkv: float32 [8192, 3072], P('fsdp')
- grad_w_out: float32 [8192, 1024], P('fsdp')
- grad_gain_ffn: float32 [8192], P('fsdp')
- grad_w_gate_up: float32 [8192, 5632], P('fsdp')
- grad_w_down: float32 [22528, 1024], P('fsdp')
The draws below stay inside these ranges and needn't reach their ends.
Inputs may be any that keep to these rules, and one draw needn't show every extreme that they name: `segment_ids`: within each frame of 8 tokens the ids are 1 on a leading run of 1 to 8 tokens and 0 on the rest.
All inputs are finite; a program needn't handle non-finite values.
Results may differ from the reference program's by a relative error of at most 0.01.
Values may be sent and summed in bfloat16 or wider, within the bound.
No kernel may reach another device: no remote copies, remote signals or barrier semaphores. Data moves between devices by JAX's collectives and lax.ppermute only.
A program may use at most 192 MiB of HBM per device.

```python
import math
import jax
import jax.numpy as jnp
from jax import lax

D = 1024
FF = 2816
HEADS = 16
HEAD_DIM = 64
POS = 8
FRAMES = 512
TOKENS = 4096


def draw_segment_ids(key, part):
    lengths = jax.random.randint(key, (FRAMES, 1), 1, POS + 1)
    position = jnp.arange(POS, dtype=jnp.int32)[None, :]
    return (position < lengths).astype(jnp.int32).reshape(FRAMES * POS)


def shard_levels(rng, shape, split, smallest, largest):
    level = 1.0
    for dim, blocks in split:
        heights = jax.random.uniform(jax.random.fold_in(jax.random.fold_in(rng, 6), dim), (blocks,), jnp.float32, smallest / len(split), largest / len(split))
        level = level * jnp.repeat(jnp.exp(heights), shape[dim] // blocks).reshape((-1,) + (1,) * (len(shape) - 1 - dim))
    return level


def noise(key, dims, width, most, pieces=(), kind=jnp.bfloat16):
    values = width * jax.random.normal(key, dims, jnp.float32)
    if pieces:
        values = values * shard_levels(key, dims, pieces, -0.22, 0.18)
    return jnp.clip(values, -most, most).astype(kind)


def setup_inputs(seed: int = 0) -> dict:
    splits = jax.random.split(jax.random.key(seed), 10)
    return {
        "frames_in": noise(splits[0], (TOKENS, D), 1.0, 6.0, ((0, 32),)),
        "segment_ids": draw_segment_ids(jax.random.fold_in(splits[9], 71), 0),
        "gain_attn": jnp.clip(1.0 + 0.18 * jax.random.normal(splits[2], (POS * D,), jnp.float32), 0.099609375, 1.8984375).astype(jnp.bfloat16),
        "w_qkv": noise(splits[3], (POS * D, 3 * D), D ** -0.5, 0.1875, ((0, 32),)),
        "w_out": noise(splits[4], (POS * D, D), (D // 4) ** -0.5, 0.375, ((0, 32),)),
        "gain_ffn": jnp.clip(1.0 + 0.18 * jax.random.normal(splits[5], (POS * D,), jnp.float32), 0.099609375, 1.8984375).astype(jnp.bfloat16),
        "w_gate_up": noise(splits[6], (POS * D, 2 * FF), D ** -0.5, 0.1875, ((0, 32),)),
        "w_down": noise(splits[7], (POS * FF, D), FF ** -0.5, 0.109375, ((0, 32),)),
        "cotangent": noise(splits[8], (TOKENS, D), 1.0, 6.0, ((0, 32),)),
    }


EPSILON = 1e-05

@jax.custom_vjp
def low(v):
    return lax.optimization_barrier(v.astype(jnp.bfloat16)).astype(jnp.float32)

@jax.custom_vjp
def low_back(v):
    return v

def low_keep(v):
    return (low(v), None)

def low_pass(kept, grad):
    return (grad,)

def back_keep(v):
    return (v, None)

def back_low(kept, grad):
    return (low(grad),)
low.defvjp(low_keep, low_pass)
low_back.defvjp(back_keep, back_low)

def normalize(vectors):
    return vectors * lax.rsqrt(lax.optimization_barrier(jnp.mean(vectors * vectors, axis=-1, keepdims=True)) + EPSILON)

def per_position(inputs, weights):
    return jnp.einsum('bpd,pde->bpe', inputs, weights, precision=lax.Precision.HIGHEST)

def block_forward(frames, validity, gain_attn, w_qkv, w_out, gain_ffn, w_gate_up, w_down):
    blocks = frames.shape[0]
    normed = low(normalize(frames) * gain_attn[None])
    project = low(low_back(per_position(normed, w_qkv)))
    split_heads = project.reshape(blocks, POS, 3, HEADS, HEAD_DIM)
    queries = split_heads[:, :, 0]
    key_rows = split_heads[:, :, 1]
    value_rows = split_heads[:, :, 2]
    scores = low_back(jnp.einsum('bqhd,bkhd->bhqk', queries, key_rows, precision=lax.Precision.HIGHEST) * HEAD_DIM ** (-0.5))
    position = jnp.arange(POS, dtype=jnp.int32)
    causal = position[None, :] <= position[:, None]
    same_segment = validity[:, :, None] == validity[:, None, :]
    allowed = (causal[None] & same_segment)[:, None]
    scores = jnp.where(allowed, scores, -jnp.inf)
    attn_probs = low(jax.nn.softmax(scores, axis=-1))
    attended = jnp.einsum('bhqk,bkhd->bqhd', attn_probs, value_rows, precision=lax.Precision.HIGHEST).reshape(blocks, POS, D)
    mixed_heads = low(low_back(attended))
    residual = frames + low_back(per_position(mixed_heads, w_out))
    normed_ffn = low(normalize(residual) * gain_ffn[None])
    gate_up = low_back(per_position(normed_ffn, w_gate_up))
    hidden = low(jax.nn.silu(gate_up[..., :FF]) * gate_up[..., FF:])
    return residual + low_back(per_position(hidden, w_down))

def reference(frames_in, segment_ids, gain_attn, w_qkv, w_out, gain_ffn, w_gate_up, w_down, cotangent):
    params = (gain_attn.astype(jnp.float32).reshape(POS, D), w_qkv.astype(jnp.float32).reshape(POS, D, 3 * D), w_out.astype(jnp.float32).reshape(POS, D, D), gain_ffn.astype(jnp.float32).reshape(POS, D), w_gate_up.astype(jnp.float32).reshape(POS, D, 2 * FF), w_down.astype(jnp.float32).reshape(POS, FF, D))
    block_frames = math.gcd(FRAMES, 256)
    block_count = FRAMES // block_frames
    inputs = frames_in.astype(jnp.float32).reshape(block_count, block_frames, POS, D)
    validity = segment_ids.reshape(block_count, block_frames, POS)
    cotangents = cotangent.astype(jnp.float32).reshape(block_count, block_frames, POS, D)

    def visit(totals, sliced):
        frames, valid_ids, upstream = sliced

        def forward(block_in, *weights):
            return block_forward(block_in, valid_ids, *weights)
        block_result, pullback = jax.vjp(forward, frames, *params)
        gradients = pullback(upstream)
        summed = tuple((running + update for running, update in zip(totals, gradients[1:])))
        return (summed, (block_result, gradients[0]))
    initial = tuple((jnp.zeros_like(weight) for weight in params))
    totals, (outputs, input_grads) = lax.scan(visit, initial, (inputs, validity, cotangents))
    return (outputs.reshape(TOKENS, D).astype(jnp.bfloat16), input_grads.reshape(TOKENS, D), totals[0].reshape(POS * D), totals[1].reshape(POS * D, 3 * D), totals[2].reshape(POS * D, D), totals[3].reshape(POS * D), totals[4].reshape(POS * D, 2 * FF), totals[5].reshape(POS * FF, D))
```

```python
import jax
import jax.numpy as jnp
from jax import lax
from jax.sharding import PartitionSpec as P

D = 1024
FF = 2816
HEADS = 16
HEAD_DIM = 64
POS = 8


EPSILON = 1e-05


def for_sending(array):

    def short(part):
        return part.astype(jnp.bfloat16) if part.dtype == jnp.float32 else part

    return jax.tree.map(short, array)


def swapped(block, axis, stride):
    count = lax.axis_size(axis)
    route = []
    for low in range(count):
        high = low | 1 << stride
        if high != low and high < count:
            route += [(low, high), (high, low)]
    return lax.ppermute(block, axis, route)


def positions_layout(frame_rows, groups):
    width = frame_rows.shape[-1]
    per_piece = frame_rows.shape[0] // POS // groups
    shaped = frame_rows.reshape(groups, per_piece, POS, width).transpose(2, 0, 1, 3)
    return shaped.reshape(POS * groups, per_piece, width)


def frames_layout(piece_rows, groups):
    width = piece_rows.shape[-1]
    per_piece = piece_rows.shape[1]
    shaped = piece_rows.reshape(POS, groups, per_piece, width).transpose(1, 2, 0, 3)
    return shaped.reshape(groups * per_piece * POS, width)


def inner_rows(left, right):
    return lax.dot_general(
        left, right, (((0,), (0,)), ((), ())), preferred_element_type=jnp.float32
    )


def times_transposed(left, right):
    return lax.dot_general(
        left, right, (((1,), (1,)), ((), ())), preferred_element_type=jnp.float32
    )


def join_pieces(current, partner, member, bit_level):
    upper_half = member >> bit_level & 1 == 1
    return tuple(
        (
            jnp.where(
                upper_half,
                jnp.concatenate([theirs, own_piece], 0),
                jnp.concatenate([own_piece, theirs], 0),
            )
            for own_piece, theirs in zip(current, partner)
        )
    )


def collect_forward(pieces, member, levels):
    current = pieces
    for bit_level in range(levels):
        partner = jax.tree.map(
            lambda part, own: part.astype(own.dtype),
            swapped(for_sending(current), "fsdp", bit_level),
            current,
        )
        current = join_pieces(current, partner, member, bit_level)
    return current


def collect_again(pieces, member, levels):
    current = pieces
    for bit_level in range(levels):
        partner = jax.tree.map(
            lambda part, own: part.astype(own.dtype),
            swapped(for_sending(current), "fsdp", bit_level),
            current,
        )
        current = join_pieces(current, partner, member, bit_level)
    return current


def halving_sum(terms, member, levels, sender):
    current = terms
    for bit_level in reversed(range(levels)):
        upper_half = member >> bit_level & 1 == 1
        leaving = tuple(
            (
                jnp.where(
                    upper_half,
                    term_part[: term_part.shape[0] // 2],
                    term_part[term_part.shape[0] // 2 :],
                )
                for term_part in current
            )
        )
        staying = tuple(
            (
                jnp.where(
                    upper_half,
                    term_part[term_part.shape[0] // 2 :],
                    term_part[: term_part.shape[0] // 2],
                )
                for term_part in current
            )
        )
        arrived = sender(leaving, bit_level)
        current = tuple((held_part + come_part for held_part, come_part in zip(staying, arrived)))
    return current


def send_whole(parts, bit_level):
    return jax.tree.map(
        lambda part, own: part.astype(own.dtype),
        swapped(for_sending(parts), "fsdp", bit_level),
        parts,
    )


def permitted(validity):
    row_place = lax.broadcasted_iota(jnp.int32, (POS, POS), 0)
    column_place = lax.broadcasted_iota(jnp.int32, (POS, POS), 1)
    causal = column_place <= row_place
    same_segment = validity[:, :, None] == validity[:, None, :]
    return (causal[None] & same_segment)[:, None]


def split_projections(qkv_frames):
    frames = qkv_frames.shape[0] // POS
    shaped = qkv_frames.reshape(frames, POS, 3, HEADS, HEAD_DIM)
    return (shaped[:, :, 0], shaped[:, :, 1], shaped[:, :, 2])


def masked_scores(queries, key_rows, allowed):
    scores = jnp.einsum(
        "fqhd,fkhd->fhqk", queries, key_rows, preferred_element_type=jnp.float32
    ) * HEAD_DIM ** (-0.5)
    return jnp.where(allowed, scores, -jnp.inf)


def attend(qkv_frames, validity):
    queries, key_rows, value_rows = split_projections(qkv_frames)
    scores = masked_scores(queries, key_rows, permitted(validity))
    highest = jnp.max(scores, axis=-1, keepdims=True)
    raised = jnp.exp(scores - highest)
    totals = jnp.sum(raised, axis=-1, keepdims=True)
    attn_probs = (raised / totals).astype(jnp.bfloat16)
    attended = jnp.einsum(
        "fhqk,fkhd->fqhd", attn_probs, value_rows, preferred_element_type=jnp.float32
    )
    mixed_heads = attended.reshape(qkv_frames.shape[0], D).astype(jnp.bfloat16)
    return (mixed_heads, highest + jnp.log(totals))


def attend_back(qkv_frames, validity, log_total, d_mixed):
    queries, key_rows, value_rows = split_projections(qkv_frames)
    frames = queries.shape[0]
    scores = masked_scores(queries, key_rows, permitted(validity))
    weights_full = jnp.exp(scores - log_total)
    attn_probs = weights_full.astype(jnp.bfloat16)
    d_heads = d_mixed.reshape(frames, POS, HEADS, HEAD_DIM)
    d_probs = jnp.einsum("fqhd,fkhd->fhqk", d_heads, value_rows, preferred_element_type=jnp.float32)
    d_values = jnp.einsum(
        "fhqk,fqhd->fkhd", attn_probs, d_heads, preferred_element_type=jnp.float32
    )
    d_scores = weights_full * (d_probs - jnp.sum(d_probs * weights_full, axis=-1, keepdims=True))
    d_scores = d_scores.astype(jnp.bfloat16)
    d_queries = jnp.einsum(
        "fhqk,fkhd->fqhd", d_scores, key_rows, preferred_element_type=jnp.float32
    ) * HEAD_DIM ** (-0.5)
    d_keys = jnp.einsum(
        "fhqk,fqhd->fkhd", d_scores, queries, preferred_element_type=jnp.float32
    ) * HEAD_DIM ** (-0.5)
    stacked = jnp.stack([d_queries, d_keys, d_values], axis=2)
    return stacked.reshape(frames * POS, 3 * D).astype(jnp.bfloat16)


def body(frames_in, segment_ids, gain_attn, w_qkv, w_out, gain_ffn, w_gate_up, w_down, cotangent):
    devices = lax.axis_size("fsdp")
    groups = devices // POS
    levels = groups.bit_length() - 1
    member = lax.axis_index("fsdp") % groups
    per_piece = frames_in.shape[0] // POS // groups
    validity = segment_ids.reshape(-1, POS)
    moved_input, moved_cotangent = (
        lax.all_to_all(
            positions_layout(frames_in, groups), "fsdp", split_axis=0, concat_axis=0, tiled=True
        ),
        lax.all_to_all(
            positions_layout(cotangent, groups), "fsdp", split_axis=0, concat_axis=0, tiled=True
        ),
    )
    inputs = moved_input.reshape(-1, D).astype(jnp.float32)
    upstream = moved_cotangent.reshape(-1, D)
    own_pieces = (w_qkv, w_out, w_gate_up, w_down, gain_attn, gain_ffn)
    collected = collect_forward(own_pieces, member, levels)
    whole_qkv, whole_out, whole_gate_up, whole_down, whole_gain_attn, whole_gain_ffn = collected
    gain_first = whole_gain_attn.astype(jnp.float32)
    gain_second = whole_gain_ffn.astype(jnp.float32)
    scale_first = lax.rsqrt(jnp.mean(inputs * inputs, axis=-1, keepdims=True) + EPSILON)
    normed_first = inputs * scale_first
    lowered_first = (normed_first * gain_first).astype(jnp.bfloat16)
    projected = jnp.dot(lowered_first, whole_qkv, preferred_element_type=jnp.float32).astype(
        jnp.bfloat16
    )
    qkv_frames = frames_layout(
        lax.all_to_all(
            projected.reshape(devices, per_piece, 3 * D),
            "fsdp",
            split_axis=0,
            concat_axis=0,
            tiled=True,
        ),
        groups,
    )
    mixed_frames, log_total = attend(qkv_frames, validity)
    mixed_rows = lax.all_to_all(
        positions_layout(mixed_frames, groups), "fsdp", split_axis=0, concat_axis=0, tiled=True
    ).reshape(-1, D)
    residual = inputs + jnp.dot(mixed_rows, whole_out, preferred_element_type=jnp.float32)
    scale_second = lax.rsqrt(jnp.mean(residual * residual, axis=-1, keepdims=True) + EPSILON)
    normed_second = residual * scale_second
    lowered_second = (normed_second * gain_second).astype(jnp.bfloat16)
    gate_up = jnp.dot(lowered_second, whole_gate_up, preferred_element_type=jnp.float32)
    gate_part = gate_up[:, :FF]
    up_part = gate_up[:, FF:]
    sigmoid_gate = jax.nn.sigmoid(gate_part)
    activated = gate_part * sigmoid_gate
    hidden = (activated * up_part).astype(jnp.bfloat16)
    result_rows = (
        residual + jnp.dot(hidden, whole_down, preferred_element_type=jnp.float32)
    ).astype(jnp.bfloat16)
    block_out = frames_layout(
        lax.all_to_all(
            result_rows.reshape(devices, per_piece, D),
            "fsdp",
            split_axis=0,
            concat_axis=0,
            tiled=True,
        ),
        groups,
    )
    collected = collect_again(own_pieces, member, levels)
    whole_qkv, whole_out, whole_gate_up, whole_down, whole_gain_attn, whole_gain_ffn = collected
    gain_first = whole_gain_attn.astype(jnp.float32)
    gain_second = whole_gain_ffn.astype(jnp.float32)
    grad_down_term = inner_rows(hidden, upstream)
    d_hidden = times_transposed(upstream, whole_down)
    d_gate = d_hidden * up_part * sigmoid_gate * (1.0 + gate_part * (1.0 - sigmoid_gate))
    d_up = d_hidden * activated
    d_gate_up = jnp.concatenate([d_gate, d_up], axis=1).astype(jnp.bfloat16)
    grad_gate_up_term = inner_rows(lowered_second, d_gate_up)
    d_second = times_transposed(d_gate_up, whole_gate_up)
    grad_gain_ffn_term = jnp.sum(d_second * normed_second, axis=0)
    scaled_second = d_second * gain_second
    d_residual = upstream.astype(jnp.float32) + scale_second * (
        scaled_second
        - normed_second * jnp.mean(scaled_second * normed_second, axis=-1, keepdims=True)
    )
    d_branch = d_residual.astype(jnp.bfloat16)
    grad_out_term = inner_rows(mixed_rows, d_branch)
    d_mixed = times_transposed(d_branch, whole_out).astype(jnp.bfloat16)
    d_mixed_frames = frames_layout(
        lax.all_to_all(
            d_mixed.reshape(devices, per_piece, D), "fsdp", split_axis=0, concat_axis=0, tiled=True
        ),
        groups,
    )
    d_qkv_frames = attend_back(qkv_frames, validity, log_total, d_mixed_frames)
    d_projected = lax.all_to_all(
        positions_layout(d_qkv_frames, groups), "fsdp", split_axis=0, concat_axis=0, tiled=True
    ).reshape(-1, 3 * D)
    grad_qkv_term = inner_rows(lowered_first, d_projected)
    d_first = times_transposed(d_projected, whole_qkv)
    grad_gain_attn_term = jnp.sum(d_first * normed_first, axis=0)
    scaled_first = d_first * gain_first
    d_inputs = d_residual + scale_first * (
        scaled_first - normed_first * jnp.mean(scaled_first * normed_first, axis=-1, keepdims=True)
    )
    grad_in = frames_layout(
        lax.all_to_all(
            d_inputs.reshape(devices, per_piece, D).astype(jnp.bfloat16),
            "fsdp",
            split_axis=0,
            concat_axis=0,
            tiled=True,
        ).astype(jnp.float32),
        groups,
    )
    shares = halving_sum(
        (
            grad_qkv_term,
            grad_out_term,
            grad_gate_up_term,
            grad_down_term,
            grad_gain_attn_term,
            grad_gain_ffn_term,
        ),
        member,
        levels,
        send_whole,
    )
    return (block_out, grad_in, shares[4], shares[0], shares[1], shares[5], shares[2], shares[3])

def swap(block, mask):
    count = lax.axis_size("fsdp")
    return lax.ppermute(block, "fsdp", [(i, i ^ mask) for i in range(count)])


def exchange(blocks):
    count = lax.axis_size("fsdp")
    stride = count // POS
    lanes = [[r + stride * k for k in range(POS)] for r in range(stride)]
    return lax.all_to_all(
        blocks, "fsdp", split_axis=0, concat_axis=0, tiled=True, axis_index_groups=lanes
    )


def to_positions(rows):
    return rows.reshape(-1, POS, rows.shape[-1]).transpose(1, 0, 2)


def to_frames(blocks):
    return blocks.transpose(1, 0, 2).reshape(-1, blocks.shape[-1])


def in_member_order(own, far, near, across, member):
    ranked = jnp.stack([own, near, far, across])
    return jnp.take(ranked, jnp.arange(4) ^ member, axis=0).reshape((-1,) + own.shape[1:])


def chip_order(own, near, core):
    return jnp.where(
        core == 0, jnp.concatenate([own, near], 0), jnp.concatenate([near, own], 0)
    )


def gathered_halves(weight, parts, side, member):
    width = weight.shape[1] // parts // 2
    shaped = weight.reshape(weight.shape[0], parts, 2, width)
    kept = lax.dynamic_index_in_dim(shaped, side, 2, keepdims=False).reshape(-1, parts * width)
    leaving = lax.dynamic_index_in_dim(shaped, 1 - side, 2, keepdims=False).reshape(
        -1, parts * width
    )
    far = swap(leaving, 2)
    rest = swap(jnp.stack([kept, far]), 1)
    return in_member_order(kept, far, rest[0], rest[1], member)


def attn_masks(validity):
    place = lax.broadcasted_iota(jnp.int32, validity.shape, 1)
    frame = lax.broadcasted_iota(jnp.int32, validity.shape, 2)
    flat = lambda a: a.reshape(2, -1)
    ids, place, frame = flat(validity), flat(place), flat(frame)
    same = lambda a: a[:, :, None] == a[:, None, :]
    return same(ids) & same(frame) & (place[:, None, :] <= place[:, :, None])


def heads_of(blocks):
    pieces = blocks.transpose(1, 0, 2, 3).reshape(2, -1, 3, blocks.shape[-1] // 3 // HEAD_DIM, HEAD_DIM)
    return pieces[:, :, 0], pieces[:, :, 1], pieces[:, :, 2]


def dense_probs(queries, key_rows, masks):
    scores = jnp.einsum(
        "rqhd,rkhd->rhqk", queries, key_rows, preferred_element_type=jnp.float32
    ) * HEAD_DIM ** (-0.5)
    scores = jnp.where(masks[:, None], scores, -jnp.inf)
    raised = jnp.exp(scores - jnp.max(scores, -1, keepdims=True))
    return raised / jnp.sum(raised, -1, keepdims=True)


def from_heads(rows, frames):
    return rows.reshape(2, POS, frames, -1).transpose(1, 0, 2, 3).astype(jnp.bfloat16)


def attend_dense(qkv_blocks, masks):
    queries, key_rows, value_rows = heads_of(qkv_blocks)
    probs = dense_probs(queries, key_rows, masks).astype(jnp.bfloat16)
    mixed = jnp.einsum("rhqk,rkhd->rqhd", probs, value_rows, preferred_element_type=jnp.float32)
    return from_heads(mixed, qkv_blocks.shape[2])


def attend_dense_back(qkv_blocks, masks, d_mixed_blocks):
    queries, key_rows, value_rows = heads_of(qkv_blocks)
    probs = dense_probs(queries, key_rows, masks)
    d_heads = d_mixed_blocks.transpose(1, 0, 2, 3).reshape(queries.shape)
    lowered = probs.astype(jnp.bfloat16)
    dot = lambda spec, a, b: jnp.einsum(spec, a, b, preferred_element_type=jnp.float32)
    d_probs = dot("rqhd,rkhd->rhqk", d_heads, value_rows)
    d_values = dot("rhqk,rqhd->rkhd", lowered, d_heads)
    d_scores = (probs * (d_probs - jnp.sum(d_probs * probs, -1, keepdims=True))).astype(jnp.bfloat16)
    d_queries = dot("rhqk,rkhd->rqhd", d_scores, key_rows) * HEAD_DIM ** (-0.5)
    d_keys = dot("rhqk,rqhd->rkhd", d_scores, queries) * HEAD_DIM ** (-0.5)
    return from_heads(jnp.stack([d_queries, d_keys, d_values], 2), qkv_blocks.shape[2])


def owned_columns(rows, member, width):
    return lax.dynamic_slice_in_dim(rows, member * width, width, 1)


def rows_to_blocks(rows):
    width = rows.shape[-1]
    return rows.reshape(2, POS, -1, width).transpose(1, 0, 2, 3).reshape(POS, -1, width)


def blocks_to_rows(blocks):
    width = blocks.shape[-1]
    return blocks.reshape(POS, 2, -1, width).transpose(1, 0, 2, 3).reshape(-1, width)


def turned(rows):
    half = rows.shape[0] // 2
    return jnp.concatenate([rows[half:], rows[:half]], 0)


def column_halves_gradient(left, right, parts, side, member, width):
    far_member = member ^ 2
    leaving = inner_rows(owned_columns(left, far_member, width), right).astype(jnp.bfloat16)
    own = inner_rows(owned_columns(left, member, width), right)
    come = swap(leaving, 2).astype(jnp.float32)
    own, come = (a.reshape(width, parts, 1, -1) for a in (own, come))
    joined = jnp.where(
        side == 0, jnp.concatenate([own, come], 2), jnp.concatenate([come, own], 2)
    )
    return joined.reshape(width, -1)


def pair_body(frames_in, segment_ids, gain_attn, w_qkv, w_out, gain_ffn, w_gate_up, w_down, cotangent):
    member = lax.axis_index("fsdp") % 4
    side, core = member >> 1, member & 1
    frames = frames_in.shape[0] // POS
    half = POS * frames
    width = w_qkv.shape[0]

    x_own = exchange(to_positions(frames_in)).reshape(half, D)
    x_rows = jnp.concatenate([x_own, swap(x_own, 2)], 0).astype(jnp.float32)
    c_own = exchange(to_positions(cotangent)).reshape(half, D)
    upstream = jnp.concatenate([c_own, swap(c_own, 2)], 0)
    ids_own = segment_ids.reshape(frames, POS).T
    masks = attn_masks(jnp.stack([ids_own, swap(ids_own, 2)]))

    gains = jnp.stack([gain_attn, gain_ffn], 1)
    gains_far = swap(gains, 2)
    gains_rest = swap(jnp.stack([gains, gains_far]), 1)
    gains = in_member_order(gains, gains_far, gains_rest[0], gains_rest[1], member).astype(jnp.float32)
    gain_first, gain_second = gains[:, 0], gains[:, 1]
    half_qkv = gathered_halves(w_qkv, 3, side, member)
    half_gate_up = gathered_halves(w_gate_up, 2, side, member)
    half_out = chip_order(w_out, swap(w_out, 1), core)
    half_down = chip_order(w_down, swap(w_down, 1), core)

    scale_first = lax.rsqrt(jnp.mean(x_rows * x_rows, -1, keepdims=True) + EPSILON)
    normed_first = x_rows * scale_first
    lowered_first = (normed_first * gain_first).astype(jnp.bfloat16)
    projected = jnp.dot(lowered_first, half_qkv, preferred_element_type=jnp.float32).astype(jnp.bfloat16)
    qkv_blocks = exchange(rows_to_blocks(projected)).reshape(POS, 2, frames, -1)
    mixed_blocks = attend_dense(qkv_blocks, masks).reshape(POS, 2 * frames, -1)
    mixed_rows = blocks_to_rows(exchange(mixed_blocks))

    out_term = jnp.dot(mixed_rows, half_out, preferred_element_type=jnp.float32)
    out_far = turned(swap(out_term.astype(jnp.bfloat16), 2)).astype(jnp.float32)
    residual = x_rows + (out_term + out_far)
    scale_second = lax.rsqrt(jnp.mean(residual * residual, -1, keepdims=True) + EPSILON)
    normed_second = residual * scale_second
    lowered_second = (normed_second * gain_second).astype(jnp.bfloat16)
    gate_up = jnp.dot(lowered_second, half_gate_up, preferred_element_type=jnp.float32)
    gate_part, up_part = jnp.split(gate_up, 2, 1)
    sigmoid_gate = jax.nn.sigmoid(gate_part)
    activated = gate_part * sigmoid_gate
    hidden = (activated * up_part).astype(jnp.bfloat16)
    down_term = jnp.dot(hidden, half_down, preferred_element_type=jnp.float32)
    down_far = swap(down_term[half:].astype(jnp.bfloat16), 2).astype(jnp.float32)
    result = (residual[:half] + (down_term[:half] + down_far)).astype(jnp.bfloat16)
    block_out = to_frames(exchange(result.reshape(POS, frames, D)))

    d_hidden = times_transposed(upstream, half_down)
    d_gate = d_hidden * up_part * sigmoid_gate * (1.0 + gate_part * (1.0 - sigmoid_gate))
    d_gate_up = jnp.concatenate([d_gate, d_hidden * activated], 1).astype(jnp.bfloat16)
    second_term = times_transposed(d_gate_up, half_gate_up)
    second_far = turned(swap(second_term.astype(jnp.bfloat16), 2)).astype(jnp.float32)
    d_second = second_term + second_far
    gain_ffn_term = jnp.sum(d_second * normed_second, 0)
    scaled_second = d_second * gain_second
    d_residual = upstream.astype(jnp.float32) + scale_second * (
        scaled_second
        - normed_second * jnp.mean(scaled_second * normed_second, -1, keepdims=True)
    )
    d_branch = d_residual.astype(jnp.bfloat16)
    d_mixed = times_transposed(d_branch, half_out).astype(jnp.bfloat16)
    d_mixed_blocks = exchange(rows_to_blocks(d_mixed)).reshape(POS, 2, frames, -1)
    d_qkv_blocks = attend_dense_back(qkv_blocks, masks, d_mixed_blocks)
    d_projected = blocks_to_rows(exchange(d_qkv_blocks.reshape(POS, 2 * frames, -1)))
    first_term = times_transposed(d_projected, half_qkv)
    first_far = swap(first_term[half:].astype(jnp.bfloat16), 2).astype(jnp.float32)
    d_first = first_term[:half] + first_far
    normed, scale = normed_first[:half], scale_first[:half]
    gain_attn_term = jnp.sum(d_first * normed, 0)
    scaled_first = d_first * gain_first
    d_inputs = d_residual[:half] + scale * (
        scaled_first - normed * jnp.mean(scaled_first * normed, -1, keepdims=True)
    )
    grad_in = to_frames(
        exchange(d_inputs.astype(jnp.bfloat16).reshape(POS, frames, D))
    ).astype(jnp.float32)

    both = lambda rows: jnp.concatenate([rows, swap(rows, 1)], 0)
    all_hidden = both(hidden).reshape(-1, 2, w_down.shape[0])
    grad_down = inner_rows(
        lax.dynamic_index_in_dim(all_hidden, core, 1, keepdims=False), both(upstream)
    )
    grad_gate_up = column_halves_gradient(
        both(lowered_second), both(d_gate_up), 2, side, member, width
    )
    grad_out = inner_rows(owned_columns(both(mixed_rows), core, width), both(d_branch))
    grad_qkv = column_halves_gradient(
        both(lowered_first), both(d_projected), 3, side, member, width
    )
    gain_ffn_sum = gain_ffn_term + swap(gain_ffn_term, 1)
    gain_attn_sum = gain_attn_term + swap(gain_attn_term, 1)
    gain_attn_sum = gain_attn_sum + swap(gain_attn_sum, 2)
    own_entries = lambda total: lax.dynamic_slice_in_dim(total, member * width, width, 0)
    return (
        block_out,
        grad_in,
        own_entries(gain_attn_sum),
        grad_qkv,
        grad_out,
        own_entries(gain_ffn_sum),
        grad_gate_up,
        grad_down,
    )


def solution(mesh):
    in_specs = (
        P("fsdp", None),
        P("fsdp"),
        P("fsdp"),
        P("fsdp", None),
        P("fsdp", None),
        P("fsdp"),
        P("fsdp", None),
        P("fsdp", None),
        P("fsdp", None),
    )
    out_specs = (
        P("fsdp", None),
        P("fsdp", None),
        P("fsdp"),
        P("fsdp", None),
        P("fsdp", None),
        P("fsdp"),
        P("fsdp", None),
        P("fsdp", None),
    )
    chosen = pair_body if mesh.shape["fsdp"] == 4 * POS else body
    return jax.shard_map(chosen, mesh=mesh, in_specs=in_specs, out_specs=out_specs, check_vma=False)
```

```python
import functools
import math

import jax
import jax.numpy as jnp
from jax import lax
from jax.experimental import pallas as pl
from jax.experimental.pallas import tpu as pltpu
from jax.sharding import PartitionSpec as P

D = 1024
FF = 2816
HEADS = 16
HEAD_DIM = 64
POS = 8


EPSILON = 1e-05


def for_sending(array):

    def short(part):
        return part.astype(jnp.bfloat16) if part.dtype == jnp.float32 else part

    return jax.tree.map(short, array)


def swapped(block, axis, stride):
    count = lax.axis_size(axis)
    route = []
    for low in range(count):
        high = low | 1 << stride
        if high != low and high < count:
            route += [(low, high), (high, low)]
    return lax.ppermute(block, axis, route)


def positions_layout(frame_rows, groups):
    width = frame_rows.shape[-1]
    per_piece = frame_rows.shape[0] // POS // groups
    shaped = frame_rows.reshape(groups, per_piece, POS, width).transpose(2, 0, 1, 3)
    return shaped.reshape(POS * groups, per_piece, width)


def frames_layout(piece_rows, groups):
    width = piece_rows.shape[-1]
    per_piece = piece_rows.shape[1]
    shaped = piece_rows.reshape(POS, groups, per_piece, width).transpose(1, 2, 0, 3)
    return shaped.reshape(groups * per_piece * POS, width)


def inner_rows(left, right):
    return lax.dot_general(
        left, right, (((0,), (0,)), ((), ())), preferred_element_type=jnp.float32
    )


def times_transposed(left, right):
    return lax.dot_general(
        left, right, (((1,), (1,)), ((), ())), preferred_element_type=jnp.float32
    )


def join_pieces(current, partner, member, bit_level):
    upper_half = member >> bit_level & 1 == 1
    return tuple(
        (
            jnp.where(
                upper_half,
                jnp.concatenate([theirs, own_piece], 0),
                jnp.concatenate([own_piece, theirs], 0),
            )
            for own_piece, theirs in zip(current, partner)
        )
    )


def collect_forward(pieces, member, levels):
    current = pieces
    for bit_level in range(levels):
        partner = jax.tree.map(
            lambda part, own: part.astype(own.dtype),
            swapped(for_sending(current), "fsdp", bit_level),
            current,
        )
        current = join_pieces(current, partner, member, bit_level)
    return current


def collect_again(pieces, member, levels):
    current = pieces
    for bit_level in range(levels):
        partner = jax.tree.map(
            lambda part, own: part.astype(own.dtype),
            swapped(for_sending(current), "fsdp", bit_level),
            current,
        )
        current = join_pieces(current, partner, member, bit_level)
    return current


def halving_sum(terms, member, levels, sender):
    current = terms
    for bit_level in reversed(range(levels)):
        upper_half = member >> bit_level & 1 == 1
        leaving = tuple(
            (
                jnp.where(
                    upper_half,
                    term_part[: term_part.shape[0] // 2],
                    term_part[term_part.shape[0] // 2 :],
                )
                for term_part in current
            )
        )
        staying = tuple(
            (
                jnp.where(
                    upper_half,
                    term_part[term_part.shape[0] // 2 :],
                    term_part[: term_part.shape[0] // 2],
                )
                for term_part in current
            )
        )
        arrived = sender(leaving, bit_level)
        current = tuple((held_part + come_part for held_part, come_part in zip(staying, arrived)))
    return current


def send_whole(parts, bit_level):
    return jax.tree.map(
        lambda part, own: part.astype(own.dtype),
        swapped(for_sending(parts), "fsdp", bit_level),
        parts,
    )


def permitted(validity):
    row_place = lax.broadcasted_iota(jnp.int32, (POS, POS), 0)
    column_place = lax.broadcasted_iota(jnp.int32, (POS, POS), 1)
    causal = column_place <= row_place
    same_segment = validity[:, :, None] == validity[:, None, :]
    return (causal[None] & same_segment)[:, None]


def split_projections(qkv_frames):
    frames = qkv_frames.shape[0] // POS
    shaped = qkv_frames.reshape(frames, POS, 3, HEADS, HEAD_DIM)
    return (shaped[:, :, 0], shaped[:, :, 1], shaped[:, :, 2])


def masked_scores(queries, key_rows, allowed):
    scores = jnp.einsum(
        "fqhd,fkhd->fhqk", queries, key_rows, preferred_element_type=jnp.float32
    ) * HEAD_DIM ** (-0.5)
    return jnp.where(allowed, scores, -jnp.inf)


def attend(qkv_frames, validity):
    queries, key_rows, value_rows = split_projections(qkv_frames)
    scores = masked_scores(queries, key_rows, permitted(validity))
    highest = jnp.max(scores, axis=-1, keepdims=True)
    raised = jnp.exp(scores - highest)
    totals = jnp.sum(raised, axis=-1, keepdims=True)
    attn_probs = (raised / totals).astype(jnp.bfloat16)
    attended = jnp.einsum(
        "fhqk,fkhd->fqhd", attn_probs, value_rows, preferred_element_type=jnp.float32
    )
    mixed_heads = attended.reshape(qkv_frames.shape[0], D).astype(jnp.bfloat16)
    return (mixed_heads, highest + jnp.log(totals))


def attend_back(qkv_frames, validity, log_total, d_mixed):
    queries, key_rows, value_rows = split_projections(qkv_frames)
    frames = queries.shape[0]
    scores = masked_scores(queries, key_rows, permitted(validity))
    weights_full = jnp.exp(scores - log_total)
    attn_probs = weights_full.astype(jnp.bfloat16)
    d_heads = d_mixed.reshape(frames, POS, HEADS, HEAD_DIM)
    d_probs = jnp.einsum("fqhd,fkhd->fhqk", d_heads, value_rows, preferred_element_type=jnp.float32)
    d_values = jnp.einsum(
        "fhqk,fqhd->fkhd", attn_probs, d_heads, preferred_element_type=jnp.float32
    )
    d_scores = weights_full * (d_probs - jnp.sum(d_probs * weights_full, axis=-1, keepdims=True))
    d_scores = d_scores.astype(jnp.bfloat16)
    d_queries = jnp.einsum(
        "fhqk,fkhd->fqhd", d_scores, key_rows, preferred_element_type=jnp.float32
    ) * HEAD_DIM ** (-0.5)
    d_keys = jnp.einsum(
        "fhqk,fqhd->fkhd", d_scores, queries, preferred_element_type=jnp.float32
    ) * HEAD_DIM ** (-0.5)
    stacked = jnp.stack([d_queries, d_keys, d_values], axis=2)
    return stacked.reshape(frames * POS, 3 * D).astype(jnp.bfloat16)


def body(frames_in, segment_ids, gain_attn, w_qkv, w_out, gain_ffn, w_gate_up, w_down, cotangent):
    devices = lax.axis_size("fsdp")
    groups = devices // POS
    levels = groups.bit_length() - 1
    member = lax.axis_index("fsdp") % groups
    per_piece = frames_in.shape[0] // POS // groups
    validity = segment_ids.reshape(-1, POS)
    moved_input, moved_cotangent = (
        lax.all_to_all(
            positions_layout(frames_in, groups), "fsdp", split_axis=0, concat_axis=0, tiled=True
        ),
        lax.all_to_all(
            positions_layout(cotangent, groups), "fsdp", split_axis=0, concat_axis=0, tiled=True
        ),
    )
    inputs = moved_input.reshape(-1, D).astype(jnp.float32)
    upstream = moved_cotangent.reshape(-1, D)
    own_pieces = (w_qkv, w_out, w_gate_up, w_down, gain_attn, gain_ffn)
    collected = collect_forward(own_pieces, member, levels)
    whole_qkv, whole_out, whole_gate_up, whole_down, whole_gain_attn, whole_gain_ffn = collected
    gain_first = whole_gain_attn.astype(jnp.float32)
    gain_second = whole_gain_ffn.astype(jnp.float32)
    scale_first = lax.rsqrt(jnp.mean(inputs * inputs, axis=-1, keepdims=True) + EPSILON)
    normed_first = inputs * scale_first
    lowered_first = (normed_first * gain_first).astype(jnp.bfloat16)
    projected = jnp.dot(lowered_first, whole_qkv, preferred_element_type=jnp.float32).astype(
        jnp.bfloat16
    )
    qkv_frames = frames_layout(
        lax.all_to_all(
            projected.reshape(devices, per_piece, 3 * D),
            "fsdp",
            split_axis=0,
            concat_axis=0,
            tiled=True,
        ),
        groups,
    )
    mixed_frames, log_total = attend(qkv_frames, validity)
    mixed_rows = lax.all_to_all(
        positions_layout(mixed_frames, groups), "fsdp", split_axis=0, concat_axis=0, tiled=True
    ).reshape(-1, D)
    residual = inputs + jnp.dot(mixed_rows, whole_out, preferred_element_type=jnp.float32)
    scale_second = lax.rsqrt(jnp.mean(residual * residual, axis=-1, keepdims=True) + EPSILON)
    normed_second = residual * scale_second
    lowered_second = (normed_second * gain_second).astype(jnp.bfloat16)
    gate_up = jnp.dot(lowered_second, whole_gate_up, preferred_element_type=jnp.float32)
    gate_part = gate_up[:, :FF]
    up_part = gate_up[:, FF:]
    sigmoid_gate = jax.nn.sigmoid(gate_part)
    activated = gate_part * sigmoid_gate
    hidden = (activated * up_part).astype(jnp.bfloat16)
    result_rows = (
        residual + jnp.dot(hidden, whole_down, preferred_element_type=jnp.float32)
    ).astype(jnp.bfloat16)
    block_out = frames_layout(
        lax.all_to_all(
            result_rows.reshape(devices, per_piece, D),
            "fsdp",
            split_axis=0,
            concat_axis=0,
            tiled=True,
        ),
        groups,
    )
    collected = collect_again(own_pieces, member, levels)
    whole_qkv, whole_out, whole_gate_up, whole_down, whole_gain_attn, whole_gain_ffn = collected
    gain_first = whole_gain_attn.astype(jnp.float32)
    gain_second = whole_gain_ffn.astype(jnp.float32)
    grad_down_term = inner_rows(hidden, upstream)
    d_hidden = times_transposed(upstream, whole_down)
    d_gate = d_hidden * up_part * sigmoid_gate * (1.0 + gate_part * (1.0 - sigmoid_gate))
    d_up = d_hidden * activated
    d_gate_up = jnp.concatenate([d_gate, d_up], axis=1).astype(jnp.bfloat16)
    grad_gate_up_term = inner_rows(lowered_second, d_gate_up)
    d_second = times_transposed(d_gate_up, whole_gate_up)
    grad_gain_ffn_term = jnp.sum(d_second * normed_second, axis=0)
    scaled_second = d_second * gain_second
    d_residual = upstream.astype(jnp.float32) + scale_second * (
        scaled_second
        - normed_second * jnp.mean(scaled_second * normed_second, axis=-1, keepdims=True)
    )
    d_branch = d_residual.astype(jnp.bfloat16)
    grad_out_term = inner_rows(mixed_rows, d_branch)
    d_mixed = times_transposed(d_branch, whole_out).astype(jnp.bfloat16)
    d_mixed_frames = frames_layout(
        lax.all_to_all(
            d_mixed.reshape(devices, per_piece, D), "fsdp", split_axis=0, concat_axis=0, tiled=True
        ),
        groups,
    )
    d_qkv_frames = attend_back(qkv_frames, validity, log_total, d_mixed_frames)
    d_projected = lax.all_to_all(
        positions_layout(d_qkv_frames, groups), "fsdp", split_axis=0, concat_axis=0, tiled=True
    ).reshape(-1, 3 * D)
    grad_qkv_term = inner_rows(lowered_first, d_projected)
    d_first = times_transposed(d_projected, whole_qkv)
    grad_gain_attn_term = jnp.sum(d_first * normed_first, axis=0)
    scaled_first = d_first * gain_first
    d_inputs = d_residual + scale_first * (
        scaled_first - normed_first * jnp.mean(scaled_first * normed_first, axis=-1, keepdims=True)
    )
    grad_in = frames_layout(
        lax.all_to_all(
            d_inputs.reshape(devices, per_piece, D).astype(jnp.bfloat16),
            "fsdp",
            split_axis=0,
            concat_axis=0,
            tiled=True,
        ).astype(jnp.float32),
        groups,
    )
    shares = halving_sum(
        (
            grad_qkv_term,
            grad_out_term,
            grad_gate_up_term,
            grad_down_term,
            grad_gain_attn_term,
            grad_gain_ffn_term,
        ),
        member,
        levels,
        send_whole,
    )
    return (block_out, grad_in, shares[4], shares[0], shares[1], shares[5], shares[2], shares[3])

VMEM = pl.BlockSpec(memory_space=pltpu.VMEM)
SMEM = pl.BlockSpec(memory_space=pltpu.SMEM)
HBM = pl.BlockSpec(memory_space=pl.ANY)
BF16 = jnp.bfloat16
F32 = jnp.float32
OWN, FAR, NEAR, ACROSS, SIDE, CORE, POSITION = range(7)


def swap(block, mask):
    count = lax.axis_size("fsdp")
    return lax.ppermute(block, "fsdp", [(i, i ^ mask) for i in range(count)])


def exchange(blocks):
    stride = lax.axis_size("fsdp") // POS
    return [blocks[0]] + [swap(blocks[k], stride * k) for k in range(1, POS)]


def kernel_call(kernel, name, args, outs, scratch=()):
    held = sum(
        math.prod(ref.shape) * jnp.dtype(ref.dtype).itemsize
        for ref in scratch
        if ref.memory_space == pltpu.VMEM
    )
    return pl.pallas_call(
        kernel,
        name=name,
        in_specs=[spec for spec, _ in args],
        out_specs=[VMEM] * len(outs),
        out_shape=[jax.ShapeDtypeStruct(s, d) for s, d in outs],
        scratch_shapes=list(scratch),
        cost_estimate=pl.CostEstimate(flops=1, bytes_accessed=1, transcendentals=0),
        compiler_params=pltpu.CompilerParams(vmem_limit_bytes=held + (8 << 20)),
    )(*[a for _, a in args])


def matmul(left, right):
    return jnp.dot(left, right, preferred_element_type=F32)


def aligned(start, size, step=128):
    return pl.ds(pl.multiple_of(start, step), size)


def rows_of(refs, rel, columns=slice(None)):
    frames = refs[0].shape[0] // 2
    return jnp.concatenate([ref[rel * frames : (rel + 1) * frames, columns] for ref in refs], 0)


def put_rows(refs, rel, columns, value):
    frames = refs[0].shape[0] // 2
    for k, ref in enumerate(refs):
        ref[rel * frames : (rel + 1) * frames, columns] = value[k * frames : (k + 1) * frames]


def block_shapes(rows, width):
    return [((rows // POS, width), BF16)] * POS


def in_vmem(*arrays):
    return [(VMEM, a) for a in arrays]


def place_matrix(size, to_positions, position):
    frames = size // POS
    row = lax.broadcasted_iota(jnp.int32, (size, size), 0)
    column = lax.broadcasted_iota(jnp.int32, (size, size), 1)
    if not to_positions:
        row, column = column, row
    return (column == (row % frames) * POS + ((row // frames) ^ position)).astype(F32).astype(BF16)


def to_positions_kernel(place, x_rows, c_rows, *blocks):
    order = place_matrix(x_rows.shape[0], True, place[POSITION])
    for rel, rows in enumerate((x_rows, c_rows)):
        put_rows(blocks, rel, slice(None), matmul(order, rows[...]).astype(BF16))


def to_positions(place, x_rows, c_rows):
    size, width = x_rows.shape
    return kernel_call(
        to_positions_kernel,
        "to_positions",
        [(SMEM, place)] + in_vmem(x_rows, c_rows),
        block_shapes(2 * size, width),
    )


def collect_kernel(*refs):
    blocks, (x_own, c_own) = refs[:POS], refs[POS:]
    x_own[...] = rows_of(blocks, 0)
    c_own[...] = rows_of(blocks, 1)


def collect(blocks):
    rows, width = blocks[0].shape
    return kernel_call(
        collect_kernel, "collect", in_vmem(*blocks), [((rows * POS // 2, width), BF16)] * 2
    )


def to_frames_kernel(place, *refs):
    blocks, rows = refs[:POS], refs[POS:]
    order = place_matrix(rows[0].shape[0], False, place[POSITION])
    for rel in range(2):
        rows[rel][...] = matmul(order, rows_of(blocks, rel)).astype(rows[rel].dtype)


def to_frames(place, blocks):
    size = blocks[0].shape[0] * POS // 2
    return kernel_call(
        to_frames_kernel,
        "to_frames",
        [(SMEM, place)] + in_vmem(*blocks),
        [((size, D), F32), ((size, D), BF16)],
    )


def first_kernel(
    place, x_a, x_b, gains_own, gains_far, gains_near, gains_across, w_own, w_far, w_near, w_across,
    *rest,
):
    qkv, (lowered, gains, w, sems) = rest[:POS], rest[POS:]
    half, width = x_a.shape[0], w_own.shape[0]
    part = w.shape[1] // 3
    side = place[SIDE]
    at_rows = lambda rank: aligned(place[rank] * width, width)
    copies = [
        pltpu.make_async_copy(
            w_own.at[:, aligned((2 * k + side) * part, part)],
            w.at[at_rows(OWN), pl.ds(k * part, part)],
            sems.at[k],
        )
        for k in range(3)
    ]
    copies.append(pltpu.make_async_copy(w_far, w.at[at_rows(FAR)], sems.at[3]))
    copies.append(pltpu.make_async_copy(w_near, w.at[at_rows(NEAR)], sems.at[4]))
    copies.append(pltpu.make_async_copy(w_across, w.at[at_rows(ACROSS)], sems.at[5]))
    for copy in copies:
        copy.start()
    gains[:, at_rows(OWN)] = gains_own[...].astype(F32)
    gains[:, at_rows(FAR)] = gains_far[...].astype(F32)
    gains[:, at_rows(NEAR)] = gains_near[...].astype(F32)
    gains[:, at_rows(ACROSS)] = gains_across[...].astype(F32)
    gain = gains[0:1, :]
    for rel, ref in enumerate((x_a, x_b)):
        rows = ref[...].astype(F32)
        scale = lax.rsqrt(jnp.mean(rows * rows, axis=-1, keepdims=True) + EPSILON)
        lowered[rel * half : (rel + 1) * half, :] = (rows * scale * gain).astype(BF16)
    for copy in copies:
        copy.wait()

    def step(n, carry):
        columns = aligned(n * 256, 256, 256)
        value = matmul(lowered[...], w[:, columns]).astype(BF16)
        put_rows(qkv, 0, columns, value[:half])
        put_rows(qkv, 1, columns, value[half:])
        return carry

    lax.fori_loop(0, w.shape[1] // 256, step, 0)


def first(
    place, x_a, x_b, gains_own, gains_far, gains_near, gains_across, w_own, w_far, w_near, w_across
):
    half = x_a.shape[0]
    wide = w_far.shape[1]
    return kernel_call(
        first_kernel,
        "first",
        [(SMEM, place), (VMEM, x_a), (VMEM, x_b), (VMEM, gains_own), (VMEM, gains_far),
         (VMEM, gains_near), (VMEM, gains_across), (HBM, w_own), (HBM, w_far), (HBM, w_near),
         (HBM, w_across)],
        block_shapes(2 * half, wide) + [((2 * half, D), BF16), ((2, D), F32)],
        [pltpu.VMEM((D, wide), BF16), pltpu.SemaphoreType.DMA((6,))],
    )


def allowed_pairs(ids, position):
    size = ids.shape[1]
    frames = size // POS
    row = lax.broadcasted_iota(jnp.int32, (size, size), 0)
    column = lax.broadcasted_iota(jnp.int32, (size, size), 1)
    across = jnp.broadcast_to(ids.astype(F32), (size, size))
    same = (across == across.T) & (row % frames == column % frames)
    mask = same & ((column // frames) ^ position <= (row // frames) ^ position)
    return jnp.concatenate([mask, mask], 1)


def pair_of_heads(rows, low):
    return jnp.concatenate([rows * low, rows * (1 - low)], 0)


def lane_halves(value, reduce):
    size = value.shape[1] // 2
    parts = [
        jnp.broadcast_to(reduce(value[:, k * size : (k + 1) * size]), (value.shape[0], size))
        for k in range(2)
    ]
    return jnp.concatenate(parts, 1)


def pair_probs(query, key_pair, mask):
    scores = times_transposed(query, key_pair) * HEAD_DIM ** (-0.5)
    scores = jnp.where(mask, scores, -jnp.inf)
    raised = jnp.exp(scores - lane_halves(scores, lambda a: jnp.max(a, -1, keepdims=True)))
    return raised / lane_halves(raised, lambda a: jnp.sum(a, -1, keepdims=True))


def first_head_lanes():
    lane = lax.broadcasted_iota(jnp.int32, (1, 2 * HEAD_DIM), 1)
    return (lane < HEAD_DIM).astype(F32).astype(BF16)


def attend_kernel(place, ids_a, ids_b, *refs):
    qkv, mixed = refs[:POS], refs[POS:]
    part = mixed[0].shape[1]
    low = first_head_lanes()
    for rel, ids in enumerate((ids_a, ids_b)):
        mask = allowed_pairs(ids[...], place[POSITION])
        for base in range(0, part, 2 * HEAD_DIM):
            query, key_rows, value_rows = (
                rows_of(qkv, rel, slice(k * part + base, k * part + base + 2 * HEAD_DIM))
                for k in range(3)
            )
            probs = pair_probs(query, pair_of_heads(key_rows, low), mask)
            value = matmul(probs.astype(BF16), pair_of_heads(value_rows, low))
            put_rows(mixed, rel, slice(base, base + 2 * HEAD_DIM), value.astype(BF16))


def attend_local(place, ids_a, ids_b, qkv):
    rows, wide = qkv[0].shape
    return kernel_call(
        attend_kernel,
        "attend",
        [(SMEM, place)] + in_vmem(ids_a, ids_b, *qkv),
        block_shapes(rows * POS, wide // 3),
    )


def attend_back_kernel(place, ids_a, ids_b, *refs):
    qkv, d_mixed, d_qkv = refs[:POS], refs[POS : 2 * POS], refs[2 * POS :]
    part = d_mixed[0].shape[1]
    pair = 2 * HEAD_DIM
    low = first_head_lanes()
    size = POS * d_mixed[0].shape[0] // 2
    low_full = lax.broadcasted_iota(jnp.int32, (size, pair), 1) < HEAD_DIM
    scale = HEAD_DIM ** (-0.5)
    for rel, ids in enumerate((ids_a, ids_b)):
        mask = allowed_pairs(ids[...], place[POSITION])
        for base in range(0, part, pair):
            query, key_rows, value_rows = (
                rows_of(qkv, rel, slice(k * part + base, k * part + base + pair))
                for k in range(3)
            )
            d_rows = rows_of(d_mixed, rel, slice(base, base + pair))
            keys = pair_of_heads(key_rows, low)
            probs = pair_probs(query, keys, mask)
            d_probs = times_transposed(d_rows, pair_of_heads(value_rows, low))
            inner = lane_halves(d_probs * probs, lambda a: jnp.sum(a, -1, keepdims=True))
            d_scores = (probs * (d_probs - inner)).astype(BF16)
            d_query = matmul(d_scores, keys) * scale
            d_key = inner_rows(d_scores, query) * scale
            d_value = inner_rows(probs.astype(BF16), d_rows)
            d_key = jnp.where(low_full, d_key[:size], d_key[size:])
            d_value = jnp.where(low_full, d_value[:size], d_value[size:])
            for k, value in enumerate((d_query, d_key, d_value)):
                columns = slice(k * part + base, k * part + base + pair)
                put_rows(d_qkv, rel, columns, value.astype(BF16))


def attend_back_local(place, ids_a, ids_b, qkv, d_mixed):
    rows, wide = qkv[0].shape
    return kernel_call(
        attend_back_kernel,
        "attend_back",
        [(SMEM, place)] + in_vmem(ids_a, ids_b, *qkv, *d_mixed),
        block_shapes(rows * POS, wide),
    )


def chip_rows(place, own, near, whole, sems):
    count = own.shape[0]
    core = place[CORE]
    return [
        pltpu.make_async_copy(own, whole.at[aligned(core * count, count, 64)], sems.at[0]),
        pltpu.make_async_copy(near, whole.at[aligned((1 - core) * count, count, 64)], sems.at[1]),
    ]


def out_kernel(place, w_own, w_near, *refs):
    mixed, (term, leaving, mixed_rows, w, sems) = refs[:POS], refs[POS:]
    copies = chip_rows(place, w_own, w_near, w, sems)
    for copy in copies:
        copy.start()
    rows = jnp.concatenate([rows_of(mixed, 0), rows_of(mixed, 1)], 0)
    mixed_rows[...] = rows
    half = rows.shape[0] // 2
    for copy in copies:
        copy.wait()
    for base in range(0, D, 512):
        value = matmul(rows, w[:, base : base + 512])
        term[:, base : base + 512] = value
        lowered = value.astype(BF16)
        leaving[:half, base : base + 512] = lowered[half:]
        leaving[half:, base : base + 512] = lowered[:half]


def out_term(place, mixed, w_own, w_near):
    rows = POS * mixed[0].shape[0]
    inner = 2 * w_own.shape[0]
    return kernel_call(
        out_kernel,
        "out_term",
        [(SMEM, place), (HBM, w_own), (HBM, w_near)] + in_vmem(*mixed),
        [((rows, D), F32), ((rows, D), BF16), ((rows, inner), BF16)],
        [pltpu.VMEM((inner, D), BF16), pltpu.SemaphoreType.DMA((2,))],
    )


def ffn_kernel(
    place, x_a, x_b, term, far, gains, c_a, c_b, *rest
):
    pieces, (wd_own, wd_near) = (rest[:4], rest[4:8]), rest[8:10]
    resid, lowered, hidden, d_gate_up, second, leaving = rest[10:16]
    w, wd, upstream, sems, down_sems = rest[16:]
    half, width, steps = x_a.shape[0], pieces[0][0].shape[0], w.shape[0]
    split = pieces[0][0].shape[1] // 256

    def copies(j, sources, base):
        return [
            pltpu.make_async_copy(
                source.at[:, aligned((j - base) * 256, 256)],
                w.at[j, aligned(place[rank] * width, width)],
                sems.at[j, rank],
            )
            for rank, source in enumerate(sources)
        ]

    def begin(sources, base, j, carry):
        for copy in copies(j, sources, base):
            copy.start()
        return carry

    down_copies = chip_rows(place, wd_own, wd_near, wd, down_sems)
    for copy in down_copies:
        copy.start()
    lax.fori_loop(0, split, functools.partial(begin, pieces[0], 0), 0)
    lax.fori_loop(split, steps, functools.partial(begin, pieces[1], split), 0)
    gain = gains[1:2, :]
    for rel, (x_ref, c_ref) in enumerate(((x_a, c_a), (x_b, c_b))):
        at = pl.ds(rel * half, half)
        rows = x_ref[...].astype(F32) + (term[at, :] + far[at, :].astype(F32))
        resid[at, :] = rows
        scale = lax.rsqrt(jnp.mean(rows * rows, axis=-1, keepdims=True) + EPSILON)
        lowered[at, :] = (rows * scale * gain).astype(BF16)
        upstream[at, :] = c_ref[...]
    for copy in down_copies:
        copy.wait()

    def step(j, carry):
        for rank in range(4):
            rows = w.at[j, pl.ds(rank * width, width)]
            pltpu.make_async_copy(rows, rows, sems.at[j, rank]).wait()
        gate_up = matmul(lowered[...], w[j])
        gate, up = gate_up[:, :128], gate_up[:, 128:]
        d_hidden = times_transposed(upstream[...], wd[aligned(j * 128, 128), :])
        sigmoid = jax.nn.sigmoid(gate)
        activated = gate * sigmoid
        hidden[:, aligned(j * 128, 128)] = (activated * up).astype(BF16)
        d_gate = d_hidden * up * sigmoid * (1.0 + gate * (1.0 - sigmoid))
        d_gate_up[:, aligned(j * 256, 128)] = d_gate.astype(BF16)
        d_gate_up[:, aligned(j * 256 + 128, 128)] = (d_hidden * activated).astype(BF16)
        return carry

    lax.fori_loop(0, steps, step, 0)

    def back(n, carry):
        columns = aligned(n * 256, 256)
        value = times_transposed(d_gate_up[:, 0:256], w[0, columns, :])
        for j in range(1, steps):
            value += times_transposed(d_gate_up[:, j * 256 : (j + 1) * 256], w[j, columns, :])
        second[:, columns] = value
        lower = value.astype(BF16)
        leaving[:half, columns] = lower[half:]
        leaving[half:, columns] = lower[:half]
        return carry

    lax.fori_loop(0, D // 256, back, 0)


def ffn(place, x_a, x_b, term, far, gains, c_a, c_b, pieces, wd_own, wd_near):
    rows = term.shape[0]
    inner = 2 * wd_own.shape[0]
    wide, steps = 2 * inner, inner // 128
    return kernel_call(
        ffn_kernel,
        "ffn",
        [(SMEM, place)]
        + [(VMEM, a) for a in (x_a, x_b, term, far, gains, c_a, c_b)]
        + [(HBM, a) for a in pieces + (wd_own, wd_near)],
        [((rows, D), F32), ((rows, D), BF16), ((rows, inner), BF16), ((rows, wide), BF16),
         ((rows, D), F32), ((rows, D), BF16)],
        [pltpu.VMEM((steps, D, 256), BF16), pltpu.VMEM((inner, D), BF16),
         pltpu.VMEM((rows, D), BF16), pltpu.SemaphoreType.DMA((steps, 4)),
         pltpu.SemaphoreType.DMA((2,))],
    )


def down_kernel(place, hidden, resid, w_own, w_near, kept, leaving, w, sems):
    copies = chip_rows(place, w_own, w_near, w, sems)
    for copy in copies:
        copy.start()
    half = kept.shape[0]
    for copy in copies:
        copy.wait()

    def step(n, carry):
        columns = aligned(n * 256, 256)
        value = matmul(hidden[...], w[:, columns])
        kept[:, columns] = resid[:half, columns] + value[:half]
        leaving[:, columns] = value[half:].astype(BF16)
        return carry

    lax.fori_loop(0, D // 256, step, 0)


def down_term(place, hidden, resid, w_own, w_near):
    rows, inner = hidden.shape
    return kernel_call(
        down_kernel,
        "down_term",
        [(SMEM, place), (VMEM, hidden), (VMEM, resid), (HBM, w_own), (HBM, w_near)],
        [((rows // 2, D), F32), ((rows // 2, D), BF16)],
        [pltpu.VMEM((inner, D), BF16), pltpu.SemaphoreType.DMA((2,))],
    )


def mid_kernel(
    place, second, far, resid, gains, c_a, c_b, w_own, w_near,
    d_resid, d_branch, gain_terms, *rest,
):
    d_mixed, (w, sums, sems) = rest[:POS], rest[POS:]
    copies = chip_rows(place, w_own, w_near, w, sems)
    for copy in copies:
        copy.start()
    half, width = c_a.shape[0], w_own.shape[0]
    gain = gains[1:2, :]
    total = None
    for rel, c_ref in enumerate((c_a, c_b)):
        at = pl.ds(rel * half, half)
        rows = resid[at, :]
        scale = lax.rsqrt(jnp.mean(rows * rows, axis=-1, keepdims=True) + EPSILON)
        normed = rows * scale
        d_rows = second[at, :] + far[at, :].astype(F32)
        part = jnp.sum(d_rows * normed, axis=0, keepdims=True)
        total = part if total is None else total + part
        scaled = d_rows * gain
        value = c_ref[...].astype(F32) + scale * (
            scaled - normed * jnp.mean(scaled * normed, axis=-1, keepdims=True)
        )
        if rel == 0:
            d_resid[...] = value
        d_branch[at, :] = value.astype(BF16)
    sums[...] = total
    gain_terms[0] = sums[:, aligned(place[OWN] * width, width)]
    gain_terms[1] = sums[:, aligned(place[NEAR] * width, width)]
    for copy in copies:
        copy.wait()
    for base in range(0, w.shape[0], 256):
        value = times_transposed(d_branch[...], w[base : base + 256, :]).astype(BF16)
        put_rows(d_mixed, 0, slice(base, base + 256), value[:half])
        put_rows(d_mixed, 1, slice(base, base + 256), value[half:])


def mid(place, second, far, resid, gains, c_a, c_b, w_own, w_near):
    rows = second.shape[0]
    width = w_own.shape[0]
    return kernel_call(
        mid_kernel,
        "mid",
        [(SMEM, place), (VMEM, second), (VMEM, far), (VMEM, resid), (VMEM, gains),
         (VMEM, c_a), (VMEM, c_b), (HBM, w_own), (HBM, w_near)],
        [((rows // 2, D), F32), ((rows, D), BF16), ((2, 1, width), F32)]
        + block_shapes(rows, 2 * width),
        [pltpu.VMEM((2 * width, D), BF16), pltpu.VMEM((1, D), F32),
         pltpu.SemaphoreType.DMA((2,))],
    )


def back_first_kernel(place, w_own, w_far, w_near, w_across, *refs):
    d_qkv, (kept, leaving, rows, w, sems) = refs[:POS], refs[POS:]
    half, width = kept.shape[0], w_own.shape[0]
    part = w.shape[2] // 3
    side = place[SIDE]
    copies = [
        pltpu.make_async_copy(
            w_own.at[:, aligned((2 * k + side) * part, part)],
            w.at[0, :, pl.ds(k * part, part)],
            sems.at[k],
        )
        for k in range(3)
    ]
    copies.append(pltpu.make_async_copy(w_far, w.at[1], sems.at[3]))
    copies.append(pltpu.make_async_copy(w_near, w.at[2], sems.at[4]))
    copies.append(pltpu.make_async_copy(w_across, w.at[3], sems.at[5]))
    for copy in copies:
        copy.start()
    rows[:half, :] = rows_of(d_qkv, 0)
    rows[half:, :] = rows_of(d_qkv, 1)
    for copy in copies:
        copy.wait()

    def step(rank, carry):
        columns = aligned(place[rank] * width, width)
        value = times_transposed(rows[...], w[rank])
        kept[:, columns] = value[:half]
        leaving[:, columns] = value[half:].astype(BF16)
        return carry

    lax.fori_loop(0, 4, step, 0)


def back_first(place, d_qkv, w_own, w_far, w_near, w_across):
    rows, wide = POS * d_qkv[0].shape[0], d_qkv[0].shape[1]
    return kernel_call(
        back_first_kernel,
        "back_first",
        [(SMEM, place), (HBM, w_own), (HBM, w_far), (HBM, w_near), (HBM, w_across)]
        + in_vmem(*d_qkv),
        [((rows // 2, D), F32), ((rows // 2, D), BF16), ((rows, wide), BF16)],
        [pltpu.VMEM((4, w_own.shape[0], wide), BF16), pltpu.SemaphoreType.DMA((6,))],
    )


def last_kernel(
    place, kept, far, x_a, gains, d_resid, down_kept, down_far, *rest
):
    blocks, (gain_terms, sums) = rest[:POS], rest[POS:]
    width = gain_terms.shape[2]
    rows = x_a[...].astype(F32)
    scale = lax.rsqrt(jnp.mean(rows * rows, axis=-1, keepdims=True) + EPSILON)
    normed = rows * scale
    d_rows = kept[...] + far[...].astype(F32)
    sums[...] = jnp.sum(d_rows * normed, axis=0, keepdims=True)
    scaled = d_rows * gains[0:1, :]
    value = d_resid[...] + scale * (
        scaled - normed * jnp.mean(scaled * normed, axis=-1, keepdims=True)
    )
    put_rows(blocks, 0, slice(None), value.astype(BF16))
    put_rows(blocks, 1, slice(None), (down_kept[...] + down_far[...].astype(F32)).astype(BF16))
    for slot, rank in enumerate((OWN, NEAR, FAR, ACROSS)):
        gain_terms[slot] = sums[:, aligned(place[rank] * width, width)]


def last(place, kept, far, x_a, gains, d_resid, down_kept, down_far):
    half = kept.shape[0]
    arrays = (kept, far, x_a, gains, d_resid, down_kept, down_far)
    return kernel_call(
        last_kernel,
        "last",
        [(SMEM, place)] + [(VMEM, a) for a in arrays],
        block_shapes(2 * half, D) + [((4, 1, D // 4), F32)],
        [pltpu.VMEM((1, D), F32)],
    )


def both_rows(own, near, columns):
    return jnp.concatenate([own[:, columns], near[:, columns]], 0)


def leaving_kernel(first_block, place, left_own, left_near, right_own, right_near, leaving):
    width = leaving.shape[0]
    left = both_rows(left_own, left_near, aligned(place[ACROSS] * width, width))

    def step(j, carry):
        columns = aligned(j * 256, 256)
        right = both_rows(
            right_own, right_near, aligned((first_block + j) * 256, 256)
        )
        leaving[:, columns] = inner_rows(left, right).astype(BF16)
        return carry

    lax.fori_loop(0, leaving.shape[1] // 256, step, 0)


def leaving_gradient(place, blocks, left_own, left_near, right_own, right_near):
    width, wide = D // 4, 256 * (blocks[1] - blocks[0])
    return kernel_call(
        functools.partial(leaving_kernel, blocks[0]),
        "leaving_gradient",
        [(SMEM, place), (VMEM, left_own), (VMEM, left_near), (VMEM, right_own),
         (VMEM, right_near)],
        [((width, wide), BF16)],
    )[0]


def staying_kernel(parts, place, left_own, left_near, right_own, right_near, *rest):
    come, grad = rest[:-1], rest[-1]
    width = grad.shape[0]
    part = grad.shape[1] // 2 // parts
    side = place[SIDE]
    left = both_rows(left_own, left_near, aligned(place[OWN] * width, width))

    def put(block, who, value):
        if parts == 2:
            spots = [(0, block * 128, 0, 128), (1, block * 128, 128, 256)]
        else:
            spots = [(block // 2, (block % 2) * 256, 0, 256)]
        for k, start, low, high in spots:
            grad[:, aligned((2 * k + who) * part + start, high - low)] = value[:, low:high]

    def step(j, carry):
        right = both_rows(right_own, right_near, aligned(j * 256, 256))
        put(j, side, inner_rows(left, right))
        return carry

    lax.fori_loop(0, right_own.shape[1] // 256, step, 0)
    base = 0
    for piece in come:
        count = piece.shape[1] // 256

        def take(j, carry, piece=piece, base=base):
            put(base + j, 1 - side, piece[:, aligned(j * 256, 256)].astype(F32))
            return carry

        lax.fori_loop(0, count, take, 0)
        base += count


def staying_gradient(parts, place, left_own, left_near, right_own, right_near, *come):
    width = D // 4
    arrays = (left_own, left_near, right_own, right_near) + come
    return kernel_call(
        functools.partial(staying_kernel, parts),
        "staying_gradient",
        [(SMEM, place)] + [(VMEM, a) for a in arrays],
        [((width, 2 * right_own.shape[1]), F32)],
    )[0]


def grad_out_kernel(place, mixed_own, mixed_near, d_own, d_near, grad):
    left = both_rows(
        mixed_own, mixed_near, aligned(place[CORE] * grad.shape[0], grad.shape[0])
    )
    for base in range(0, D, 512):
        at = slice(base, base + 512)
        grad[:, at] = inner_rows(left, jnp.concatenate([d_own[:, at], d_near[:, at]], 0))


def grad_out_rows(place, mixed_own, mixed_near, d_own, d_near):
    width = mixed_own.shape[1] // 2
    return kernel_call(
        grad_out_kernel,
        "grad_out",
        [(SMEM, place), (VMEM, mixed_own), (VMEM, mixed_near), (VMEM, d_own), (VMEM, d_near)],
        [((width, D), F32)],
    )[0]


def grad_down_kernel(place, h_own, h_near, ca_own, cb_own, ca_near, cb_near, grad, wide):
    count, window = grad.shape[0], wide.shape[0]
    core = place[CORE]
    skip = h_own.shape[1] - window
    left = both_rows(h_own, h_near, aligned(core * skip, window))

    def step(n, carry):
        columns = aligned(n * 256, 256)
        right = jnp.concatenate(
            [ref[:, columns] for ref in (ca_own, cb_own, ca_near, cb_near)], 0
        )
        wide[:, columns] = inner_rows(left, right)
        return carry

    lax.fori_loop(0, D // 256, step, 0)
    grad[...] = wide[aligned(core * (count - skip), count, 64), :]


def grad_down_rows(place, h_own, h_near, ca_own, cb_own, ca_near, cb_near):
    count = h_own.shape[1] // 2
    window = -(-count // 128) * 128
    return kernel_call(
        grad_down_kernel,
        "grad_down",
        [(SMEM, place)]
        + [(VMEM, a) for a in (h_own, h_near, ca_own, cb_own, ca_near, cb_near)],
        [((count, D), F32)],
        [pltpu.VMEM((window, D), F32)],
    )[0]


def half_columns_kernel(parts, far, place, weight, half, sems):
    part = half.shape[1] // parts
    side = 1 - place[SIDE] if far else place[SIDE]
    copies = [
        pltpu.make_async_copy(
            weight.at[:, aligned((2 * k + side) * part, part)],
            half.at[:, pl.ds(k * part, part)],
            sems.at[k],
        )
        for k in range(parts)
    ]
    for copy in copies:
        copy.start()
    for copy in copies:
        copy.wait()


def half_columns(place, weight, parts, far):
    count, width = weight.shape
    return kernel_call(
        functools.partial(half_columns_kernel, parts, far),
        "far_columns" if far else "kept_columns",
        [(SMEM, place), (HBM, weight)],
        [((count, width // 2), BF16)],
        [pltpu.SemaphoreType.DMA((parts,))],
    )[0]


def spread_kernel(split, place, weight, kept_a, kept_b, leaving_a, leaving_b, sems):
    part = weight.shape[1] // 4
    side = place[SIDE]
    copies = []
    for k in range(2):
        for j in range(part // 128):
            for who, targets in ((side, (kept_a, kept_b)), (1 - side, (leaving_a, leaving_b))):
                target, at = (targets[0], j) if j < split else (targets[1], j - split)
                copies.append(
                    pltpu.make_async_copy(
                        weight.at[:, aligned((2 * k + who) * part + j * 128, 128)],
                        target.at[:, pl.ds(at * 256 + k * 128, 128)],
                        sems.at[len(copies)],
                    )
                )
    for copy in copies:
        copy.start()
    for copy in copies:
        copy.wait()


def spread(place, weight, split):
    count, width = weight.shape
    sizes = (256 * split, width // 2 - 256 * split) * 2
    return kernel_call(
        functools.partial(spread_kernel, split),
        "spread",
        [(SMEM, place), (HBM, weight)],
        [((count, size), BF16) for size in sizes],
        [pltpu.SemaphoreType.DMA((width // 128,))],
    )


def sync(*values):
    return lax.optimization_barrier(values)


def after(value, *earlier):
    return lax.optimization_barrier((value,) + earlier)[0]


def pair_body(frames_in, segment_ids, gain_attn, w_qkv, w_out, gain_ffn, w_gate_up, w_down, cotangent):
    member = lax.axis_index("fsdp") % 4
    side, core = member >> 1, member & 1
    position = lax.axis_index("fsdp") // 4
    place = jnp.stack([member, member ^ 2, member ^ 1, member ^ 3, side, core, position])
    place = place.astype(jnp.int32)
    frames = frames_in.shape[0] // POS
    half = POS * frames

    blocks = w_gate_up.shape[1] // 512
    split = (blocks + 1) // 2
    near = lambda rows: swap(rows, 1)

    qkv_leaving = half_columns(place, w_qkv, 3, True)
    qkv_across = swap(qkv_leaving, 3)
    sent = to_positions(place, after(frames_in, qkv_leaving), cotangent)
    came = exchange(sent)
    sent = sent[0]
    ids_own = segment_ids.reshape(frames, POS).T
    ids_own = jnp.take(ids_own, jnp.arange(POS) ^ position, axis=0).reshape(1, half)
    ids_far = swap(after(ids_own, sent), 2)
    gains_own = jnp.stack([gain_attn, gain_ffn])
    gains_far = swap(after(gains_own, sent), 2)
    qkv_kept = half_columns(place, after(w_qkv, sent), 3, False)
    came, ids_far, gains_far, qkv_kept = sync(came, ids_far, gains_far, qkv_kept)

    x_own, c_own = collect(came)
    x_far = swap(x_own, 2)
    gains_near = near(jnp.stack([gains_own, gains_far]))
    qkv_near = near(qkv_kept)
    qkv_far = near(qkv_across)
    kept_a, kept_b, leaving_a, leaving_b = spread(place, after(w_gate_up, x_own), split)
    x_far, qkv_far, gains_near, qkv_near, leaving_a, c_own = sync(
        x_far, qkv_far, gains_near, qkv_near, leaving_a, c_own
    )

    *qkv_sent, lowered_first, gains = first(
        place, x_own, x_far, gains_own, gains_far, gains_near[0], gains_near[1],
        w_qkv, qkv_far, qkv_near, qkv_across,
    )
    across_a = swap(after(leaving_a, lowered_first), 3)
    c_far = swap(after(c_own, lowered_first), 2)
    near_a, near_b, out_near, down_near = (
        near(after(a, lowered_first)) for a in (kept_a, kept_b, w_out, w_down)
    )
    qkv, c_far, near_a, near_b, out_near, down_near = sync(
        exchange(qkv_sent), c_far, near_a, near_b, out_near, down_near
    )

    mixed_sent = attend_local(place, ids_own, ids_far, qkv)
    across_b = swap(after(leaving_b, across_a), 3)
    far_a = near(across_a)
    c_own_near, c_far_near, lowered_first_near = (
        near(after(a, mixed_sent[0])) for a in (c_own, c_far, lowered_first)
    )
    mixed, across_b, far_a, c_own_near, c_far_near, lowered_first_near = sync(
        exchange(mixed_sent), across_b, far_a, c_own_near, c_far_near, lowered_first_near
    )

    term, leaving, mixed = out_term(place, mixed, w_out, out_near)
    far = swap(leaving, 2)
    far, mixed_near, far_b = sync(far, near(mixed), near(after(across_b, leaving)))
    pieces = (kept_a, far_a, near_a, across_a, kept_b, far_b, near_b, across_b)
    resid, lowered_second, hidden, d_gate_up, second, leaving = ffn(
        place, x_own, x_far, term, far, gains, c_own, c_far, pieces, w_down, down_near
    )

    second_far = swap(leaving, 2)
    hidden_near, lowered_second_near, d_gate_up_near = (
        near(after(rows, leaving)) for rows in (hidden, lowered_second, d_gate_up)
    )
    down_kept, down_leaving = down_term(place, after(hidden, leaving), resid, w_down, down_near)
    sides = (lowered_second, lowered_second_near, d_gate_up, d_gate_up_near)
    cut = blocks // 4
    gate_up_leaving = leaving_gradient(place, (0, cut), *sides)
    second_far, down_leaving, gate_up_leaving, hidden_near, lowered_second_near = sync(
        second_far, down_leaving, gate_up_leaving, hidden_near, lowered_second_near
    )

    d_resid, d_branch, gain_ffn_terms, *d_mixed = mid(
        place, second, second_far, resid, gains, c_own, c_far, w_out, out_near
    )
    gate_up_come = swap(gate_up_leaving, 3)
    down_far = swap(after(down_leaving, d_branch), 2)
    sides = (after(lowered_second, d_branch), lowered_second_near, d_gate_up, d_gate_up_near)
    gate_up_leaving_rest = leaving_gradient(place, (cut, blocks), *sides)
    d_branch_near, gain_ffn_near = near(d_branch), near(gain_ffn_terms[1])
    d_mixed, gate_up_come, down_far, gate_up_leaving_rest, d_branch_near, gain_ffn_near = sync(
        exchange(d_mixed), gate_up_come, down_far, gate_up_leaving_rest, d_branch_near,
        gain_ffn_near,
    )

    d_qkv_sent = attend_back_local(place, ids_own, ids_far, qkv, d_mixed)
    gate_up_come_rest = swap(gate_up_leaving_rest, 3)
    grad_down = grad_down_rows(
        place, after(hidden, d_qkv_sent[0]), hidden_near, c_own, c_far, c_own_near, c_far_near
    )
    grad_out = grad_out_rows(place, mixed, mixed_near, after(d_branch, d_qkv_sent[0]), d_branch_near)
    d_qkv, gate_up_come_rest, grad_down, grad_out = sync(
        exchange(d_qkv_sent), gate_up_come_rest, grad_down, grad_out
    )

    kept, leaving, d_projected = back_first(
        place, d_qkv, w_qkv, qkv_far, qkv_near, qkv_across
    )
    first_far = swap(leaving, 2)
    qkv_sides = (lowered_first, lowered_first_near, d_projected, near(d_projected))
    qkv_grad_leaving = leaving_gradient(place, (0, qkv_leaving.shape[1] // 256), *qkv_sides)
    first_far, qkv_grad_leaving = sync(first_far, qkv_grad_leaving)

    qkv_come = swap(qkv_grad_leaving, 3)
    *out_sent, gain_attn_terms = last(
        place, kept, first_far, x_own, gains, d_resid, down_kept, down_far
    )
    grad_gate_up = staying_gradient(
        2, place, after(sides[0], gain_attn_terms), *sides[1:], gate_up_come, gate_up_come_rest
    )
    gain_sums = gain_attn_terms[:2] + swap(gain_attn_terms[2:], 2)
    gain_attn_grad = gain_sums[0] + near(gain_sums[1])
    out_come, grad_gate_up = sync(exchange(out_sent), grad_gate_up)
    grad_qkv = staying_gradient(3, place, *qkv_sides, qkv_come)
    grad_in, block_out = to_frames(place, out_come)
    gain_ffn_grad = (gain_ffn_terms[0] + gain_ffn_near).reshape(-1)
    return (
        block_out,
        grad_in,
        gain_attn_grad.reshape(-1),
        grad_qkv,
        grad_out,
        gain_ffn_grad,
        grad_gate_up,
        grad_down,
    )


def solution(mesh):
    in_specs = (
        P("fsdp", None),
        P("fsdp"),
        P("fsdp"),
        P("fsdp", None),
        P("fsdp", None),
        P("fsdp"),
        P("fsdp", None),
        P("fsdp", None),
        P("fsdp", None),
    )
    out_specs = (
        P("fsdp", None),
        P("fsdp", None),
        P("fsdp"),
        P("fsdp", None),
        P("fsdp", None),
        P("fsdp"),
        P("fsdp", None),
        P("fsdp", None),
    )
    chosen = pair_body if mesh.shape["fsdp"] == 4 * POS else body
    return jax.shard_map(chosen, mesh=mesh, in_specs=in_specs, out_specs=out_specs, check_vma=False)
```

```python
import functools
import math

import jax
import jax.numpy as jnp
from jax import lax
from jax.experimental import pallas as pl
from jax.experimental.pallas import tpu as pltpu
from jax.sharding import PartitionSpec as P

D = 1024
FF = 2816
HEADS = 16
HEAD_DIM = 64
POS = 8


EPSILON = 1e-05


def for_sending(array):

    def short(part):
        return part.astype(jnp.bfloat16) if part.dtype == jnp.float32 else part

    return jax.tree.map(short, array)


def swapped(block, axis, stride):
    count = lax.axis_size(axis)
    route = []
    for low in range(count):
        high = low | 1 << stride
        if high != low and high < count:
            route += [(low, high), (high, low)]
    return lax.ppermute(block, axis, route)


def positions_layout(frame_rows, groups):
    width = frame_rows.shape[-1]
    per_piece = frame_rows.shape[0] // POS // groups
    shaped = frame_rows.reshape(groups, per_piece, POS, width).transpose(2, 0, 1, 3)
    return shaped.reshape(POS * groups, per_piece, width)


def frames_layout(piece_rows, groups):
    width = piece_rows.shape[-1]
    per_piece = piece_rows.shape[1]
    shaped = piece_rows.reshape(POS, groups, per_piece, width).transpose(1, 2, 0, 3)
    return shaped.reshape(groups * per_piece * POS, width)


def inner_rows(left, right):
    return lax.dot_general(
        left, right, (((0,), (0,)), ((), ())), preferred_element_type=jnp.float32
    )


def times_transposed(left, right):
    return lax.dot_general(
        left, right, (((1,), (1,)), ((), ())), preferred_element_type=jnp.float32
    )


def join_pieces(current, partner, member, bit_level):
    upper_half = member >> bit_level & 1 == 1
    return tuple(
        (
            jnp.where(
                upper_half,
                jnp.concatenate([theirs, own_piece], 0),
                jnp.concatenate([own_piece, theirs], 0),
            )
            for own_piece, theirs in zip(current, partner)
        )
    )


def collect_forward(pieces, member, levels):
    current = pieces
    for bit_level in range(levels):
        partner = jax.tree.map(
            lambda part, own: part.astype(own.dtype),
            swapped(for_sending(current), "fsdp", bit_level),
            current,
        )
        current = join_pieces(current, partner, member, bit_level)
    return current


def collect_again(pieces, member, levels):
    current = pieces
    for bit_level in range(levels):
        partner = jax.tree.map(
            lambda part, own: part.astype(own.dtype),
            swapped(for_sending(current), "fsdp", bit_level),
            current,
        )
        current = join_pieces(current, partner, member, bit_level)
    return current


def halving_sum(terms, member, levels, sender):
    current = terms
    for bit_level in reversed(range(levels)):
        upper_half = member >> bit_level & 1 == 1
        leaving = tuple(
            (
                jnp.where(
                    upper_half,
                    term_part[: term_part.shape[0] // 2],
                    term_part[term_part.shape[0] // 2 :],
                )
                for term_part in current
            )
        )
        staying = tuple(
            (
                jnp.where(
                    upper_half,
                    term_part[term_part.shape[0] // 2 :],
                    term_part[: term_part.shape[0] // 2],
                )
                for term_part in current
            )
        )
        arrived = sender(leaving, bit_level)
        current = tuple((held_part + come_part for held_part, come_part in zip(staying, arrived)))
    return current


def send_whole(parts, bit_level):
    return jax.tree.map(
        lambda part, own: part.astype(own.dtype),
        swapped(for_sending(parts), "fsdp", bit_level),
        parts,
    )


def permitted(validity):
    row_place = lax.broadcasted_iota(jnp.int32, (POS, POS), 0)
    column_place = lax.broadcasted_iota(jnp.int32, (POS, POS), 1)
    causal = column_place <= row_place
    same_segment = validity[:, :, None] == validity[:, None, :]
    return (causal[None] & same_segment)[:, None]


def split_projections(qkv_frames):
    frames = qkv_frames.shape[0] // POS
    shaped = qkv_frames.reshape(frames, POS, 3, HEADS, HEAD_DIM)
    return (shaped[:, :, 0], shaped[:, :, 1], shaped[:, :, 2])


def masked_scores(queries, key_rows, allowed):
    scores = jnp.einsum(
        "fqhd,fkhd->fhqk", queries, key_rows, preferred_element_type=jnp.float32
    ) * HEAD_DIM ** (-0.5)
    return jnp.where(allowed, scores, -jnp.inf)


def attend(qkv_frames, validity):
    queries, key_rows, value_rows = split_projections(qkv_frames)
    scores = masked_scores(queries, key_rows, permitted(validity))
    highest = jnp.max(scores, axis=-1, keepdims=True)
    raised = jnp.exp(scores - highest)
    totals = jnp.sum(raised, axis=-1, keepdims=True)
    attn_probs = (raised / totals).astype(jnp.bfloat16)
    attended = jnp.einsum(
        "fhqk,fkhd->fqhd", attn_probs, value_rows, preferred_element_type=jnp.float32
    )
    mixed_heads = attended.reshape(qkv_frames.shape[0], D).astype(jnp.bfloat16)
    return (mixed_heads, highest + jnp.log(totals))


def attend_back(qkv_frames, validity, log_total, d_mixed):
    queries, key_rows, value_rows = split_projections(qkv_frames)
    frames = queries.shape[0]
    scores = masked_scores(queries, key_rows, permitted(validity))
    weights_full = jnp.exp(scores - log_total)
    attn_probs = weights_full.astype(jnp.bfloat16)
    d_heads = d_mixed.reshape(frames, POS, HEADS, HEAD_DIM)
    d_probs = jnp.einsum("fqhd,fkhd->fhqk", d_heads, value_rows, preferred_element_type=jnp.float32)
    d_values = jnp.einsum(
        "fhqk,fqhd->fkhd", attn_probs, d_heads, preferred_element_type=jnp.float32
    )
    d_scores = weights_full * (d_probs - jnp.sum(d_probs * weights_full, axis=-1, keepdims=True))
    d_scores = d_scores.astype(jnp.bfloat16)
    d_queries = jnp.einsum(
        "fhqk,fkhd->fqhd", d_scores, key_rows, preferred_element_type=jnp.float32
    ) * HEAD_DIM ** (-0.5)
    d_keys = jnp.einsum(
        "fhqk,fqhd->fkhd", d_scores, queries, preferred_element_type=jnp.float32
    ) * HEAD_DIM ** (-0.5)
    stacked = jnp.stack([d_queries, d_keys, d_values], axis=2)
    return stacked.reshape(frames * POS, 3 * D).astype(jnp.bfloat16)


def body(frames_in, segment_ids, gain_attn, w_qkv, w_out, gain_ffn, w_gate_up, w_down, cotangent):
    devices = lax.axis_size("fsdp")
    groups = devices // POS
    levels = groups.bit_length() - 1
    member = lax.axis_index("fsdp") % groups
    per_piece = frames_in.shape[0] // POS // groups
    validity = segment_ids.reshape(-1, POS)
    moved_input, moved_cotangent = (
        lax.all_to_all(
            positions_layout(frames_in, groups), "fsdp", split_axis=0, concat_axis=0, tiled=True
        ),
        lax.all_to_all(
            positions_layout(cotangent, groups), "fsdp", split_axis=0, concat_axis=0, tiled=True
        ),
    )
    inputs = moved_input.reshape(-1, D).astype(jnp.float32)
    upstream = moved_cotangent.reshape(-1, D)
    own_pieces = (w_qkv, w_out, w_gate_up, w_down, gain_attn, gain_ffn)
    collected = collect_forward(own_pieces, member, levels)
    whole_qkv, whole_out, whole_gate_up, whole_down, whole_gain_attn, whole_gain_ffn = collected
    gain_first = whole_gain_attn.astype(jnp.float32)
    gain_second = whole_gain_ffn.astype(jnp.float32)
    scale_first = lax.rsqrt(jnp.mean(inputs * inputs, axis=-1, keepdims=True) + EPSILON)
    normed_first = inputs * scale_first
    lowered_first = (normed_first * gain_first).astype(jnp.bfloat16)
    projected = jnp.dot(lowered_first, whole_qkv, preferred_element_type=jnp.float32).astype(
        jnp.bfloat16
    )
    qkv_frames = frames_layout(
        lax.all_to_all(
            projected.reshape(devices, per_piece, 3 * D),
            "fsdp",
            split_axis=0,
            concat_axis=0,
            tiled=True,
        ),
        groups,
    )
    mixed_frames, log_total = attend(qkv_frames, validity)
    mixed_rows = lax.all_to_all(
        positions_layout(mixed_frames, groups), "fsdp", split_axis=0, concat_axis=0, tiled=True
    ).reshape(-1, D)
    residual = inputs + jnp.dot(mixed_rows, whole_out, preferred_element_type=jnp.float32)
    scale_second = lax.rsqrt(jnp.mean(residual * residual, axis=-1, keepdims=True) + EPSILON)
    normed_second = residual * scale_second
    lowered_second = (normed_second * gain_second).astype(jnp.bfloat16)
    gate_up = jnp.dot(lowered_second, whole_gate_up, preferred_element_type=jnp.float32)
    gate_part = gate_up[:, :FF]
    up_part = gate_up[:, FF:]
    sigmoid_gate = jax.nn.sigmoid(gate_part)
    activated = gate_part * sigmoid_gate
    hidden = (activated * up_part).astype(jnp.bfloat16)
    result_rows = (
        residual + jnp.dot(hidden, whole_down, preferred_element_type=jnp.float32)
    ).astype(jnp.bfloat16)
    block_out = frames_layout(
        lax.all_to_all(
            result_rows.reshape(devices, per_piece, D),
            "fsdp",
            split_axis=0,
            concat_axis=0,
            tiled=True,
        ),
        groups,
    )
    collected = collect_again(own_pieces, member, levels)
    whole_qkv, whole_out, whole_gate_up, whole_down, whole_gain_attn, whole_gain_ffn = collected
    gain_first = whole_gain_attn.astype(jnp.float32)
    gain_second = whole_gain_ffn.astype(jnp.float32)
    grad_down_term = inner_rows(hidden, upstream)
    d_hidden = times_transposed(upstream, whole_down)
    d_gate = d_hidden * up_part * sigmoid_gate * (1.0 + gate_part * (1.0 - sigmoid_gate))
    d_up = d_hidden * activated
    d_gate_up = jnp.concatenate([d_gate, d_up], axis=1).astype(jnp.bfloat16)
    grad_gate_up_term = inner_rows(lowered_second, d_gate_up)
    d_second = times_transposed(d_gate_up, whole_gate_up)
    grad_gain_ffn_term = jnp.sum(d_second * normed_second, axis=0)
    scaled_second = d_second * gain_second
    d_residual = upstream.astype(jnp.float32) + scale_second * (
        scaled_second
        - normed_second * jnp.mean(scaled_second * normed_second, axis=-1, keepdims=True)
    )
    d_branch = d_residual.astype(jnp.bfloat16)
    grad_out_term = inner_rows(mixed_rows, d_branch)
    d_mixed = times_transposed(d_branch, whole_out).astype(jnp.bfloat16)
    d_mixed_frames = frames_layout(
        lax.all_to_all(
            d_mixed.reshape(devices, per_piece, D), "fsdp", split_axis=0, concat_axis=0, tiled=True
        ),
        groups,
    )
    d_qkv_frames = attend_back(qkv_frames, validity, log_total, d_mixed_frames)
    d_projected = lax.all_to_all(
        positions_layout(d_qkv_frames, groups), "fsdp", split_axis=0, concat_axis=0, tiled=True
    ).reshape(-1, 3 * D)
    grad_qkv_term = inner_rows(lowered_first, d_projected)
    d_first = times_transposed(d_projected, whole_qkv)
    grad_gain_attn_term = jnp.sum(d_first * normed_first, axis=0)
    scaled_first = d_first * gain_first
    d_inputs = d_residual + scale_first * (
        scaled_first - normed_first * jnp.mean(scaled_first * normed_first, axis=-1, keepdims=True)
    )
    grad_in = frames_layout(
        lax.all_to_all(
            d_inputs.reshape(devices, per_piece, D).astype(jnp.bfloat16),
            "fsdp",
            split_axis=0,
            concat_axis=0,
            tiled=True,
        ).astype(jnp.float32),
        groups,
    )
    shares = halving_sum(
        (
            grad_qkv_term,
            grad_out_term,
            grad_gate_up_term,
            grad_down_term,
            grad_gain_attn_term,
            grad_gain_ffn_term,
        ),
        member,
        levels,
        send_whole,
    )
    return (block_out, grad_in, shares[4], shares[0], shares[1], shares[5], shares[2], shares[3])

VMEM = pl.BlockSpec(memory_space=pltpu.VMEM)
SMEM = pl.BlockSpec(memory_space=pltpu.SMEM)
HBM = pl.BlockSpec(memory_space=pltpu.HBM)
STAGED = pl.BlockSpec(memory_space=pltpu.HBM)
BF16 = jnp.bfloat16
F32 = jnp.float32
OWN, FAR, NEAR, ACROSS, SIDE, CORE, POSITION = range(7)


def swap(block, mask):
    count = lax.axis_size("fsdp")
    return lax.ppermute(block, "fsdp", [(i, i ^ mask) for i in range(count)])


def exchange(blocks):
    count = lax.axis_size("fsdp")
    stride = count // POS
    if len(blocks) == POS:
        return [blocks[0]] + [swap(blocks[k], stride * k) for k in range(1, POS)]
    lanes = [[r + stride * k for k in range(POS)] for r in range(stride)]
    return [
        lax.all_to_all(
            blocks[0], "fsdp", split_axis=0, concat_axis=0, tiled=True, axis_index_groups=lanes
        )
    ]


def kernel_call(kernel, name, args, outs, scratch=()):
    flat = lambda items: [p for item in items for p in (item if isinstance(item, list) else [item])]
    staged = [n for n, (spec, _) in enumerate(flat(args)) if spec is STAGED]
    arrays = [
        pltpu.with_memory_space_constraint(a, pltpu.HBM) if spec is STAGED or spec is HBM else a
        for spec, a in flat(args)
    ]
    scratch = list(scratch)
    own = len(scratch)
    scratch += [pltpu.VMEM(arrays[n].shape, arrays[n].dtype) for n in staged]
    scratch += [pltpu.SemaphoreType.DMA((max(len(staged), 1),))]
    held = sum(
        math.prod(ref.shape) * jnp.dtype(ref.dtype).itemsize
        for ref in scratch
        if ref.memory_space == pltpu.VMEM
    )

    def grouped(items, values):
        return [
            [next(values) for _ in item] if isinstance(item, list) else next(values)
            for item in items
        ]

    def body_kernel(*refs):
        inputs, outputs = list(refs[: len(arrays)]), refs[len(arrays) :]
        outputs, extra = outputs[: len(flat(outs))], outputs[len(flat(outs)) :]
        extra, landing, sems = extra[:own], extra[own:-1], extra[-1]
        copies = []
        for k, n in enumerate(staged):
            copies.append(pltpu.make_async_copy(inputs[n], landing[k], sems.at[k]))
            inputs[n] = landing[k]
        for copy in copies:
            copy.start()

        def ready():
            for copy in copies:
                copy.wait()

        kernel(ready, *grouped(args, iter(inputs)), *grouped(outs, iter(outputs)), *extra)

    result = pl.pallas_call(
        body_kernel,
        name=name,
        in_specs=[spec for spec, _ in flat(args)],
        out_specs=[VMEM] * len(flat(outs)),
        out_shape=[jax.ShapeDtypeStruct(s, d) for s, d in flat(outs)],
        scratch_shapes=scratch,
        cost_estimate=pl.CostEstimate(flops=1, bytes_accessed=1, transcendentals=0),
        compiler_params=pltpu.CompilerParams(vmem_limit_bytes=held + (8 << 20)),
    )(*arrays)
    return grouped(outs, iter(result))


def views(blocks, place):
    if len(blocks) == POS:
        return blocks
    return [blocks[0].at[place[POSITION] ^ k] for k in range(POS)]


def matmul(left, right):
    return jnp.dot(left, right, preferred_element_type=F32)


def aligned(start, size, step=128):
    return pl.ds(pl.multiple_of(start, step), size)


def rows_of(refs, rel, columns=slice(None)):
    frames = refs[0].shape[0] // 2
    return jnp.concatenate([ref[rel * frames : (rel + 1) * frames, columns] for ref in refs], 0)


def put_rows(refs, rel, columns, value):
    frames = refs[0].shape[0] // 2
    for k, ref in enumerate(refs):
        ref[rel * frames : (rel + 1) * frames, columns] = value[k * frames : (k + 1) * frames]


def block_shapes(rows, width, joined):
    if joined:
        return [((POS, rows // POS, width), BF16)]
    return [((rows // POS, width), BF16)] * POS


def in_vmem(*arrays):
    return [(VMEM, a) for a in arrays]


def in_stage(*arrays):
    return [(STAGED, a) for a in arrays]


def place_matrix(size, to_positions, position):
    frames = size // POS
    row = lax.broadcasted_iota(jnp.int32, (size, size), 0)
    column = lax.broadcasted_iota(jnp.int32, (size, size), 1)
    if not to_positions:
        row, column = column, row
    return (column == (row % frames) * POS + ((row // frames) ^ position)).astype(F32).astype(BF16)


def to_positions_kernel(ready, place, x_rows, c_rows, blocks):
    blocks = views(blocks, place)
    order = place_matrix(x_rows.shape[0], True, place[POSITION])
    ready()
    for rel, rows in enumerate((x_rows, c_rows)):
        put_rows(blocks, rel, slice(None), matmul(order, rows[...]).astype(BF16))


def to_positions(place, x_rows, c_rows):
    size, width = x_rows.shape
    return kernel_call(
        to_positions_kernel,
        "to_positions",
        [(SMEM, place)] + in_stage(x_rows, c_rows),
        [block_shapes(2 * size, width, True)],
    )[0]


def collect_kernel(ready, place, blocks, x_own, c_own):
    ready()
    blocks = views(blocks, place)
    x_own[...] = rows_of(blocks, 0)
    c_own[...] = rows_of(blocks, 1)


def collect(place, blocks):
    rows, width = blocks[0].shape[-2:]
    return kernel_call(
        collect_kernel,
        "collect",
        [(SMEM, place), in_vmem(*blocks)],
        [((rows * POS // 2, width), BF16)] * 2,
    )


def to_frames_kernel(ready, place, blocks, *rows):
    ready()
    blocks = views(blocks, place)
    order = place_matrix(rows[0].shape[0], False, place[POSITION])
    for rel in range(2):
        rows[rel][...] = matmul(order, rows_of(blocks, rel)).astype(rows[rel].dtype)


def to_frames(place, blocks):
    size = blocks[0].shape[-2] * POS // 2
    return kernel_call(
        to_frames_kernel,
        "to_frames",
        [(SMEM, place), in_vmem(*blocks)],
        [((size, D), F32), ((size, D), BF16)],
    )


def first_kernel(
    ready, place, x_a, x_b, gains_own, gains_far, gains_near, gains_across, w_own, w_far, w_near, w_across,
    qkv, lowered, gains, w, sems,
):
    qkv = views(qkv, place)
    half, width = x_a.shape[0], w_own.shape[0]
    part = w.shape[1] // 3
    side = place[SIDE]
    at_rows = lambda rank: aligned(place[rank] * width, width)
    copies = [
        pltpu.make_async_copy(
            w_own.at[:, aligned((2 * k + side) * part, part)],
            w.at[at_rows(OWN), pl.ds(k * part, part)],
            sems.at[k],
        )
        for k in range(3)
    ]
    copies.append(pltpu.make_async_copy(w_far, w.at[at_rows(FAR)], sems.at[3]))
    copies.append(pltpu.make_async_copy(w_near, w.at[at_rows(NEAR)], sems.at[4]))
    copies.append(pltpu.make_async_copy(w_across, w.at[at_rows(ACROSS)], sems.at[5]))
    for copy in copies:
        copy.start()
    ready()
    gains[:, at_rows(OWN)] = gains_own[...].astype(F32)
    gains[:, at_rows(FAR)] = gains_far[...].astype(F32)
    gains[:, at_rows(NEAR)] = gains_near[...].astype(F32)
    gains[:, at_rows(ACROSS)] = gains_across[...].astype(F32)
    gain = gains[0:1, :]
    for rel, ref in enumerate((x_a, x_b)):
        rows = ref[...].astype(F32)
        scale = lax.rsqrt(jnp.mean(rows * rows, axis=-1, keepdims=True) + EPSILON)
        lowered[rel * half : (rel + 1) * half, :] = (rows * scale * gain).astype(BF16)
    for copy in copies:
        copy.wait()

    def step(n, carry):
        columns = aligned(n * 256, 256, 256)
        value = matmul(lowered[...], w[:, columns]).astype(BF16)
        put_rows(qkv, 0, columns, value[:half])
        put_rows(qkv, 1, columns, value[half:])
        return carry

    lax.fori_loop(0, w.shape[1] // 256, step, 0)


def first(
    place, x_a, x_b, gains_own, gains_far, gains_near, gains_across, w_own, w_far, w_near, w_across
):
    half = x_a.shape[0]
    wide = w_far.shape[1]
    return kernel_call(
        first_kernel,
        "first",
        [(SMEM, place), (STAGED, x_a), (STAGED, x_b), (VMEM, gains_own), (VMEM, gains_far),
         (VMEM, gains_near), (VMEM, gains_across), (HBM, w_own), (HBM, w_far), (HBM, w_near),
         (HBM, w_across)],
        [block_shapes(2 * half, wide, False), ((2 * half, D), BF16), ((2, D), F32)],
        [pltpu.VMEM((D, wide), BF16), pltpu.SemaphoreType.DMA((6,))],
    )


def allowed_pairs(ids, position):
    size = ids.shape[1]
    frames = size // POS
    row = lax.broadcasted_iota(jnp.int32, (size, size), 0)
    column = lax.broadcasted_iota(jnp.int32, (size, size), 1)
    across = jnp.broadcast_to(ids.astype(F32), (size, size))
    same = (across == across.T) & (row % frames == column % frames)
    mask = same & ((column // frames) ^ position <= (row // frames) ^ position)
    return jnp.concatenate([mask, mask], 1)


def pair_of_heads(rows, low):
    return jnp.concatenate([rows * low, rows * (1 - low)], 0)


def lane_halves(value, reduce):
    size = value.shape[1] // 2
    parts = [
        jnp.broadcast_to(reduce(value[:, k * size : (k + 1) * size]), (value.shape[0], size))
        for k in range(2)
    ]
    return jnp.concatenate(parts, 1)


def pair_probs(query, key_pair, mask):
    scores = times_transposed(query, key_pair) * HEAD_DIM ** (-0.5)
    scores = jnp.where(mask, scores, -jnp.inf)
    raised = jnp.exp(scores - lane_halves(scores, lambda a: jnp.max(a, -1, keepdims=True)))
    return raised / lane_halves(raised, lambda a: jnp.sum(a, -1, keepdims=True))


def first_head_lanes():
    lane = lax.broadcasted_iota(jnp.int32, (1, 2 * HEAD_DIM), 1)
    return (lane < HEAD_DIM).astype(F32).astype(BF16)


def attend_kernel(ready, place, ids_a, ids_b, qkv, mixed):
    qkv, mixed = views(qkv, place), views(mixed, place)
    part = mixed[0].shape[1]
    low = first_head_lanes()
    ready()
    for rel, ids in enumerate((ids_a, ids_b)):
        mask = allowed_pairs(ids[...], place[POSITION])
        for base in range(0, part, 2 * HEAD_DIM):
            query, key_rows, value_rows = (
                rows_of(qkv, rel, slice(k * part + base, k * part + base + 2 * HEAD_DIM))
                for k in range(3)
            )
            probs = pair_probs(query, pair_of_heads(key_rows, low), mask)
            value = matmul(probs.astype(BF16), pair_of_heads(value_rows, low))
            put_rows(mixed, rel, slice(base, base + 2 * HEAD_DIM), value.astype(BF16))


def attend_local(place, ids_a, ids_b, qkv):
    rows, wide = qkv[0].shape[-2:]
    return kernel_call(
        attend_kernel,
        "attend",
        [(SMEM, place), (STAGED, ids_a), (STAGED, ids_b), in_stage(*qkv)],
        [block_shapes(rows * POS, wide // 3, True)],
    )[0]


def attend_back_kernel(ready, place, ids_a, ids_b, qkv, d_mixed, d_qkv):
    qkv, d_mixed, d_qkv = (views(blocks, place) for blocks in (qkv, d_mixed, d_qkv))
    part = d_mixed[0].shape[1]
    pair = 2 * HEAD_DIM
    low = first_head_lanes()
    size = POS * d_mixed[0].shape[0] // 2
    low_full = lax.broadcasted_iota(jnp.int32, (size, pair), 1) < HEAD_DIM
    scale = HEAD_DIM ** (-0.5)
    ready()
    for rel, ids in enumerate((ids_a, ids_b)):
        mask = allowed_pairs(ids[...], place[POSITION])
        for base in range(0, part, pair):
            query, key_rows, value_rows = (
                rows_of(qkv, rel, slice(k * part + base, k * part + base + pair))
                for k in range(3)
            )
            d_rows = rows_of(d_mixed, rel, slice(base, base + pair))
            keys = pair_of_heads(key_rows, low)
            probs = pair_probs(query, keys, mask)
            d_probs = times_transposed(d_rows, pair_of_heads(value_rows, low))
            inner = lane_halves(d_probs * probs, lambda a: jnp.sum(a, -1, keepdims=True))
            d_scores = (probs * (d_probs - inner)).astype(BF16)
            d_query = matmul(d_scores, keys) * scale
            d_key = inner_rows(d_scores, query) * scale
            d_value = inner_rows(probs.astype(BF16), d_rows)
            d_key = jnp.where(low_full, d_key[:size], d_key[size:])
            d_value = jnp.where(low_full, d_value[:size], d_value[size:])
            for k, value in enumerate((d_query, d_key, d_value)):
                columns = slice(k * part + base, k * part + base + pair)
                put_rows(d_qkv, rel, columns, value.astype(BF16))


def attend_back_local(place, ids_a, ids_b, qkv, d_mixed):
    rows, wide = qkv[0].shape[-2:]
    return kernel_call(
        attend_back_kernel,
        "attend_back",
        [(SMEM, place), (STAGED, ids_a), (STAGED, ids_b), in_stage(*qkv), in_vmem(*d_mixed)],
        [block_shapes(rows * POS, wide, False)],
    )[0]


def chip_rows(place, own, near, whole, sems):
    count = own.shape[0]
    core = place[CORE]
    return [
        pltpu.make_async_copy(own, whole.at[aligned(core * count, count, 64)], sems.at[0]),
        pltpu.make_async_copy(near, whole.at[aligned((1 - core) * count, count, 64)], sems.at[1]),
    ]


def out_kernel(ready, place, w_own, w_near, mixed, term, leaving, mixed_rows, w, sems):
    mixed = views(mixed, place)
    copies = chip_rows(place, w_own, w_near, w, sems)
    for copy in copies:
        copy.start()
    ready()
    rows = jnp.concatenate([rows_of(mixed, 0), rows_of(mixed, 1)], 0)
    mixed_rows[...] = rows
    half = rows.shape[0] // 2
    for copy in copies:
        copy.wait()
    for base in range(0, D, 512):
        value = matmul(rows, w[:, base : base + 512])
        term[:, base : base + 512] = value
        lowered = value.astype(BF16)
        leaving[:half, base : base + 512] = lowered[half:]
        leaving[half:, base : base + 512] = lowered[:half]


def out_term(place, mixed, w_own, w_near):
    rows = POS * mixed[0].shape[-2]
    inner = 2 * w_own.shape[0]
    return kernel_call(
        out_kernel,
        "out_term",
        [(SMEM, place), (HBM, w_own), (HBM, w_near), in_vmem(*mixed)],
        [((rows, D), F32), ((rows, D), BF16), ((rows, inner), BF16)],
        [pltpu.VMEM((inner, D), BF16), pltpu.SemaphoreType.DMA((2,))],
    )


def ffn_kernel(
    ready, place, x_a, x_b, term, far, gains, c_a, c_b, *rest
):
    pieces, (wd_own, wd_near) = (rest[:4], rest[4:8]), rest[8:10]
    resid, lowered, hidden, d_gate_up, second, leaving = rest[10:16]
    w, wd, upstream, sems, down_sems = rest[16:]
    half, width, steps = x_a.shape[0], pieces[0][0].shape[0], w.shape[0]
    split = pieces[0][0].shape[1] // 256

    def copies(j, sources, base):
        return [
            pltpu.make_async_copy(
                source.at[:, aligned((j - base) * 256, 256)],
                w.at[j, aligned(place[rank] * width, width)],
                sems.at[j, rank],
            )
            for rank, source in enumerate(sources)
        ]

    def begin(sources, base, j, carry):
        for copy in copies(j, sources, base):
            copy.start()
        return carry

    down_copies = chip_rows(place, wd_own, wd_near, wd, down_sems)
    for copy in down_copies:
        copy.start()
    lax.fori_loop(0, split, functools.partial(begin, pieces[0], 0), 0)
    lax.fori_loop(split, steps, functools.partial(begin, pieces[1], split), 0)
    ready()
    gain = gains[1:2, :]
    for rel, (x_ref, c_ref) in enumerate(((x_a, c_a), (x_b, c_b))):
        at = pl.ds(rel * half, half)
        rows = x_ref[...].astype(F32) + (term[at, :] + far[at, :].astype(F32))
        resid[at, :] = rows
        scale = lax.rsqrt(jnp.mean(rows * rows, axis=-1, keepdims=True) + EPSILON)
        lowered[at, :] = (rows * scale * gain).astype(BF16)
        upstream[at, :] = c_ref[...]
    for copy in down_copies:
        copy.wait()

    def step(j, carry):
        for rank in range(4):
            rows = w.at[j, pl.ds(rank * width, width)]
            pltpu.make_async_copy(rows, rows, sems.at[j, rank]).wait()
        gate_up = matmul(lowered[...], w[j])
        gate, up = gate_up[:, :128], gate_up[:, 128:]
        d_hidden = times_transposed(upstream[...], wd[aligned(j * 128, 128), :])
        sigmoid = jax.nn.sigmoid(gate)
        activated = gate * sigmoid
        hidden[:, aligned(j * 128, 128)] = (activated * up).astype(BF16)
        d_gate = d_hidden * up * sigmoid * (1.0 + gate * (1.0 - sigmoid))
        d_gate_up[:, aligned(j * 256, 128)] = d_gate.astype(BF16)
        d_gate_up[:, aligned(j * 256 + 128, 128)] = (d_hidden * activated).astype(BF16)
        return carry

    lax.fori_loop(0, steps, step, 0)

    def back(n, carry):
        columns = aligned(n * 256, 256)
        value = times_transposed(d_gate_up[:, 0:256], w[0, columns, :])
        for j in range(1, steps):
            value += times_transposed(d_gate_up[:, j * 256 : (j + 1) * 256], w[j, columns, :])
        second[:, columns] = value
        lower = value.astype(BF16)
        leaving[:half, columns] = lower[half:]
        leaving[half:, columns] = lower[:half]
        return carry

    lax.fori_loop(0, D // 256, back, 0)


def ffn(place, x_a, x_b, term, far, gains, c_a, c_b, pieces, wd_own, wd_near):
    rows = term.shape[0]
    inner = 2 * wd_own.shape[0]
    wide, steps = 2 * inner, inner // 128
    return kernel_call(
        ffn_kernel,
        "ffn",
        [(SMEM, place)]
        + in_stage(x_a, x_b) + in_vmem(term, far) + in_stage(gains, c_a, c_b)
        + [(HBM, a) for a in pieces + (wd_own, wd_near)],
        [((rows, D), F32), ((rows, D), BF16), ((rows, inner), BF16), ((rows, wide), BF16),
         ((rows, D), F32), ((rows, D), BF16)],
        [pltpu.VMEM((steps, D, 256), BF16), pltpu.VMEM((inner, D), BF16),
         pltpu.VMEM((rows, D), BF16), pltpu.SemaphoreType.DMA((steps, 4)),
         pltpu.SemaphoreType.DMA((2,))],
    )


def down_kernel(ready, place, hidden, resid, w_own, w_near, kept, leaving, w, sems):
    copies = chip_rows(place, w_own, w_near, w, sems)
    for copy in copies:
        copy.start()
    half = kept.shape[0]
    ready()
    for copy in copies:
        copy.wait()

    def step(n, carry):
        columns = aligned(n * 256, 256)
        value = matmul(hidden[...], w[:, columns])
        kept[:, columns] = resid[:half, columns] + value[:half]
        leaving[:, columns] = value[half:].astype(BF16)
        return carry

    lax.fori_loop(0, D // 256, step, 0)


def down_term(place, hidden, resid, w_own, w_near):
    rows, inner = hidden.shape
    return kernel_call(
        down_kernel,
        "down_term",
        [(SMEM, place), (STAGED, hidden), (VMEM, resid), (HBM, w_own), (HBM, w_near)],
        [((rows // 2, D), F32), ((rows // 2, D), BF16)],
        [pltpu.VMEM((inner, D), BF16), pltpu.SemaphoreType.DMA((2,))],
    )


def mid_kernel(
    ready, place, second, far, resid, gains, c_a, c_b, w_own, w_near,
    d_resid, d_branch, gain_terms, d_mixed, w, sums, sems,
):
    d_mixed = views(d_mixed, place)
    copies = chip_rows(place, w_own, w_near, w, sems)
    for copy in copies:
        copy.start()
    half, width = c_a.shape[0], w_own.shape[0]
    ready()
    gain = gains[1:2, :]
    total = None
    for rel, c_ref in enumerate((c_a, c_b)):
        at = pl.ds(rel * half, half)
        rows = resid[at, :]
        scale = lax.rsqrt(jnp.mean(rows * rows, axis=-1, keepdims=True) + EPSILON)
        normed = rows * scale
        d_rows = second[at, :] + far[at, :].astype(F32)
        part = jnp.sum(d_rows * normed, axis=0, keepdims=True)
        total = part if total is None else total + part
        scaled = d_rows * gain
        value = c_ref[...].astype(F32) + scale * (
            scaled - normed * jnp.mean(scaled * normed, axis=-1, keepdims=True)
        )
        if rel == 0:
            d_resid[...] = value
        d_branch[at, :] = value.astype(BF16)
    sums[...] = total
    gain_terms[0] = sums[:, aligned(place[OWN] * width, width)]
    gain_terms[1] = sums[:, aligned(place[NEAR] * width, width)]
    for copy in copies:
        copy.wait()
    for base in range(0, w.shape[0], 256):
        value = times_transposed(d_branch[...], w[base : base + 256, :]).astype(BF16)
        put_rows(d_mixed, 0, slice(base, base + 256), value[:half])
        put_rows(d_mixed, 1, slice(base, base + 256), value[half:])


def mid(place, second, far, resid, gains, c_a, c_b, w_own, w_near):
    rows = second.shape[0]
    width = w_own.shape[0]
    return kernel_call(
        mid_kernel,
        "mid",
        [(SMEM, place), (VMEM, second), (VMEM, far), (VMEM, resid), (STAGED, gains),
         (STAGED, c_a), (STAGED, c_b), (HBM, w_own), (HBM, w_near)],
        [((rows // 2, D), F32), ((rows, D), BF16), ((2, 1, width), F32),
         block_shapes(rows, 2 * width, True)],
        [pltpu.VMEM((2 * width, D), BF16), pltpu.VMEM((1, D), F32),
         pltpu.SemaphoreType.DMA((2,))],
    )


def back_first_kernel(
    ready, place, w_own, w_far, w_near, w_across, d_qkv, kept, leaving, rows, w, sems
):
    d_qkv = views(d_qkv, place)
    half, width = kept.shape[0], w_own.shape[0]
    part = w.shape[2] // 3
    side = place[SIDE]
    copies = [
        pltpu.make_async_copy(
            w_own.at[:, aligned((2 * k + side) * part, part)],
            w.at[0, :, pl.ds(k * part, part)],
            sems.at[k],
        )
        for k in range(3)
    ]
    copies.append(pltpu.make_async_copy(w_far, w.at[1], sems.at[3]))
    copies.append(pltpu.make_async_copy(w_near, w.at[2], sems.at[4]))
    copies.append(pltpu.make_async_copy(w_across, w.at[3], sems.at[5]))
    for copy in copies:
        copy.start()
    ready()
    rows[:half, :] = rows_of(d_qkv, 0)
    rows[half:, :] = rows_of(d_qkv, 1)
    for copy in copies:
        copy.wait()

    def step(rank, carry):
        columns = aligned(place[rank] * width, width)
        value = times_transposed(rows[...], w[rank])
        kept[:, columns] = value[:half]
        leaving[:, columns] = value[half:].astype(BF16)
        return carry

    lax.fori_loop(0, 4, step, 0)


def back_first(place, d_qkv, w_own, w_far, w_near, w_across):
    rows, wide = POS * d_qkv[0].shape[-2], d_qkv[0].shape[-1]
    return kernel_call(
        back_first_kernel,
        "back_first",
        [(SMEM, place), (HBM, w_own), (HBM, w_far), (HBM, w_near), (HBM, w_across),
         in_vmem(*d_qkv)],
        [((rows // 2, D), F32), ((rows // 2, D), BF16), ((rows, wide), BF16)],
        [pltpu.VMEM((4, w_own.shape[0], wide), BF16), pltpu.SemaphoreType.DMA((6,))],
    )


def last_kernel(
    ready, place, kept, far, x_a, gains, d_resid, down_kept, down_far, blocks, gain_terms, sums
):
    ready()
    blocks = views(blocks, place)
    width = gain_terms.shape[2]
    rows = x_a[...].astype(F32)
    scale = lax.rsqrt(jnp.mean(rows * rows, axis=-1, keepdims=True) + EPSILON)
    normed = rows * scale
    d_rows = kept[...] + far[...].astype(F32)
    sums[...] = jnp.sum(d_rows * normed, axis=0, keepdims=True)
    scaled = d_rows * gains[0:1, :]
    value = d_resid[...] + scale * (
        scaled - normed * jnp.mean(scaled * normed, axis=-1, keepdims=True)
    )
    put_rows(blocks, 0, slice(None), value.astype(BF16))
    put_rows(blocks, 1, slice(None), (down_kept[...] + down_far[...].astype(F32)).astype(BF16))
    for slot, rank in enumerate((OWN, NEAR, FAR, ACROSS)):
        gain_terms[slot] = sums[:, aligned(place[rank] * width, width)]


def last(place, kept, far, x_a, gains, d_resid, down_kept, down_far):
    half = kept.shape[0]
    return kernel_call(
        last_kernel,
        "last",
        [(SMEM, place)]
        + in_vmem(kept, far)
        + in_stage(x_a, gains, d_resid, down_kept)
        + in_vmem(down_far),
        [block_shapes(2 * half, D, True), ((4, 1, D // 4), F32)],
        [pltpu.VMEM((1, D), F32)],
    )


def both_rows(own, near, columns):
    return jnp.concatenate([own[:, columns], near[:, columns]], 0)


def leaving_kernel(
    first_block, ready, place, left_own, left_near, right_own, right_near, leaving
):
    ready()
    width = leaving.shape[0]
    left = both_rows(left_own, left_near, aligned(place[ACROSS] * width, width))

    def step(j, carry):
        columns = aligned(j * 256, 256)
        right = both_rows(
            right_own, right_near, aligned((first_block + j) * 256, 256)
        )
        leaving[:, columns] = inner_rows(left, right).astype(BF16)
        return carry

    lax.fori_loop(0, leaving.shape[1] // 256, step, 0)


def leaving_gradient(place, blocks, left_own, left_near, right_own, right_near):
    width, wide = D // 4, 256 * (blocks[1] - blocks[0])
    return kernel_call(
        functools.partial(leaving_kernel, blocks[0]),
        "leaving_gradient",
        [(SMEM, place)] + in_stage(left_own, left_near, right_own, right_near),
        [((width, wide), BF16)],
    )[0]


def staying_kernel(parts, ready, place, left_own, left_near, right_own, right_near, *rest):
    ready()
    come, grad = rest[:-1], rest[-1]
    width = grad.shape[0]
    part = grad.shape[1] // 2 // parts
    side = place[SIDE]
    left = both_rows(left_own, left_near, aligned(place[OWN] * width, width))

    def put(block, who, value):
        if parts == 2:
            spots = [(0, block * 128, 0, 128), (1, block * 128, 128, 256)]
        else:
            spots = [(block // 2, (block % 2) * 256, 0, 256)]
        for k, start, low, high in spots:
            grad[:, aligned((2 * k + who) * part + start, high - low)] = value[:, low:high]

    def step(j, carry):
        right = both_rows(right_own, right_near, aligned(j * 256, 256))
        put(j, side, inner_rows(left, right))
        return carry

    lax.fori_loop(0, right_own.shape[1] // 256, step, 0)
    base = 0
    for piece in come:
        count = piece.shape[1] // 256

        def take(j, carry, piece=piece, base=base):
            put(base + j, 1 - side, piece[:, aligned(j * 256, 256)].astype(F32))
            return carry

        lax.fori_loop(0, count, take, 0)
        base += count


def staying_gradient(parts, place, left_own, left_near, right_own, right_near, *come):
    width = D // 4
    arrays = (left_own, left_near, right_own, right_near) + come
    return kernel_call(
        functools.partial(staying_kernel, parts),
        "staying_gradient",
        [(SMEM, place)] + in_stage(*arrays),
        [((width, 2 * right_own.shape[1]), F32)],
    )[0]


def grad_out_kernel(ready, place, mixed_own, mixed_near, d_own, d_near, grad):
    ready()
    left = both_rows(
        mixed_own, mixed_near, aligned(place[CORE] * grad.shape[0], grad.shape[0])
    )
    for base in range(0, D, 512):
        at = slice(base, base + 512)
        grad[:, at] = inner_rows(left, jnp.concatenate([d_own[:, at], d_near[:, at]], 0))


def grad_out_rows(place, mixed_own, mixed_near, d_own, d_near):
    width = mixed_own.shape[1] // 2
    return kernel_call(
        grad_out_kernel,
        "grad_out",
        [(SMEM, place)] + in_stage(mixed_own, mixed_near, d_own, d_near),
        [((width, D), F32)],
    )[0]


def grad_down_kernel(ready, place, h_own, h_near, ca_own, cb_own, ca_near, cb_near, grad, wide):
    ready()
    count, window = grad.shape[0], wide.shape[0]
    core = place[CORE]
    skip = h_own.shape[1] - window
    left = both_rows(h_own, h_near, aligned(core * skip, window))

    def step(n, carry):
        columns = aligned(n * 256, 256)
        right = jnp.concatenate(
            [ref[:, columns] for ref in (ca_own, cb_own, ca_near, cb_near)], 0
        )
        wide[:, columns] = inner_rows(left, right)
        return carry

    lax.fori_loop(0, D // 256, step, 0)
    grad[...] = wide[aligned(core * (count - skip), count, 64), :]


def grad_down_rows(place, h_own, h_near, ca_own, cb_own, ca_near, cb_near):
    count = h_own.shape[1] // 2
    window = -(-count // 128) * 128
    return kernel_call(
        grad_down_kernel,
        "grad_down",
        [(SMEM, place)] + in_stage(h_own, h_near, ca_own, cb_own, ca_near, cb_near),
        [((count, D), F32)],
        [pltpu.VMEM((window, D), F32)],
    )[0]


def half_columns_kernel(parts, far, ready, place, weight, half, sems):
    part = half.shape[1] // parts
    side = 1 - place[SIDE] if far else place[SIDE]
    copies = [
        pltpu.make_async_copy(
            weight.at[:, aligned((2 * k + side) * part, part)],
            half.at[:, pl.ds(k * part, part)],
            sems.at[k],
        )
        for k in range(parts)
    ]
    for copy in copies:
        copy.start()
    for copy in copies:
        copy.wait()


def half_columns(place, weight, parts, far):
    count, width = weight.shape
    return kernel_call(
        functools.partial(half_columns_kernel, parts, far),
        "far_columns" if far else "kept_columns",
        [(SMEM, place), (HBM, weight)],
        [((count, width // 2), BF16)],
        [pltpu.SemaphoreType.DMA((parts,))],
    )[0]


def spread_kernel(split, ready, place, weight, kept_a, kept_b, leaving_a, leaving_b, sems):
    part = weight.shape[1] // 4
    side = place[SIDE]
    copies = []
    for k in range(2):
        for j in range(part // 128):
            for who, targets in ((side, (kept_a, kept_b)), (1 - side, (leaving_a, leaving_b))):
                target, at = (targets[0], j) if j < split else (targets[1], j - split)
                copies.append(
                    pltpu.make_async_copy(
                        weight.at[:, aligned((2 * k + who) * part + j * 128, 128)],
                        target.at[:, pl.ds(at * 256 + k * 128, 128)],
                        sems.at[len(copies)],
                    )
                )
    for copy in copies:
        copy.start()
    for copy in copies:
        copy.wait()


def spread(place, weight, split):
    count, width = weight.shape
    sizes = (256 * split, width // 2 - 256 * split) * 2
    return kernel_call(
        functools.partial(spread_kernel, split),
        "spread",
        [(SMEM, place), (HBM, weight)],
        [((count, size), BF16) for size in sizes],
        [pltpu.SemaphoreType.DMA((width // 128,))],
    )


def sync(*values):
    return lax.optimization_barrier(values)


def after(value, *earlier):
    return lax.optimization_barrier((value,) + earlier)[0]


def pair_body(frames_in, segment_ids, gain_attn, w_qkv, w_out, gain_ffn, w_gate_up, w_down, cotangent):
    member = lax.axis_index("fsdp") % 4
    side, core = member >> 1, member & 1
    position = lax.axis_index("fsdp") // 4
    place = jnp.stack([member, member ^ 2, member ^ 1, member ^ 3, side, core, position])
    place = place.astype(jnp.int32)
    frames = frames_in.shape[0] // POS
    half = POS * frames

    blocks = w_gate_up.shape[1] // 512
    split = (blocks * 7) // 11
    near = lambda rows: swap(rows, 1)

    qkv_leaving = half_columns(place, w_qkv, 3, True)
    qkv_across = swap(qkv_leaving, 3)
    qkv_far = near(qkv_across)
    sent = to_positions(place, after(frames_in, qkv_leaving), cotangent)
    came = exchange(sent)
    sent = sent[0]
    ids_own = segment_ids.reshape(frames, POS).T
    ids_own = jnp.take(ids_own, jnp.arange(POS) ^ position, axis=0).reshape(1, half)
    ids_far = swap(after(ids_own, sent), 2)
    gains_own = jnp.stack([gain_attn, gain_ffn])
    gains_far = swap(after(gains_own, sent), 2)
    qkv_kept = half_columns(place, after(w_qkv, sent), 3, False)
    came, ids_far, gains_far, qkv_kept, qkv_far = sync(came, ids_far, gains_far, qkv_kept, qkv_far)

    x_own, c_own = collect(place, came)
    x_far, c_far = swap(x_own, 2), swap(c_own, 2)
    gains_near = near(jnp.stack([gains_own, gains_far]))
    qkv_near = near(qkv_kept)
    kept_a, kept_b, leaving_a, leaving_b = spread(place, after(w_gate_up, x_own), split)
    x_far, gains_near, qkv_near, leaving_a, c_own, c_far = sync(
        x_far, gains_near, qkv_near, leaving_a, c_own, c_far
    )

    qkv_sent, lowered_first, gains = first(
        place, x_own, x_far, gains_own, gains_far, gains_near[0], gains_near[1],
        w_qkv, qkv_far, qkv_near, qkv_across,
    )
    across_a = swap(after(leaving_a, lowered_first), 3)
    near_a, near_b, out_near, down_near = (
        near(after(a, lowered_first)) for a in (kept_a, kept_b, w_out, w_down)
    )
    qkv, across_a, near_a, near_b, out_near, down_near = sync(
        exchange(qkv_sent), across_a, near_a, near_b, out_near, down_near
    )

    mixed_sent = attend_local(place, ids_own, ids_far, qkv)
    across_b = swap(after(leaving_b, across_a), 3)
    far_a = near(across_a)
    c_own_near, c_far_near, lowered_first_near = (
        near(after(a, mixed_sent[0])) for a in (c_own, c_far, lowered_first)
    )
    mixed, across_b, far_a, c_own_near, c_far_near, lowered_first_near = sync(
        exchange(mixed_sent), across_b, far_a, c_own_near, c_far_near, lowered_first_near
    )

    term, leaving, mixed = out_term(place, mixed, w_out, out_near)
    far = swap(leaving, 2)
    far, mixed_near, far_b = sync(far, near(mixed), near(after(across_b, leaving)))
    pieces = (kept_a, far_a, near_a, across_a, kept_b, far_b, near_b, across_b)
    resid, lowered_second, hidden, d_gate_up, second, leaving = ffn(
        place, x_own, x_far, term, far, gains, c_own, c_far, pieces, w_down, down_near
    )

    second_far = swap(leaving, 2)
    hidden_near, lowered_second_near, d_gate_up_near = (
        near(after(rows, leaving)) for rows in (hidden, lowered_second, d_gate_up)
    )
    down_kept, down_leaving = down_term(place, after(hidden, leaving), resid, w_down, down_near)
    sides = (lowered_second, lowered_second_near, d_gate_up, d_gate_up_near)
    cut = (blocks * 5) // 11
    gate_up_leaving = leaving_gradient(place, (0, cut), *sides)
    second_far, down_leaving, gate_up_leaving, hidden_near, lowered_second_near = sync(
        second_far, down_leaving, gate_up_leaving, hidden_near, lowered_second_near
    )

    d_resid, d_branch, gain_ffn_terms, d_mixed = mid(
        place, second, second_far, resid, gains, c_own, c_far, w_out, out_near
    )
    gate_up_come = swap(gate_up_leaving, 3)
    sides = (after(lowered_second, d_branch), lowered_second_near, d_gate_up, d_gate_up_near)
    gate_up_leaving_rest = leaving_gradient(place, (cut, blocks), *sides)
    d_branch_near, gain_ffn_near = near(d_branch), near(gain_ffn_terms[1])
    d_mixed, gate_up_come, gate_up_leaving_rest, d_branch_near, gain_ffn_near = sync(
        exchange(d_mixed), gate_up_come, gate_up_leaving_rest, d_branch_near, gain_ffn_near,
    )

    d_qkv_sent = attend_back_local(place, ids_own, ids_far, qkv, d_mixed)
    gate_up_come_rest = swap(gate_up_leaving_rest, 3)
    grad_down = grad_down_rows(
        place, after(hidden, d_qkv_sent[0]), hidden_near, c_own, c_far, c_own_near, c_far_near
    )
    grad_out = grad_out_rows(place, mixed, mixed_near, after(d_branch, d_qkv_sent[0]), d_branch_near)
    d_qkv, gate_up_come_rest, grad_down, grad_out = sync(
        exchange(d_qkv_sent), gate_up_come_rest, grad_down, grad_out
    )

    kept, leaving, d_projected = back_first(
        place, d_qkv, w_qkv, qkv_far, qkv_near, qkv_across
    )
    first_far = swap(leaving, 2)
    down_far = swap(after(down_leaving, leaving), 2)
    qkv_sides = (lowered_first, lowered_first_near, d_projected, near(d_projected))
    qkv_grad_leaving = leaving_gradient(place, (0, qkv_leaving.shape[1] // 256), *qkv_sides)
    first_far, down_far, qkv_grad_leaving = sync(first_far, down_far, qkv_grad_leaving)

    qkv_come = swap(qkv_grad_leaving, 3)
    out_sent, gain_attn_terms = last(
        place, kept, first_far, x_own, gains, d_resid, down_kept, down_far
    )
    grad_gate_up = staying_gradient(
        2, place, after(sides[0], gain_attn_terms), *sides[1:], gate_up_come, gate_up_come_rest
    )
    gain_sums = gain_attn_terms[:2] + swap(gain_attn_terms[2:], 2)
    gain_attn_grad = gain_sums[0] + near(gain_sums[1])
    out_come, grad_gate_up = sync(exchange(out_sent), grad_gate_up)
    grad_qkv = staying_gradient(3, place, *qkv_sides, qkv_come)
    grad_in, block_out = to_frames(place, out_come)
    gain_ffn_grad = (gain_ffn_terms[0] + gain_ffn_near).reshape(-1)
    return (
        block_out,
        grad_in,
        gain_attn_grad.reshape(-1),
        grad_qkv,
        grad_out,
        gain_ffn_grad,
        grad_gate_up,
        grad_down,
    )


def solution(mesh):
    in_specs = (
        P("fsdp", None),
        P("fsdp"),
        P("fsdp"),
        P("fsdp", None),
        P("fsdp", None),
        P("fsdp"),
        P("fsdp", None),
        P("fsdp", None),
        P("fsdp", None),
    )
    out_specs = (
        P("fsdp", None),
        P("fsdp", None),
        P("fsdp"),
        P("fsdp", None),
        P("fsdp", None),
        P("fsdp"),
        P("fsdp", None),
        P("fsdp", None),
    )
    chosen = pair_body if mesh.shape["fsdp"] == 4 * POS else body
    return jax.shard_map(chosen, mesh=mesh, in_specs=in_specs, out_specs=out_specs, check_vma=False)
```

```python
import functools
import math

import jax
import jax.numpy as jnp
from jax import lax
from jax.experimental import pallas as pl
from jax.experimental.pallas import tpu as pltpu
from jax.sharding import PartitionSpec as P

D = 1024
FF = 2816
HEADS = 16
HEAD_DIM = 64
POS = 8


EPSILON = 1e-05


def for_sending(array):

    def short(part):
        return part.astype(jnp.bfloat16) if part.dtype == jnp.float32 else part

    return jax.tree.map(short, array)


def swapped(block, axis, stride):
    count = lax.axis_size(axis)
    route = []
    for low in range(count):
        high = low | 1 << stride
        if high != low and high < count:
            route += [(low, high), (high, low)]
    return lax.ppermute(block, axis, route)


def positions_layout(frame_rows, groups):
    width = frame_rows.shape[-1]
    per_piece = frame_rows.shape[0] // POS // groups
    shaped = frame_rows.reshape(groups, per_piece, POS, width).transpose(2, 0, 1, 3)
    return shaped.reshape(POS * groups, per_piece, width)


def frames_layout(piece_rows, groups):
    width = piece_rows.shape[-1]
    per_piece = piece_rows.shape[1]
    shaped = piece_rows.reshape(POS, groups, per_piece, width).transpose(1, 2, 0, 3)
    return shaped.reshape(groups * per_piece * POS, width)


def inner_rows(left, right):
    return lax.dot_general(
        left, right, (((0,), (0,)), ((), ())), preferred_element_type=jnp.float32
    )


def times_transposed(left, right):
    return lax.dot_general(
        left, right, (((1,), (1,)), ((), ())), preferred_element_type=jnp.float32
    )


def join_pieces(current, partner, member, bit_level):
    upper_half = member >> bit_level & 1 == 1
    return tuple(
        (
            jnp.where(
                upper_half,
                jnp.concatenate([theirs, own_piece], 0),
                jnp.concatenate([own_piece, theirs], 0),
            )
            for own_piece, theirs in zip(current, partner)
        )
    )


def collect_forward(pieces, member, levels):
    current = pieces
    for bit_level in range(levels):
        partner = jax.tree.map(
            lambda part, own: part.astype(own.dtype),
            swapped(for_sending(current), "fsdp", bit_level),
            current,
        )
        current = join_pieces(current, partner, member, bit_level)
    return current


def collect_again(pieces, member, levels):
    current = pieces
    for bit_level in range(levels):
        partner = jax.tree.map(
            lambda part, own: part.astype(own.dtype),
            swapped(for_sending(current), "fsdp", bit_level),
            current,
        )
        current = join_pieces(current, partner, member, bit_level)
    return current


def halving_sum(terms, member, levels, sender):
    current = terms
    for bit_level in reversed(range(levels)):
        upper_half = member >> bit_level & 1 == 1
        leaving = tuple(
            (
                jnp.where(
                    upper_half,
                    term_part[: term_part.shape[0] // 2],
                    term_part[term_part.shape[0] // 2 :],
                )
                for term_part in current
            )
        )
        staying = tuple(
            (
                jnp.where(
                    upper_half,
                    term_part[term_part.shape[0] // 2 :],
                    term_part[: term_part.shape[0] // 2],
                )
                for term_part in current
            )
        )
        arrived = sender(leaving, bit_level)
        current = tuple((held_part + come_part for held_part, come_part in zip(staying, arrived)))
    return current


def send_whole(parts, bit_level):
    return jax.tree.map(
        lambda part, own: part.astype(own.dtype),
        swapped(for_sending(parts), "fsdp", bit_level),
        parts,
    )


def permitted(validity):
    row_place = lax.broadcasted_iota(jnp.int32, (POS, POS), 0)
    column_place = lax.broadcasted_iota(jnp.int32, (POS, POS), 1)
    causal = column_place <= row_place
    same_segment = validity[:, :, None] == validity[:, None, :]
    return (causal[None] & same_segment)[:, None]


def split_projections(qkv_frames):
    frames = qkv_frames.shape[0] // POS
    shaped = qkv_frames.reshape(frames, POS, 3, HEADS, HEAD_DIM)
    return (shaped[:, :, 0], shaped[:, :, 1], shaped[:, :, 2])


def masked_scores(queries, key_rows, allowed):
    scores = jnp.einsum(
        "fqhd,fkhd->fhqk", queries, key_rows, preferred_element_type=jnp.float32
    ) * HEAD_DIM ** (-0.5)
    return jnp.where(allowed, scores, -jnp.inf)


def attend(qkv_frames, validity):
    queries, key_rows, value_rows = split_projections(qkv_frames)
    scores = masked_scores(queries, key_rows, permitted(validity))
    highest = jnp.max(scores, axis=-1, keepdims=True)
    raised = jnp.exp(scores - highest)
    totals = jnp.sum(raised, axis=-1, keepdims=True)
    attn_probs = (raised / totals).astype(jnp.bfloat16)
    attended = jnp.einsum(
        "fhqk,fkhd->fqhd", attn_probs, value_rows, preferred_element_type=jnp.float32
    )
    mixed_heads = attended.reshape(qkv_frames.shape[0], D).astype(jnp.bfloat16)
    return (mixed_heads, highest + jnp.log(totals))


def attend_back(qkv_frames, validity, log_total, d_mixed):
    queries, key_rows, value_rows = split_projections(qkv_frames)
    frames = queries.shape[0]
    scores = masked_scores(queries, key_rows, permitted(validity))
    weights_full = jnp.exp(scores - log_total)
    attn_probs = weights_full.astype(jnp.bfloat16)
    d_heads = d_mixed.reshape(frames, POS, HEADS, HEAD_DIM)
    d_probs = jnp.einsum("fqhd,fkhd->fhqk", d_heads, value_rows, preferred_element_type=jnp.float32)
    d_values = jnp.einsum(
        "fhqk,fqhd->fkhd", attn_probs, d_heads, preferred_element_type=jnp.float32
    )
    d_scores = weights_full * (d_probs - jnp.sum(d_probs * weights_full, axis=-1, keepdims=True))
    d_scores = d_scores.astype(jnp.bfloat16)
    d_queries = jnp.einsum(
        "fhqk,fkhd->fqhd", d_scores, key_rows, preferred_element_type=jnp.float32
    ) * HEAD_DIM ** (-0.5)
    d_keys = jnp.einsum(
        "fhqk,fqhd->fkhd", d_scores, queries, preferred_element_type=jnp.float32
    ) * HEAD_DIM ** (-0.5)
    stacked = jnp.stack([d_queries, d_keys, d_values], axis=2)
    return stacked.reshape(frames * POS, 3 * D).astype(jnp.bfloat16)


def body(frames_in, segment_ids, gain_attn, w_qkv, w_out, gain_ffn, w_gate_up, w_down, cotangent):
    devices = lax.axis_size("fsdp")
    groups = devices // POS
    levels = groups.bit_length() - 1
    member = lax.axis_index("fsdp") % groups
    per_piece = frames_in.shape[0] // POS // groups
    validity = segment_ids.reshape(-1, POS)
    moved_input, moved_cotangent = (
        lax.all_to_all(
            positions_layout(frames_in, groups), "fsdp", split_axis=0, concat_axis=0, tiled=True
        ),
        lax.all_to_all(
            positions_layout(cotangent, groups), "fsdp", split_axis=0, concat_axis=0, tiled=True
        ),
    )
    inputs = moved_input.reshape(-1, D).astype(jnp.float32)
    upstream = moved_cotangent.reshape(-1, D)
    own_pieces = (w_qkv, w_out, w_gate_up, w_down, gain_attn, gain_ffn)
    collected = collect_forward(own_pieces, member, levels)
    whole_qkv, whole_out, whole_gate_up, whole_down, whole_gain_attn, whole_gain_ffn = collected
    gain_first = whole_gain_attn.astype(jnp.float32)
    gain_second = whole_gain_ffn.astype(jnp.float32)
    scale_first = lax.rsqrt(jnp.mean(inputs * inputs, axis=-1, keepdims=True) + EPSILON)
    normed_first = inputs * scale_first
    lowered_first = (normed_first * gain_first).astype(jnp.bfloat16)
    projected = jnp.dot(lowered_first, whole_qkv, preferred_element_type=jnp.float32).astype(
        jnp.bfloat16
    )
    qkv_frames = frames_layout(
        lax.all_to_all(
            projected.reshape(devices, per_piece, 3 * D),
            "fsdp",
            split_axis=0,
            concat_axis=0,
            tiled=True,
        ),
        groups,
    )
    mixed_frames, log_total = attend(qkv_frames, validity)
    mixed_rows = lax.all_to_all(
        positions_layout(mixed_frames, groups), "fsdp", split_axis=0, concat_axis=0, tiled=True
    ).reshape(-1, D)
    residual = inputs + jnp.dot(mixed_rows, whole_out, preferred_element_type=jnp.float32)
    scale_second = lax.rsqrt(jnp.mean(residual * residual, axis=-1, keepdims=True) + EPSILON)
    normed_second = residual * scale_second
    lowered_second = (normed_second * gain_second).astype(jnp.bfloat16)
    gate_up = jnp.dot(lowered_second, whole_gate_up, preferred_element_type=jnp.float32)
    gate_part = gate_up[:, :FF]
    up_part = gate_up[:, FF:]
    sigmoid_gate = jax.nn.sigmoid(gate_part)
    activated = gate_part * sigmoid_gate
    hidden = (activated * up_part).astype(jnp.bfloat16)
    result_rows = (
        residual + jnp.dot(hidden, whole_down, preferred_element_type=jnp.float32)
    ).astype(jnp.bfloat16)
    block_out = frames_layout(
        lax.all_to_all(
            result_rows.reshape(devices, per_piece, D),
            "fsdp",
            split_axis=0,
            concat_axis=0,
            tiled=True,
        ),
        groups,
    )
    collected = collect_again(own_pieces, member, levels)
    whole_qkv, whole_out, whole_gate_up, whole_down, whole_gain_attn, whole_gain_ffn = collected
    gain_first = whole_gain_attn.astype(jnp.float32)
    gain_second = whole_gain_ffn.astype(jnp.float32)
    grad_down_term = inner_rows(hidden, upstream)
    d_hidden = times_transposed(upstream, whole_down)
    d_gate = d_hidden * up_part * sigmoid_gate * (1.0 + gate_part * (1.0 - sigmoid_gate))
    d_up = d_hidden * activated
    d_gate_up = jnp.concatenate([d_gate, d_up], axis=1).astype(jnp.bfloat16)
    grad_gate_up_term = inner_rows(lowered_second, d_gate_up)
    d_second = times_transposed(d_gate_up, whole_gate_up)
    grad_gain_ffn_term = jnp.sum(d_second * normed_second, axis=0)
    scaled_second = d_second * gain_second
    d_residual = upstream.astype(jnp.float32) + scale_second * (
        scaled_second
        - normed_second * jnp.mean(scaled_second * normed_second, axis=-1, keepdims=True)
    )
    d_branch = d_residual.astype(jnp.bfloat16)
    grad_out_term = inner_rows(mixed_rows, d_branch)
    d_mixed = times_transposed(d_branch, whole_out).astype(jnp.bfloat16)
    d_mixed_frames = frames_layout(
        lax.all_to_all(
            d_mixed.reshape(devices, per_piece, D), "fsdp", split_axis=0, concat_axis=0, tiled=True
        ),
        groups,
    )
    d_qkv_frames = attend_back(qkv_frames, validity, log_total, d_mixed_frames)
    d_projected = lax.all_to_all(
        positions_layout(d_qkv_frames, groups), "fsdp", split_axis=0, concat_axis=0, tiled=True
    ).reshape(-1, 3 * D)
    grad_qkv_term = inner_rows(lowered_first, d_projected)
    d_first = times_transposed(d_projected, whole_qkv)
    grad_gain_attn_term = jnp.sum(d_first * normed_first, axis=0)
    scaled_first = d_first * gain_first
    d_inputs = d_residual + scale_first * (
        scaled_first - normed_first * jnp.mean(scaled_first * normed_first, axis=-1, keepdims=True)
    )
    grad_in = frames_layout(
        lax.all_to_all(
            d_inputs.reshape(devices, per_piece, D).astype(jnp.bfloat16),
            "fsdp",
            split_axis=0,
            concat_axis=0,
            tiled=True,
        ).astype(jnp.float32),
        groups,
    )
    shares = halving_sum(
        (
            grad_qkv_term,
            grad_out_term,
            grad_gate_up_term,
            grad_down_term,
            grad_gain_attn_term,
            grad_gain_ffn_term,
        ),
        member,
        levels,
        send_whole,
    )
    return (block_out, grad_in, shares[4], shares[0], shares[1], shares[5], shares[2], shares[3])

VMEM = pl.BlockSpec(memory_space=pltpu.VMEM)
SMEM = pl.BlockSpec(memory_space=pltpu.SMEM)
HBM = pl.BlockSpec(memory_space=pltpu.HBM)
STAGED = pl.BlockSpec(memory_space=pltpu.HBM)
MOVED = pl.BlockSpec(memory_space=pl.ANY)
BF16 = jnp.bfloat16
F32 = jnp.float32
OWN, FAR, NEAR, ACROSS, SIDE, CORE, POSITION = range(7)


def swap(block, mask):
    count = lax.axis_size("fsdp")
    return lax.ppermute(block, "fsdp", [(i, i ^ mask) for i in range(count)])


def exchange(blocks):
    count = lax.axis_size("fsdp")
    stride = count // POS
    if len(blocks) == POS:
        return [blocks[0]] + [swap(blocks[k], stride * k) for k in range(1, POS)]
    lanes = [[r + stride * k for k in range(POS)] for r in range(stride)]
    return [
        lax.all_to_all(
            blocks[0], "fsdp", split_axis=0, concat_axis=0, tiled=True, axis_index_groups=lanes
        )
    ]


def kernel_call(kernel, name, args, outs, scratch=(), out_spec=None, aliases=()):
    flat = lambda items: [p for item in items for p in (item if isinstance(item, list) else [item])]
    staged = [n for n, (spec, _) in enumerate(flat(args)) if spec is STAGED or spec is MOVED]
    arrays = [
        pltpu.with_memory_space_constraint(a, pltpu.HBM) if spec is STAGED or spec is HBM else a
        for spec, a in flat(args)
    ]
    scratch = list(scratch)
    own = len(scratch)
    scratch += [pltpu.VMEM(arrays[n].shape, arrays[n].dtype) for n in staged]
    scratch += [pltpu.SemaphoreType.DMA((max(len(staged), 1),))]
    held = sum(
        math.prod(ref.shape) * jnp.dtype(ref.dtype).itemsize
        for ref in scratch
        if ref.memory_space == pltpu.VMEM
    )

    def grouped(items, values):
        return [
            [next(values) for _ in item] if isinstance(item, list) else next(values)
            for item in items
        ]

    def body_kernel(*refs):
        inputs, outputs = list(refs[: len(arrays)]), refs[len(arrays) :]
        outputs, extra = outputs[: len(flat(outs))], outputs[len(flat(outs)) :]
        extra, landing, sems = extra[:own], extra[own:-1], extra[-1]
        copies = []
        for k, n in enumerate(staged):
            copies.append(pltpu.make_async_copy(inputs[n], landing[k], sems.at[k]))
            inputs[n] = landing[k]
        for copy in copies:
            copy.start()

        def ready():
            for copy in copies:
                copy.wait()

        kernel(ready, *grouped(args, iter(inputs)), *grouped(outs, iter(outputs)), *extra)

    result = pl.pallas_call(
        body_kernel,
        name=name,
        in_specs=[spec for spec, _ in flat(args)],
        out_specs=[out_spec or VMEM] * len(flat(outs)),
        out_shape=[
            pltpu.HBM(s, d) if out_spec is HBM else jax.ShapeDtypeStruct(s, d)
            for s, d in flat(outs)
        ],
        input_output_aliases=dict(aliases),
        scratch_shapes=scratch,
        cost_estimate=pl.CostEstimate(flops=1, bytes_accessed=1, transcendentals=0),
        compiler_params=pltpu.CompilerParams(vmem_limit_bytes=held + (8 << 20)),
    )(*arrays)
    return grouped(outs, iter(result))


def views(blocks, place):
    if len(blocks) == POS:
        return blocks
    return [blocks[0].at[place[POSITION] ^ k] for k in range(POS)]


def matmul(left, right):
    return jnp.dot(left, right, preferred_element_type=F32)


def aligned(start, size, step=128):
    return pl.ds(pl.multiple_of(start, step), size)


def rows_of(refs, rel, columns=slice(None)):
    frames = refs[0].shape[0] // 2
    return jnp.concatenate([ref[rel * frames : (rel + 1) * frames, columns] for ref in refs], 0)


def put_rows(refs, rel, columns, value):
    frames = refs[0].shape[0] // 2
    for k, ref in enumerate(refs):
        ref[rel * frames : (rel + 1) * frames, columns] = value[k * frames : (k + 1) * frames]


def block_shapes(rows, width, joined):
    if joined:
        return [((POS, rows // POS, width), BF16)]
    return [((rows // POS, width), BF16)] * POS


def in_vmem(*arrays):
    return [(VMEM, a) for a in arrays]


def in_stage(*arrays):
    return [(STAGED, a) for a in arrays]


def moved(*arrays):
    return [(MOVED, a) for a in arrays]


def place_matrix(size, to_positions, position):
    frames = size // POS
    row = lax.broadcasted_iota(jnp.int32, (size, size), 0)
    column = lax.broadcasted_iota(jnp.int32, (size, size), 1)
    if not to_positions:
        row, column = column, row
    return (column == (row % frames) * POS + ((row // frames) ^ position)).astype(F32).astype(BF16)


def to_positions_kernel(ready, place, x_rows, c_rows, blocks):
    blocks = views(blocks, place)
    order = place_matrix(x_rows.shape[0], True, place[POSITION])
    ready()
    for rel, rows in enumerate((x_rows, c_rows)):
        put_rows(blocks, rel, slice(None), matmul(order, rows[...]).astype(BF16))


def to_positions(place, x_rows, c_rows):
    size, width = x_rows.shape
    return kernel_call(
        to_positions_kernel,
        "to_positions",
        [(SMEM, place)] + in_stage(x_rows, c_rows),
        [block_shapes(2 * size, width, True)],
    )[0]


def collect_kernel(ready, place, blocks, x_own, c_own):
    ready()
    blocks = views(blocks, place)
    x_own[...] = rows_of(blocks, 0)
    c_own[...] = rows_of(blocks, 1)


def collect(place, blocks):
    rows, width = blocks[0].shape[-2:]
    return kernel_call(
        collect_kernel,
        "collect",
        [(SMEM, place), in_vmem(*blocks)],
        [((rows * POS // 2, width), BF16)] * 2,
    )


def to_frames_kernel(ready, place, blocks, *rows):
    ready()
    blocks = views(blocks, place)
    order = place_matrix(rows[0].shape[0], False, place[POSITION])
    for rel in range(2):
        rows[rel][...] = matmul(order, rows_of(blocks, rel)).astype(rows[rel].dtype)


def to_frames(place, blocks):
    size = blocks[0].shape[-2] * POS // 2
    return kernel_call(
        to_frames_kernel,
        "to_frames",
        [(SMEM, place), in_vmem(*blocks)],
        [((size, D), F32), ((size, D), BF16)],
    )


def first_kernel(
    ready, place, x_a, x_b, gains_own, gains_far, gains_near, gains_across, w_own, w_far, w_near, w_across,
    qkv, lowered, gains, w, sems,
):
    qkv = views(qkv, place)
    half, width = x_a.shape[0], w_own.shape[0]
    part = w.shape[1] // 3
    side = place[SIDE]
    at_rows = lambda rank: aligned(place[rank] * width, width)
    copies = [
        pltpu.make_async_copy(
            w_own.at[:, aligned((2 * k + side) * part, part)],
            w.at[at_rows(OWN), pl.ds(k * part, part)],
            sems.at[k],
        )
        for k in range(3)
    ]
    copies.append(pltpu.make_async_copy(w_far, w.at[at_rows(FAR)], sems.at[3]))
    copies.append(pltpu.make_async_copy(w_near, w.at[at_rows(NEAR)], sems.at[4]))
    copies.append(pltpu.make_async_copy(w_across, w.at[at_rows(ACROSS)], sems.at[5]))
    for copy in copies:
        copy.start()
    ready()
    gains[:, at_rows(OWN)] = gains_own[...].astype(F32)
    gains[:, at_rows(FAR)] = gains_far[...].astype(F32)
    gains[:, at_rows(NEAR)] = gains_near[...].astype(F32)
    gains[:, at_rows(ACROSS)] = gains_across[...].astype(F32)
    gain = gains[0:1, :]
    for rel, ref in enumerate((x_a, x_b)):
        rows = ref[...].astype(F32)
        scale = lax.rsqrt(jnp.mean(rows * rows, axis=-1, keepdims=True) + EPSILON)
        lowered[rel * half : (rel + 1) * half, :] = (rows * scale * gain).astype(BF16)
    for copy in copies:
        copy.wait()

    def step(n, carry):
        columns = aligned(n * 256, 256, 256)
        value = matmul(lowered[...], w[:, columns]).astype(BF16)
        put_rows(qkv, 0, columns, value[:half])
        put_rows(qkv, 1, columns, value[half:])
        return carry

    lax.fori_loop(0, w.shape[1] // 256, step, 0)


def first(
    place, x_a, x_b, gains_own, gains_far, gains_near, gains_across, w_own, w_far, w_near, w_across
):
    half = x_a.shape[0]
    wide = w_far.shape[1]
    return kernel_call(
        first_kernel,
        "first",
        [(SMEM, place), (MOVED, x_a), (MOVED, x_b), (VMEM, gains_own), (VMEM, gains_far),
         (VMEM, gains_near), (VMEM, gains_across), (HBM, w_own), (HBM, w_far), (HBM, w_near),
         (HBM, w_across)],
        [block_shapes(2 * half, wide, True), ((2 * half, D), BF16), ((2, D), F32)],
        [pltpu.VMEM((D, wide), BF16), pltpu.SemaphoreType.DMA((6,))],
    )


def allowed_pairs(ids, position):
    size = ids.shape[1]
    frames = size // POS
    row = lax.broadcasted_iota(jnp.int32, (size, size), 0)
    column = lax.broadcasted_iota(jnp.int32, (size, size), 1)
    across = jnp.broadcast_to(ids.astype(F32), (size, size))
    same = (across == across.T) & (row % frames == column % frames)
    mask = same & ((column // frames) ^ position <= (row // frames) ^ position)
    return jnp.concatenate([mask, mask], 1)


def pair_of_heads(rows, low):
    return jnp.concatenate([rows * low, rows * (1 - low)], 0)


def lane_halves(value, reduce):
    size = value.shape[1] // 2
    parts = [
        jnp.broadcast_to(reduce(value[:, k * size : (k + 1) * size]), (value.shape[0], size))
        for k in range(2)
    ]
    return jnp.concatenate(parts, 1)


def pair_probs(query, key_pair, mask):
    scores = times_transposed(query, key_pair) * HEAD_DIM ** (-0.5)
    scores = jnp.where(mask, scores, -jnp.inf)
    raised = jnp.exp(scores - lane_halves(scores, lambda a: jnp.max(a, -1, keepdims=True)))
    return raised / lane_halves(raised, lambda a: jnp.sum(a, -1, keepdims=True))


def first_head_lanes():
    lane = lax.broadcasted_iota(jnp.int32, (1, 2 * HEAD_DIM), 1)
    return (lane < HEAD_DIM).astype(F32).astype(BF16)


def attend_kernel(ready, place, ids_a, ids_b, qkv, mixed):
    qkv, mixed = views(qkv, place), views(mixed, place)
    part = mixed[0].shape[1]
    low = first_head_lanes()
    ready()
    for rel, ids in enumerate((ids_a, ids_b)):
        mask = allowed_pairs(ids[...], place[POSITION])
        for base in range(0, part, 2 * HEAD_DIM):
            query, key_rows, value_rows = (
                rows_of(qkv, rel, slice(k * part + base, k * part + base + 2 * HEAD_DIM))
                for k in range(3)
            )
            probs = pair_probs(query, pair_of_heads(key_rows, low), mask)
            value = matmul(probs.astype(BF16), pair_of_heads(value_rows, low))
            put_rows(mixed, rel, slice(base, base + 2 * HEAD_DIM), value.astype(BF16))


def attend_local(place, ids_a, ids_b, qkv):
    rows, wide = qkv[0].shape[-2:]
    return kernel_call(
        attend_kernel,
        "attend",
        [(SMEM, place), (MOVED, ids_a), (MOVED, ids_b), moved(*qkv)],
        [block_shapes(rows * POS, wide // 3, True)],
    )[0]


def attend_back_kernel(ready, place, ids_a, ids_b, qkv, d_mixed, d_qkv):
    qkv, d_mixed, d_qkv = (views(blocks, place) for blocks in (qkv, d_mixed, d_qkv))
    part = d_mixed[0].shape[1]
    pair = 2 * HEAD_DIM
    low = first_head_lanes()
    size = POS * d_mixed[0].shape[0] // 2
    low_full = lax.broadcasted_iota(jnp.int32, (size, pair), 1) < HEAD_DIM
    scale = HEAD_DIM ** (-0.5)
    ready()
    for rel, ids in enumerate((ids_a, ids_b)):
        mask = allowed_pairs(ids[...], place[POSITION])
        for base in range(0, part, pair):
            query, key_rows, value_rows = (
                rows_of(qkv, rel, slice(k * part + base, k * part + base + pair))
                for k in range(3)
            )
            d_rows = rows_of(d_mixed, rel, slice(base, base + pair))
            keys = pair_of_heads(key_rows, low)
            probs = pair_probs(query, keys, mask)
            d_probs = times_transposed(d_rows, pair_of_heads(value_rows, low))
            inner = lane_halves(d_probs * probs, lambda a: jnp.sum(a, -1, keepdims=True))
            d_scores = (probs * (d_probs - inner)).astype(BF16)
            d_query = matmul(d_scores, keys) * scale
            d_key = inner_rows(d_scores, query) * scale
            d_value = inner_rows(probs.astype(BF16), d_rows)
            d_key = jnp.where(low_full, d_key[:size], d_key[size:])
            d_value = jnp.where(low_full, d_value[:size], d_value[size:])
            for k, value in enumerate((d_query, d_key, d_value)):
                columns = slice(k * part + base, k * part + base + pair)
                put_rows(d_qkv, rel, columns, value.astype(BF16))


def attend_back_local(place, ids_a, ids_b, qkv, d_mixed):
    rows, wide = qkv[0].shape[-2:]
    return kernel_call(
        attend_back_kernel,
        "attend_back",
        [(SMEM, place), (MOVED, ids_a), (MOVED, ids_b), moved(*qkv), in_vmem(*d_mixed)],
        [block_shapes(rows * POS, wide, True)],
    )[0]


def chip_rows(place, own, near, whole, sems):
    count = own.shape[0]
    core = place[CORE]
    return [
        pltpu.make_async_copy(own, whole.at[aligned(core * count, count, 64)], sems.at[0]),
        pltpu.make_async_copy(near, whole.at[aligned((1 - core) * count, count, 64)], sems.at[1]),
    ]


def out_kernel(ready, place, w_own, w_near, mixed, term, leaving, mixed_rows, w, sems):
    mixed = views(mixed, place)
    copies = chip_rows(place, w_own, w_near, w, sems)
    for copy in copies:
        copy.start()
    ready()
    rows = jnp.concatenate([rows_of(mixed, 0), rows_of(mixed, 1)], 0)
    mixed_rows[...] = rows
    half = rows.shape[0] // 2
    for copy in copies:
        copy.wait()
    for base in range(0, D, 512):
        value = matmul(rows, w[:, base : base + 512])
        term[:, base : base + 512] = value
        lowered = value.astype(BF16)
        leaving[:half, base : base + 512] = lowered[half:]
        leaving[half:, base : base + 512] = lowered[:half]


def out_term(place, mixed, w_own, w_near):
    rows = POS * mixed[0].shape[-2]
    inner = 2 * w_own.shape[0]
    return kernel_call(
        out_kernel,
        "out_term",
        [(SMEM, place), (HBM, w_own), (HBM, w_near), in_vmem(*mixed)],
        [((rows, D), F32), ((rows, D), BF16), ((rows, inner), BF16)],
        [pltpu.VMEM((inner, D), BF16), pltpu.SemaphoreType.DMA((2,))],
    )


def ffn_kernel(
    ready, place, x_a, x_b, term, far, gains, c_a, c_b, *rest
):
    pieces, (wd_own, wd_near) = rest[:4], rest[4:6]
    resid, lowered, hidden, d_gate_up, second, leaving = rest[6:12]
    w, wd, upstream, sems, down_sems = rest[12:]
    half, width, steps = x_a.shape[0], pieces[0].shape[0], w.shape[0]

    def begin(j, carry):
        for rank, source in enumerate(pieces):
            pltpu.make_async_copy(
                source.at[:, aligned(j * 256, 256)],
                w.at[j, aligned(place[rank] * width, width)],
                sems.at[j, rank],
            ).start()
        return carry

    down_copies = chip_rows(place, wd_own, wd_near, wd, down_sems)
    for copy in down_copies:
        copy.start()
    lax.fori_loop(0, steps, begin, 0)
    ready()
    gain = gains[1:2, :]
    for rel, (x_ref, c_ref) in enumerate(((x_a, c_a), (x_b, c_b))):
        at = pl.ds(rel * half, half)
        rows = x_ref[...].astype(F32) + (term[at, :] + far[at, :].astype(F32))
        resid[at, :] = rows
        scale = lax.rsqrt(jnp.mean(rows * rows, axis=-1, keepdims=True) + EPSILON)
        lowered[at, :] = (rows * scale * gain).astype(BF16)
        upstream[at, :] = c_ref[...]
    for copy in down_copies:
        copy.wait()

    def step(j, carry):
        for rank in range(4):
            rows = w.at[j, pl.ds(rank * width, width)]
            pltpu.make_async_copy(rows, rows, sems.at[j, rank]).wait()
        gate_up = matmul(lowered[...], w[j])
        gate, up = gate_up[:, :128], gate_up[:, 128:]
        d_hidden = times_transposed(upstream[...], wd[aligned(j * 128, 128), :])
        sigmoid = jax.nn.sigmoid(gate)
        activated = gate * sigmoid
        hidden[:, aligned(j * 128, 128)] = (activated * up).astype(BF16)
        d_gate = d_hidden * up * sigmoid * (1.0 + gate * (1.0 - sigmoid))
        d_gate_up[:, aligned(j * 256, 128)] = d_gate.astype(BF16)
        d_gate_up[:, aligned(j * 256 + 128, 128)] = (d_hidden * activated).astype(BF16)
        return carry

    lax.fori_loop(0, steps, step, 0)

    def back(n, carry):
        columns = aligned(n * 256, 256)
        value = times_transposed(d_gate_up[:, 0:256], w[0, columns, :])
        for j in range(1, steps):
            value += times_transposed(d_gate_up[:, j * 256 : (j + 1) * 256], w[j, columns, :])
        second[:, columns] = value
        lower = value.astype(BF16)
        leaving[:half, columns] = lower[half:]
        leaving[half:, columns] = lower[:half]
        return carry

    lax.fori_loop(0, D // 256, back, 0)


def ffn(place, x_a, x_b, term, far, gains, c_a, c_b, pieces, wd_own, wd_near):
    rows = term.shape[0]
    inner = 2 * wd_own.shape[0]
    wide, steps = 2 * inner, inner // 128
    return kernel_call(
        ffn_kernel,
        "ffn",
        [(SMEM, place)]
        + in_stage(x_a, x_b) + in_vmem(term, far) + in_stage(gains, c_a, c_b)
        + [(HBM, a) for a in pieces + (wd_own, wd_near)],
        [((rows, D), F32), ((rows, D), BF16), ((rows, inner), BF16), ((rows, wide), BF16),
         ((rows, D), F32), ((rows, D), BF16)],
        [pltpu.VMEM((steps, D, 256), BF16), pltpu.VMEM((inner, D), BF16),
         pltpu.VMEM((rows, D), BF16), pltpu.SemaphoreType.DMA((steps, 4)),
         pltpu.SemaphoreType.DMA((2,))],
    )


def down_kernel(ready, place, hidden, resid, w_own, w_near, kept, leaving, w, sems):
    copies = chip_rows(place, w_own, w_near, w, sems)
    for copy in copies:
        copy.start()
    half = kept.shape[0]
    ready()
    for copy in copies:
        copy.wait()

    def step(n, carry):
        columns = aligned(n * 256, 256)
        value = matmul(hidden[...], w[:, columns])
        kept[:, columns] = resid[:half, columns] + value[:half]
        leaving[:, columns] = value[half:].astype(BF16)
        return carry

    lax.fori_loop(0, D // 256, step, 0)


def down_term(place, hidden, resid, w_own, w_near):
    rows, inner = hidden.shape
    return kernel_call(
        down_kernel,
        "down_term",
        [(SMEM, place), (STAGED, hidden), (VMEM, resid), (HBM, w_own), (HBM, w_near)],
        [((rows // 2, D), F32), ((rows // 2, D), BF16)],
        [pltpu.VMEM((inner, D), BF16), pltpu.SemaphoreType.DMA((2,))],
    )


def mid_kernel(
    ready, place, second, far, resid, gains, c_a, c_b, w_own, w_near,
    d_resid, d_branch, gain_terms, d_mixed, w, sums, sems,
):
    d_mixed = views(d_mixed, place)
    copies = chip_rows(place, w_own, w_near, w, sems)
    for copy in copies:
        copy.start()
    half, width = c_a.shape[0], w_own.shape[0]
    total = None
    for rel in range(2):
        at = pl.ds(rel * half, half)
        rows = resid[at, :]
        scale = lax.rsqrt(jnp.mean(rows * rows, axis=-1, keepdims=True) + EPSILON)
        d_rows = second[at, :] + far[at, :].astype(F32)
        part = jnp.sum(d_rows * (rows * scale), axis=0, keepdims=True)
        total = part if total is None else total + part
    ready()
    gain = gains[1:2, :]
    for rel, c_ref in enumerate((c_a, c_b)):
        at = pl.ds(rel * half, half)
        rows = resid[at, :]
        scale = lax.rsqrt(jnp.mean(rows * rows, axis=-1, keepdims=True) + EPSILON)
        normed = rows * scale
        scaled = (second[at, :] + far[at, :].astype(F32)) * gain
        value = c_ref[...].astype(F32) + scale * (
            scaled - normed * jnp.mean(scaled * normed, axis=-1, keepdims=True)
        )
        if rel == 0:
            d_resid[...] = value
        d_branch[at, :] = value.astype(BF16)
    sums[...] = total
    gain_terms[0] = sums[:, aligned(place[OWN] * width, width)]
    gain_terms[1] = sums[:, aligned(place[NEAR] * width, width)]
    for copy in copies:
        copy.wait()
    for base in range(0, w.shape[0], 256):
        value = times_transposed(d_branch[...], w[base : base + 256, :]).astype(BF16)
        put_rows(d_mixed, 0, slice(base, base + 256), value[:half])
        put_rows(d_mixed, 1, slice(base, base + 256), value[half:])


def mid(place, second, far, resid, gains, c_a, c_b, w_own, w_near):
    rows = second.shape[0]
    width = w_own.shape[0]
    return kernel_call(
        mid_kernel,
        "mid",
        [(SMEM, place), (VMEM, second), (VMEM, far), (VMEM, resid), (STAGED, gains),
         (STAGED, c_a), (STAGED, c_b), (HBM, w_own), (HBM, w_near)],
        [((rows // 2, D), F32), ((rows, D), BF16), ((2, 1, width), F32),
         block_shapes(rows, 2 * width, True)],
        [pltpu.VMEM((2 * width, D), BF16), pltpu.VMEM((1, D), F32),
         pltpu.SemaphoreType.DMA((2,))],
    )


def back_first_kernel(
    ready, place, w_own, w_far, w_near, w_across, d_qkv, kept, leaving, rows, w, sems
):
    d_qkv = views(d_qkv, place)
    half, width = kept.shape[0], w_own.shape[0]
    part = w.shape[2] // 3
    side = place[SIDE]
    copies = [
        pltpu.make_async_copy(
            w_own.at[:, aligned((2 * k + side) * part, part)],
            w.at[0, :, pl.ds(k * part, part)],
            sems.at[k],
        )
        for k in range(3)
    ]
    copies.append(pltpu.make_async_copy(w_far, w.at[1], sems.at[3]))
    copies.append(pltpu.make_async_copy(w_near, w.at[2], sems.at[4]))
    copies.append(pltpu.make_async_copy(w_across, w.at[3], sems.at[5]))
    for copy in copies:
        copy.start()
    ready()
    rows[:half, :] = rows_of(d_qkv, 0)
    rows[half:, :] = rows_of(d_qkv, 1)
    for copy in copies:
        copy.wait()

    def step(rank, carry):
        columns = aligned(place[rank] * width, width)
        value = times_transposed(rows[...], w[rank])
        kept[:, columns] = value[:half]
        leaving[:, columns] = value[half:].astype(BF16)
        return carry

    lax.fori_loop(0, 4, step, 0)


def back_first(place, d_qkv, w_own, w_far, w_near, w_across):
    rows, wide = POS * d_qkv[0].shape[-2], d_qkv[0].shape[-1]
    return kernel_call(
        back_first_kernel,
        "back_first",
        [(SMEM, place), (HBM, w_own), (HBM, w_far), (HBM, w_near), (HBM, w_across),
         in_vmem(*d_qkv)],
        [((rows // 2, D), F32), ((rows // 2, D), BF16), ((rows, wide), BF16)],
        [pltpu.VMEM((4, w_own.shape[0], wide), BF16), pltpu.SemaphoreType.DMA((6,))],
    )


def last_kernel(
    ready, place, kept, far, x_a, gains, d_resid, down_kept, down_far, blocks, gain_terms, sums
):
    ready()
    blocks = views(blocks, place)
    width = gain_terms.shape[2]
    rows = x_a[...].astype(F32)
    scale = lax.rsqrt(jnp.mean(rows * rows, axis=-1, keepdims=True) + EPSILON)
    normed = rows * scale
    d_rows = kept[...] + far[...].astype(F32)
    sums[...] = jnp.sum(d_rows * normed, axis=0, keepdims=True)
    scaled = d_rows * gains[0:1, :]
    value = d_resid[...] + scale * (
        scaled - normed * jnp.mean(scaled * normed, axis=-1, keepdims=True)
    )
    put_rows(blocks, 0, slice(None), value.astype(BF16))
    put_rows(blocks, 1, slice(None), (down_kept[...] + down_far[...].astype(F32)).astype(BF16))
    for slot, rank in enumerate((OWN, NEAR, FAR, ACROSS)):
        gain_terms[slot] = sums[:, aligned(place[rank] * width, width)]


def last(place, kept, far, x_a, gains, d_resid, down_kept, down_far):
    half = kept.shape[0]
    return kernel_call(
        last_kernel,
        "last",
        [(SMEM, place)]
        + in_vmem(kept, far)
        + moved(x_a, gains, d_resid, down_kept)
        + in_vmem(down_far),
        [block_shapes(2 * half, D, True), ((4, 1, D // 4), F32)],
        [pltpu.VMEM((1, D), F32)],
    )


def both_rows(own, near, columns):
    return jnp.concatenate([own[:, columns], near[:, columns]], 0)


def leaving_kernel(
    target, ready, place, left_own, left_near, right_own, right_near, leaving
):
    ready()
    width = leaving.shape[0]
    left = both_rows(left_own, left_near, aligned(place[target] * width, width))

    def step(j, carry):
        columns = aligned(j * 256, 256)
        right = both_rows(right_own, right_near, columns)
        leaving[:, columns] = inner_rows(left, right).astype(BF16)
        return carry

    lax.fori_loop(0, leaving.shape[1] // 256, step, 0)


def leaving_gradient(place, target, left_own, left_near, right_own, right_near):
    width, wide = D // 4, right_own.shape[1]
    return kernel_call(
        functools.partial(leaving_kernel, target),
        "leaving_gradient",
        [(SMEM, place)] + in_stage(left_own, left_near, right_own, right_near),
        [((width, wide), BF16)],
    )[0]


def put_stripe(parts, stripes, block, value):
    if parts == 2:
        at = aligned(block * 128, 128)
        stripes[0, :, at] = value[:, :128]
        stripes[1, :, at] = value[:, 128:]
    else:
        stripes[block // 2, :, aligned((block % 2) * 256, 256)] = value


def write_stripes(who, stripes, grad, sems):
    parts, _, part = stripes.shape
    copies = [
        pltpu.make_async_copy(
            stripes.at[k], grad.at[:, aligned((2 * k + who) * part, part)], sems.at[k]
        )
        for k in range(parts)
    ]
    for copy in copies:
        copy.start()
    for copy in copies:
        copy.wait()


def staying_kernel(
    ready, place, left_own, left_near, right_own, right_near, grad, stripes, sems
):
    ready()
    parts, width, _ = stripes.shape
    left = both_rows(left_own, left_near, aligned(place[OWN] * width, width))

    def step(j, carry):
        right = both_rows(right_own, right_near, aligned(j * 256, 256))
        put_stripe(parts, stripes, j, inner_rows(left, right))
        return carry

    lax.fori_loop(0, right_own.shape[1] // 256, step, 0)
    write_stripes(place[SIDE], stripes, grad, sems)


def staying_gradient(parts, place, left_own, left_near, right_own, right_near):
    width, wide = D // 4, right_own.shape[1]
    return kernel_call(
        staying_kernel,
        "staying_gradient",
        [(SMEM, place)] + in_stage(left_own, left_near, right_own, right_near),
        [((width, 2 * wide), F32)],
        [pltpu.VMEM((parts, width, wide // parts), F32), pltpu.SemaphoreType.DMA((parts,))],
        out_spec=HBM,
    )[0]


def coming_kernel(ready, place, come, before, grad, stripes, sems):
    ready()
    parts = stripes.shape[0]

    def step(j, carry):
        put_stripe(parts, stripes, j, come[:, aligned(j * 256, 256)].astype(F32))
        return carry

    lax.fori_loop(0, come.shape[1] // 256, step, 0)
    write_stripes(1 - place[SIDE], stripes, grad, sems)


def with_coming(parts, place, come, grad):
    width, wide = come.shape
    return kernel_call(
        coming_kernel,
        "coming_gradient",
        [(SMEM, place), (STAGED, come), (HBM, grad)],
        [(grad.shape, F32)],
        [pltpu.VMEM((parts, width, wide // parts), F32), pltpu.SemaphoreType.DMA((parts,))],
        out_spec=HBM,
        aliases=((2, 0),),
    )[0]


def grad_out_kernel(ready, place, mixed_own, mixed_near, d_own, d_near, grad):
    ready()
    left = both_rows(
        mixed_own, mixed_near, aligned(place[CORE] * grad.shape[0], grad.shape[0])
    )
    for base in range(0, D, 512):
        at = slice(base, base + 512)
        grad[:, at] = inner_rows(left, jnp.concatenate([d_own[:, at], d_near[:, at]], 0))


def grad_out_rows(place, mixed_own, mixed_near, d_own, d_near):
    width = mixed_own.shape[1] // 2
    return kernel_call(
        grad_out_kernel,
        "grad_out",
        [(SMEM, place)] + in_stage(mixed_own, mixed_near, d_own, d_near),
        [((width, D), F32)],
    )[0]


def grad_down_kernel(ready, place, h_own, h_near, ca_own, cb_own, ca_near, cb_near, grad, wide):
    ready()
    count, window = grad.shape[0], wide.shape[0]
    core = place[CORE]
    skip = h_own.shape[1] - window
    left = both_rows(h_own, h_near, aligned(core * skip, window))

    def step(n, carry):
        columns = aligned(n * 256, 256)
        right = jnp.concatenate(
            [ref[:, columns] for ref in (ca_own, cb_own, ca_near, cb_near)], 0
        )
        wide[:, columns] = inner_rows(left, right)
        return carry

    lax.fori_loop(0, D // 256, step, 0)
    grad[...] = wide[aligned(core * (count - skip), count, 64), :]


def grad_down_rows(place, h_own, h_near, ca_own, cb_own, ca_near, cb_near):
    count = h_own.shape[1] // 2
    window = -(-count // 128) * 128
    return kernel_call(
        grad_down_kernel,
        "grad_down",
        [(SMEM, place)] + moved(h_own, h_near, ca_own, cb_own, ca_near, cb_near),
        [((count, D), F32)],
        [pltpu.VMEM((window, D), F32)],
    )[0]


def half_columns_kernel(parts, far, ready, place, weight, half, sems):
    part = half.shape[1] // parts
    side = 1 - place[SIDE] if far else place[SIDE]
    copies = [
        pltpu.make_async_copy(
            weight.at[:, aligned((2 * k + side) * part, part)],
            half.at[:, pl.ds(k * part, part)],
            sems.at[k],
        )
        for k in range(parts)
    ]
    for copy in copies:
        copy.start()
    for copy in copies:
        copy.wait()


def half_columns(place, weight, parts, far):
    count, width = weight.shape
    return kernel_call(
        functools.partial(half_columns_kernel, parts, far),
        "far_columns" if far else "kept_columns",
        [(SMEM, place), (HBM, weight)],
        [((count, width // 2), BF16)],
        [pltpu.SemaphoreType.DMA((parts,))],
    )[0]


def spread_kernel(ready, place, weight, kept, leaving, sems):
    part = weight.shape[1] // 4
    side = place[SIDE]
    copies = []
    for k in range(2):
        for j in range(part // 128):
            for who, target in ((side, kept), (1 - side, leaving)):
                copies.append(
                    pltpu.make_async_copy(
                        weight.at[:, aligned((2 * k + who) * part + j * 128, 128)],
                        target.at[:, pl.ds(j * 256 + k * 128, 128)],
                        sems.at[len(copies)],
                    )
                )
    for copy in copies:
        copy.start()
    for copy in copies:
        copy.wait()


def spread(place, weight):
    count, width = weight.shape
    return kernel_call(
        spread_kernel,
        "spread",
        [(SMEM, place), (HBM, weight)],
        [((count, width // 2), BF16)] * 2,
        [pltpu.SemaphoreType.DMA((width // 128,))],
    )


def sync(*values):
    return lax.optimization_barrier(values)


def after(value, *earlier):
    return lax.optimization_barrier((value,) + earlier)[0]


def pair_body(frames_in, segment_ids, gain_attn, w_qkv, w_out, gain_ffn, w_gate_up, w_down, cotangent):
    member = lax.axis_index("fsdp") % 4
    side, core = member >> 1, member & 1
    position = lax.axis_index("fsdp") // 4
    place = jnp.stack([member, member ^ 2, member ^ 1, member ^ 3, side, core, position])
    place = place.astype(jnp.int32)
    frames = frames_in.shape[0] // POS
    half = POS * frames

    near = lambda rows: swap(rows, 1)

    qkv_leaving = half_columns(place, w_qkv, 3, True)
    qkv_across = swap(qkv_leaving, 3)
    qkv_far = near(qkv_across)
    sent = to_positions(place, after(frames_in, qkv_leaving), cotangent)
    came = exchange(sent)
    sent = sent[0]
    ids_own = segment_ids.reshape(frames, POS).T
    ids_own = jnp.take(ids_own, jnp.arange(POS) ^ position, axis=0).reshape(1, half)
    ids_far = swap(after(ids_own, sent), 2)
    gains_own = jnp.stack([gain_attn, gain_ffn])
    gains_far = swap(after(gains_own, sent), 2)
    qkv_kept = half_columns(place, after(w_qkv, sent), 3, False)
    came, ids_far, gains_far, qkv_kept, qkv_far = sync(came, ids_far, gains_far, qkv_kept, qkv_far)

    x_own, c_own = collect(place, came)
    x_far = swap(x_own, 2)
    gains_near = near(jnp.stack([gains_own, gains_far]))
    qkv_near = near(qkv_kept)
    w_kept, w_leaving = spread(place, after(w_gate_up, x_own))
    x_far, gains_near, qkv_near, w_leaving, c_own = sync(
        x_far, gains_near, qkv_near, w_leaving, c_own
    )

    w_across = swap(w_leaving, 3)
    qkv_sent, lowered_first, gains = first(
        place, x_own, x_far, gains_own, gains_far, gains_near[0], gains_near[1],
        w_qkv, qkv_far, qkv_near, qkv_across,
    )
    w_near, out_near, down_near = (near(after(a, lowered_first)) for a in (w_kept, w_out, w_down))
    qkv, w_near, out_near, down_near = sync(exchange(qkv_sent), w_near, out_near, down_near)

    mixed_sent = attend_local(place, ids_own, ids_far, qkv)
    c_far = swap(after(c_own, mixed_sent[0]), 2)
    c_own_near, lowered_first_near = (
        near(after(a, mixed_sent[0])) for a in (c_own, lowered_first)
    )
    mixed, w_across, c_far, c_own_near, lowered_first_near = sync(
        exchange(mixed_sent), w_across, c_far, c_own_near, lowered_first_near
    )

    term, leaving, mixed = out_term(place, mixed, w_out, out_near)
    far = swap(leaving, 2)
    far, mixed_near, w_far, c_far_near = sync(
        far, near(mixed), near(after(w_across, leaving)), near(after(c_far, leaving))
    )
    resid, lowered_second, hidden, d_gate_up, second, leaving = ffn(
        place, x_own, x_far, term, far, gains, c_own, c_far, (w_kept, w_far, w_near, w_across),
        w_down, down_near,
    )

    second_far = swap(leaving, 2)
    hidden_near, lowered_second_near, d_gate_up_near = (
        near(after(rows, leaving)) for rows in (hidden, lowered_second, d_gate_up)
    )
    down_kept, down_leaving = down_term(place, after(hidden, leaving), resid, w_down, down_near)
    sides = (lowered_second, lowered_second_near, d_gate_up, d_gate_up_near)
    gate_up_leaving = leaving_gradient(place, ACROSS, *sides)
    second_far, down_leaving, gate_up_leaving, hidden_near, lowered_second_near = sync(
        second_far, down_leaving, gate_up_leaving, hidden_near, lowered_second_near
    )

    gate_up_come = swap(gate_up_leaving, 3)
    d_resid, d_branch, gain_ffn_terms, d_mixed = mid(
        place, second, second_far, resid, gains, c_own, c_far, w_out, out_near
    )
    d_branch_near, gain_ffn_near = near(d_branch), near(gain_ffn_terms[1])
    grad_gate_up = staying_gradient(2, place, after(lowered_second, d_branch), *sides[1:])
    d_mixed, d_branch_near, gain_ffn_near, grad_gate_up = sync(
        exchange(d_mixed), d_branch_near, gain_ffn_near, grad_gate_up
    )

    d_qkv_sent = attend_back_local(place, ids_own, ids_far, qkv, d_mixed)
    grad_down = grad_down_rows(
        place, after(hidden, d_qkv_sent[0]), hidden_near, c_own, c_far, c_own_near, c_far_near
    )
    grad_out = grad_out_rows(place, mixed, mixed_near, after(d_branch, d_qkv_sent[0]), d_branch_near)
    down_far = swap(after(down_leaving, d_qkv_sent[0]), 2)
    d_qkv, gate_up_come, down_far, grad_down, grad_out = sync(
        exchange(d_qkv_sent), gate_up_come, down_far, grad_down, grad_out
    )

    kept, leaving, d_projected = back_first(
        place, d_qkv, w_qkv, qkv_far, qkv_near, qkv_across
    )
    first_far = swap(leaving, 2)
    qkv_sides = (lowered_first, lowered_first_near, d_projected, near(d_projected))
    first_far, qkv_leaving = sync(first_far, leaving_gradient(place, FAR, *qkv_sides))
    qkv_across_come = swap(qkv_leaving, 3)

    out_sent, gain_attn_terms = last(
        place, kept, first_far, x_own, gains, d_resid, down_kept, down_far
    )
    grad_gate_up = with_coming(2, place, after(gate_up_come, gain_attn_terms), grad_gate_up)
    grad_qkv = staying_gradient(3, place, after(lowered_first, gain_attn_terms), *qkv_sides[1:])
    gain_sums = gain_attn_terms[:2] + swap(gain_attn_terms[2:], 2)
    gain_attn_grad = gain_sums[0] + near(gain_sums[1])
    qkv_come = near(after(qkv_across_come, grad_gate_up, grad_qkv))
    out_come, grad_gate_up, grad_qkv, qkv_come = sync(
        exchange(out_sent), grad_gate_up, grad_qkv, qkv_come
    )
    grad_qkv = with_coming(3, place, qkv_come, grad_qkv)
    grad_in, block_out = to_frames(place, out_come)
    gain_ffn_grad = (gain_ffn_terms[0] + gain_ffn_near).reshape(-1)
    return (
        block_out,
        grad_in,
        gain_attn_grad.reshape(-1),
        grad_qkv,
        grad_out,
        gain_ffn_grad,
        grad_gate_up,
        grad_down,
    )


def solution(mesh):
    in_specs = (
        P("fsdp", None),
        P("fsdp"),
        P("fsdp"),
        P("fsdp", None),
        P("fsdp", None),
        P("fsdp"),
        P("fsdp", None),
        P("fsdp", None),
        P("fsdp", None),
    )
    out_specs = (
        P("fsdp", None),
        P("fsdp", None),
        P("fsdp"),
        P("fsdp", None),
        P("fsdp", None),
        P("fsdp"),
        P("fsdp", None),
        P("fsdp", None),
    )
    chosen = pair_body if mesh.shape["fsdp"] == 4 * POS else body
    return jax.shard_map(chosen, mesh=mesh, in_specs=in_specs, out_specs=out_specs, check_vma=False)
```

```python
import functools
import math

import jax
import jax.numpy as jnp
from jax import lax
from jax.experimental import pallas as pl
from jax.experimental.pallas import tpu as pltpu
from jax.sharding import PartitionSpec as P

D = 1024
FF = 2816
HEADS = 16
HEAD_DIM = 64
POS = 8


EPSILON = 1e-05


def for_sending(array):

    def short(part):
        return part.astype(jnp.bfloat16) if part.dtype == jnp.float32 else part

    return jax.tree.map(short, array)


def swapped(block, axis, stride):
    count = lax.axis_size(axis)
    route = []
    for low in range(count):
        high = low | 1 << stride
        if high != low and high < count:
            route += [(low, high), (high, low)]
    return lax.ppermute(block, axis, route)


def positions_layout(frame_rows, groups):
    width = frame_rows.shape[-1]
    per_piece = frame_rows.shape[0] // POS // groups
    shaped = frame_rows.reshape(groups, per_piece, POS, width).transpose(2, 0, 1, 3)
    return shaped.reshape(POS * groups, per_piece, width)


def frames_layout(piece_rows, groups):
    width = piece_rows.shape[-1]
    per_piece = piece_rows.shape[1]
    shaped = piece_rows.reshape(POS, groups, per_piece, width).transpose(1, 2, 0, 3)
    return shaped.reshape(groups * per_piece * POS, width)


def inner_rows(left, right):
    return lax.dot_general(
        left, right, (((0,), (0,)), ((), ())), preferred_element_type=jnp.float32
    )


def times_transposed(left, right):
    return lax.dot_general(
        left, right, (((1,), (1,)), ((), ())), preferred_element_type=jnp.float32
    )


def join_pieces(current, partner, member, bit_level):
    upper_half = member >> bit_level & 1 == 1
    return tuple(
        (
            jnp.where(
                upper_half,
                jnp.concatenate([theirs, own_piece], 0),
                jnp.concatenate([own_piece, theirs], 0),
            )
            for own_piece, theirs in zip(current, partner)
        )
    )


def collect_forward(pieces, member, levels):
    current = pieces
    for bit_level in range(levels):
        partner = jax.tree.map(
            lambda part, own: part.astype(own.dtype),
            swapped(for_sending(current), "fsdp", bit_level),
            current,
        )
        current = join_pieces(current, partner, member, bit_level)
    return current


def collect_again(pieces, member, levels):
    current = pieces
    for bit_level in range(levels):
        partner = jax.tree.map(
            lambda part, own: part.astype(own.dtype),
            swapped(for_sending(current), "fsdp", bit_level),
            current,
        )
        current = join_pieces(current, partner, member, bit_level)
    return current


def halving_sum(terms, member, levels, sender):
    current = terms
    for bit_level in reversed(range(levels)):
        upper_half = member >> bit_level & 1 == 1
        leaving = tuple(
            (
                jnp.where(
                    upper_half,
                    term_part[: term_part.shape[0] // 2],
                    term_part[term_part.shape[0] // 2 :],
                )
                for term_part in current
            )
        )
        staying = tuple(
            (
                jnp.where(
                    upper_half,
                    term_part[term_part.shape[0] // 2 :],
                    term_part[: term_part.shape[0] // 2],
                )
                for term_part in current
            )
        )
        arrived = sender(leaving, bit_level)
        current = tuple((held_part + come_part for held_part, come_part in zip(staying, arrived)))
    return current


def send_whole(parts, bit_level):
    return jax.tree.map(
        lambda part, own: part.astype(own.dtype),
        swapped(for_sending(parts), "fsdp", bit_level),
        parts,
    )


def permitted(validity):
    row_place = lax.broadcasted_iota(jnp.int32, (POS, POS), 0)
    column_place = lax.broadcasted_iota(jnp.int32, (POS, POS), 1)
    causal = column_place <= row_place
    same_segment = validity[:, :, None] == validity[:, None, :]
    return (causal[None] & same_segment)[:, None]


def split_projections(qkv_frames):
    frames = qkv_frames.shape[0] // POS
    shaped = qkv_frames.reshape(frames, POS, 3, HEADS, HEAD_DIM)
    return (shaped[:, :, 0], shaped[:, :, 1], shaped[:, :, 2])


def masked_scores(queries, key_rows, allowed):
    scores = jnp.einsum(
        "fqhd,fkhd->fhqk", queries, key_rows, preferred_element_type=jnp.float32
    ) * HEAD_DIM ** (-0.5)
    return jnp.where(allowed, scores, -jnp.inf)


def attend(qkv_frames, validity):
    queries, key_rows, value_rows = split_projections(qkv_frames)
    scores = masked_scores(queries, key_rows, permitted(validity))
    highest = jnp.max(scores, axis=-1, keepdims=True)
    raised = jnp.exp(scores - highest)
    totals = jnp.sum(raised, axis=-1, keepdims=True)
    attn_probs = (raised / totals).astype(jnp.bfloat16)
    attended = jnp.einsum(
        "fhqk,fkhd->fqhd", attn_probs, value_rows, preferred_element_type=jnp.float32
    )
    mixed_heads = attended.reshape(qkv_frames.shape[0], D).astype(jnp.bfloat16)
    return (mixed_heads, highest + jnp.log(totals))


def attend_back(qkv_frames, validity, log_total, d_mixed):
    queries, key_rows, value_rows = split_projections(qkv_frames)
    frames = queries.shape[0]
    scores = masked_scores(queries, key_rows, permitted(validity))
    weights_full = jnp.exp(scores - log_total)
    attn_probs = weights_full.astype(jnp.bfloat16)
    d_heads = d_mixed.reshape(frames, POS, HEADS, HEAD_DIM)
    d_probs = jnp.einsum("fqhd,fkhd->fhqk", d_heads, value_rows, preferred_element_type=jnp.float32)
    d_values = jnp.einsum(
        "fhqk,fqhd->fkhd", attn_probs, d_heads, preferred_element_type=jnp.float32
    )
    d_scores = weights_full * (d_probs - jnp.sum(d_probs * weights_full, axis=-1, keepdims=True))
    d_scores = d_scores.astype(jnp.bfloat16)
    d_queries = jnp.einsum(
        "fhqk,fkhd->fqhd", d_scores, key_rows, preferred_element_type=jnp.float32
    ) * HEAD_DIM ** (-0.5)
    d_keys = jnp.einsum(
        "fhqk,fqhd->fkhd", d_scores, queries, preferred_element_type=jnp.float32
    ) * HEAD_DIM ** (-0.5)
    stacked = jnp.stack([d_queries, d_keys, d_values], axis=2)
    return stacked.reshape(frames * POS, 3 * D).astype(jnp.bfloat16)


def body(frames_in, segment_ids, gain_attn, w_qkv, w_out, gain_ffn, w_gate_up, w_down, cotangent):
    devices = lax.axis_size("fsdp")
    groups = devices // POS
    levels = groups.bit_length() - 1
    member = lax.axis_index("fsdp") % groups
    per_piece = frames_in.shape[0] // POS // groups
    validity = segment_ids.reshape(-1, POS)
    moved_input, moved_cotangent = (
        lax.all_to_all(
            positions_layout(frames_in, groups), "fsdp", split_axis=0, concat_axis=0, tiled=True
        ),
        lax.all_to_all(
            positions_layout(cotangent, groups), "fsdp", split_axis=0, concat_axis=0, tiled=True
        ),
    )
    inputs = moved_input.reshape(-1, D).astype(jnp.float32)
    upstream = moved_cotangent.reshape(-1, D)
    own_pieces = (w_qkv, w_out, w_gate_up, w_down, gain_attn, gain_ffn)
    collected = collect_forward(own_pieces, member, levels)
    whole_qkv, whole_out, whole_gate_up, whole_down, whole_gain_attn, whole_gain_ffn = collected
    gain_first = whole_gain_attn.astype(jnp.float32)
    gain_second = whole_gain_ffn.astype(jnp.float32)
    scale_first = lax.rsqrt(jnp.mean(inputs * inputs, axis=-1, keepdims=True) + EPSILON)
    normed_first = inputs * scale_first
    lowered_first = (normed_first * gain_first).astype(jnp.bfloat16)
    projected = jnp.dot(lowered_first, whole_qkv, preferred_element_type=jnp.float32).astype(
        jnp.bfloat16
    )
    qkv_frames = frames_layout(
        lax.all_to_all(
            projected.reshape(devices, per_piece, 3 * D),
            "fsdp",
            split_axis=0,
            concat_axis=0,
            tiled=True,
        ),
        groups,
    )
    mixed_frames, log_total = attend(qkv_frames, validity)
    mixed_rows = lax.all_to_all(
        positions_layout(mixed_frames, groups), "fsdp", split_axis=0, concat_axis=0, tiled=True
    ).reshape(-1, D)
    residual = inputs + jnp.dot(mixed_rows, whole_out, preferred_element_type=jnp.float32)
    scale_second = lax.rsqrt(jnp.mean(residual * residual, axis=-1, keepdims=True) + EPSILON)
    normed_second = residual * scale_second
    lowered_second = (normed_second * gain_second).astype(jnp.bfloat16)
    gate_up = jnp.dot(lowered_second, whole_gate_up, preferred_element_type=jnp.float32)
    gate_part = gate_up[:, :FF]
    up_part = gate_up[:, FF:]
    sigmoid_gate = jax.nn.sigmoid(gate_part)
    activated = gate_part * sigmoid_gate
    hidden = (activated * up_part).astype(jnp.bfloat16)
    result_rows = (
        residual + jnp.dot(hidden, whole_down, preferred_element_type=jnp.float32)
    ).astype(jnp.bfloat16)
    block_out = frames_layout(
        lax.all_to_all(
            result_rows.reshape(devices, per_piece, D),
            "fsdp",
            split_axis=0,
            concat_axis=0,
            tiled=True,
        ),
        groups,
    )
    collected = collect_again(own_pieces, member, levels)
    whole_qkv, whole_out, whole_gate_up, whole_down, whole_gain_attn, whole_gain_ffn = collected
    gain_first = whole_gain_attn.astype(jnp.float32)
    gain_second = whole_gain_ffn.astype(jnp.float32)
    grad_down_term = inner_rows(hidden, upstream)
    d_hidden = times_transposed(upstream, whole_down)
    d_gate = d_hidden * up_part * sigmoid_gate * (1.0 + gate_part * (1.0 - sigmoid_gate))
    d_up = d_hidden * activated
    d_gate_up = jnp.concatenate([d_gate, d_up], axis=1).astype(jnp.bfloat16)
    grad_gate_up_term = inner_rows(lowered_second, d_gate_up)
    d_second = times_transposed(d_gate_up, whole_gate_up)
    grad_gain_ffn_term = jnp.sum(d_second * normed_second, axis=0)
    scaled_second = d_second * gain_second
    d_residual = upstream.astype(jnp.float32) + scale_second * (
        scaled_second
        - normed_second * jnp.mean(scaled_second * normed_second, axis=-1, keepdims=True)
    )
    d_branch = d_residual.astype(jnp.bfloat16)
    grad_out_term = inner_rows(mixed_rows, d_branch)
    d_mixed = times_transposed(d_branch, whole_out).astype(jnp.bfloat16)
    d_mixed_frames = frames_layout(
        lax.all_to_all(
            d_mixed.reshape(devices, per_piece, D), "fsdp", split_axis=0, concat_axis=0, tiled=True
        ),
        groups,
    )
    d_qkv_frames = attend_back(qkv_frames, validity, log_total, d_mixed_frames)
    d_projected = lax.all_to_all(
        positions_layout(d_qkv_frames, groups), "fsdp", split_axis=0, concat_axis=0, tiled=True
    ).reshape(-1, 3 * D)
    grad_qkv_term = inner_rows(lowered_first, d_projected)
    d_first = times_transposed(d_projected, whole_qkv)
    grad_gain_attn_term = jnp.sum(d_first * normed_first, axis=0)
    scaled_first = d_first * gain_first
    d_inputs = d_residual + scale_first * (
        scaled_first - normed_first * jnp.mean(scaled_first * normed_first, axis=-1, keepdims=True)
    )
    grad_in = frames_layout(
        lax.all_to_all(
            d_inputs.reshape(devices, per_piece, D).astype(jnp.bfloat16),
            "fsdp",
            split_axis=0,
            concat_axis=0,
            tiled=True,
        ).astype(jnp.float32),
        groups,
    )
    shares = halving_sum(
        (
            grad_qkv_term,
            grad_out_term,
            grad_gate_up_term,
            grad_down_term,
            grad_gain_attn_term,
            grad_gain_ffn_term,
        ),
        member,
        levels,
        send_whole,
    )
    return (block_out, grad_in, shares[4], shares[0], shares[1], shares[5], shares[2], shares[3])

VMEM = pl.BlockSpec(memory_space=pltpu.VMEM)
SMEM = pl.BlockSpec(memory_space=pltpu.SMEM)
HBM = pl.BlockSpec(memory_space=pltpu.HBM)
STAGED = pl.BlockSpec(memory_space=pltpu.HBM)
MOVED = pl.BlockSpec(memory_space=pl.ANY)
EITHER = pl.BlockSpec(memory_space=pl.ANY)
BF16 = jnp.bfloat16
F32 = jnp.float32
OWN, FAR, NEAR, ACROSS, SIDE, CORE, POSITION = range(7)
TAIL = 16


def swap(block, mask):
    count = lax.axis_size("fsdp")
    return lax.ppermute(block, "fsdp", [(i, i ^ mask) for i in range(count)])


def exchange(blocks):
    count = lax.axis_size("fsdp")
    stride = count // POS
    if len(blocks) == POS:
        return [blocks[0]] + [swap(blocks[k], stride * k) for k in range(1, POS)]
    lanes = [[r + stride * k for k in range(POS)] for r in range(stride)]
    return [
        lax.all_to_all(
            blocks[0], "fsdp", split_axis=0, concat_axis=0, tiled=True, axis_index_groups=lanes
        )
    ]


def kernel_call(kernel, name, args, outs, scratch=(), aliases=()):
    flat = lambda items: [p for item in items for p in (item if isinstance(item, list) else [item])]
    staged = [n for n, (spec, _) in enumerate(flat(args)) if spec is STAGED or spec is MOVED]
    arrays = [
        pltpu.with_memory_space_constraint(a, pltpu.HBM) if spec is STAGED or spec is HBM else a
        for spec, a in flat(args)
    ]
    scratch = list(scratch)
    own = len(scratch)
    scratch += [pltpu.VMEM(arrays[n].shape, arrays[n].dtype) for n in staged]
    scratch += [pltpu.SemaphoreType.DMA((max(len(staged), 1),))]
    held = sum(
        math.prod(ref.shape) * jnp.dtype(ref.dtype).itemsize
        for ref in scratch
        if ref.memory_space == pltpu.VMEM
    )

    def grouped(items, values):
        return [
            [next(values) for _ in item] if isinstance(item, list) else next(values)
            for item in items
        ]

    def body_kernel(*refs):
        inputs, outputs = list(refs[: len(arrays)]), refs[len(arrays) :]
        outputs, extra = outputs[: len(flat(outs))], outputs[len(flat(outs)) :]
        extra, landing, sems = extra[:own], extra[own:-1], extra[-1]
        copies = []
        for k, n in enumerate(staged):
            copies.append(pltpu.make_async_copy(inputs[n], landing[k], sems.at[k]))
            inputs[n] = landing[k]
        for copy in copies:
            copy.start()

        def ready():
            for copy in copies:
                copy.wait()

        kernel(ready, *grouped(args, iter(inputs)), *grouped(outs, iter(outputs)), *extra)

    result = pl.pallas_call(
        body_kernel,
        name=name,
        in_specs=[spec for spec, _ in flat(args)],
        out_specs=[spec[0] if spec else VMEM for _, _, *spec in flat(outs)],
        out_shape=[
            pltpu.HBM(s, d) if spec else jax.ShapeDtypeStruct(s, d) for s, d, *spec in flat(outs)
        ],
        input_output_aliases=dict(aliases),
        scratch_shapes=scratch,
        cost_estimate=pl.CostEstimate(flops=1, bytes_accessed=1, transcendentals=0),
        compiler_params=pltpu.CompilerParams(vmem_limit_bytes=held + (8 << 20)),
    )(*arrays)
    return grouped(outs, iter(result))


def views(blocks, place):
    if len(blocks) == POS:
        return blocks
    return [blocks[0].at[place[POSITION] ^ k] for k in range(POS)]


def matmul(left, right):
    return jnp.dot(left, right, preferred_element_type=F32)


def aligned(start, size, step=128):
    return pl.ds(pl.multiple_of(start, step), size)


def rows_of(refs, rel, columns=slice(None)):
    frames = refs[0].shape[0] // 2
    return jnp.concatenate([ref[rel * frames : (rel + 1) * frames, columns] for ref in refs], 0)


def put_rows(refs, rel, columns, value):
    frames = refs[0].shape[0] // 2
    for k, ref in enumerate(refs):
        ref[rel * frames : (rel + 1) * frames, columns] = value[k * frames : (k + 1) * frames]


def block_shapes(rows, width, joined):
    if joined:
        return [((POS, rows // POS, width), BF16)]
    return [((rows // POS, width), BF16)] * POS


def in_vmem(*arrays):
    return [(VMEM, a) for a in arrays]


def in_stage(*arrays):
    return [(STAGED, a) for a in arrays]


def moved(*arrays):
    return [(MOVED, a) for a in arrays]


def place_matrix(size, to_positions, position):
    frames = size // POS
    row = lax.broadcasted_iota(jnp.int32, (size, size), 0)
    column = lax.broadcasted_iota(jnp.int32, (size, size), 1)
    if not to_positions:
        row, column = column, row
    return (column == (row % frames) * POS + ((row // frames) ^ position)).astype(F32).astype(BF16)


def to_positions_kernel(ready, place, x_rows, c_rows, weight, x_blocks, c_blocks, half, sems):
    copies = side_columns(weight, half, 1 - place[SIDE], sems)
    for copy in copies:
        copy.start()
    order = place_matrix(x_rows.shape[0], True, place[POSITION])
    ready()
    for rows, blocks in ((x_rows, x_blocks), (c_rows, c_blocks)):
        moved_rows = matmul(order, rows[...]).astype(BF16)
        count = rows.shape[0] // POS
        for k, block in enumerate(views(blocks, place)):
            block[...] = moved_rows[k * count : (k + 1) * count]
    for copy in copies:
        copy.wait()


def to_positions(place, x_rows, c_rows, weight):
    size, width = x_rows.shape
    return kernel_call(
        to_positions_kernel,
        "to_positions",
        [(SMEM, place)] + in_stage(x_rows, c_rows) + [(HBM, weight)],
        [block_shapes(size, width, True), block_shapes(size, width, True),
         ((weight.shape[0], weight.shape[1] // 2), BF16)],
        [pltpu.SemaphoreType.DMA((3,))],
    )


def joined(blocks, place):
    return jnp.concatenate([block[...] for block in views(blocks, place)], 0)


def collect_rows_kernel(ready, place, blocks, rows):
    ready()
    rows[...] = joined(blocks, place)


def collect_rows(place, blocks):
    count, width = blocks[0].shape[-2:]
    return kernel_call(
        collect_rows_kernel,
        "collect_rows",
        [(SMEM, place), in_vmem(*blocks)],
        [((count * POS, width), BF16)],
    )[0]


def collect_kernel(ready, place, blocks, ids, gains_own, gains_near, x_own):
    ready()
    half = x_own.shape[0] - TAIL
    x_own[:half, :] = joined(blocks, place)
    padded = lambda *parts: jnp.concatenate(
        parts + (jnp.zeros((1, D - sum(p.shape[1] for p in parts)), F32),), 1
    )
    row = lax.broadcasted_iota(jnp.int32, (TAIL, D), 0)
    tail = jnp.where(row == 2, padded(ids[...].astype(F32)), 0.0)
    for k in range(2):
        gain = padded(gains_own[k : k + 1, :].astype(F32), gains_near[k : k + 1, :].astype(F32))
        tail = jnp.where(row == k, gain, tail)
    x_own[half:, :] = tail.astype(BF16)


def collect(place, blocks, ids, gains_own, gains_near):
    count, width = blocks[0].shape[-2:]
    return kernel_call(
        collect_kernel,
        "collect",
        [(SMEM, place), in_vmem(*blocks)] + in_vmem(ids, gains_own, gains_near),
        [((count * POS + TAIL, width), BF16)],
    )[0]


def to_frames_kernel(ready, place, blocks, *rows):
    ready()
    blocks = views(blocks, place)
    order = place_matrix(rows[0].shape[0], False, place[POSITION])
    for rel in range(2):
        rows[rel][...] = matmul(order, rows_of(blocks, rel)).astype(rows[rel].dtype)


def to_frames(place, blocks):
    size = blocks[0].shape[-2] * POS // 2
    return kernel_call(
        to_frames_kernel,
        "to_frames",
        [(SMEM, place), in_vmem(*blocks)],
        [((size, D), F32), ((size, D), BF16)],
    )


def first_kernel(
    ready, place, x_a, x_b, w_own, w_far, w_near, w_across, qkv, lowered_out, table_out,
    lowered, table, w, sems,
):
    qkv = views(qkv, place)
    half, width = lowered.shape[0] // 2, w_own.shape[0]
    part = w.shape[1] // 3
    side = place[SIDE]
    at_rows = lambda rank: aligned(place[rank] * width, width)
    copies = [
        pltpu.make_async_copy(
            w_own.at[:, aligned((2 * k + side) * part, part)],
            w.at[at_rows(OWN), pl.ds(k * part, part)],
            sems.at[k],
        )
        for k in range(3)
    ]
    copies.append(pltpu.make_async_copy(w_far, w.at[at_rows(FAR)], sems.at[3]))
    copies.append(pltpu.make_async_copy(w_near, w.at[at_rows(NEAR)], sems.at[4]))
    copies.append(pltpu.make_async_copy(w_across, w.at[at_rows(ACROSS)], sems.at[5]))
    for copy in copies:
        copy.start()
    ready()
    table[...] = jnp.zeros_like(table)
    for k, (ref, ranks) in enumerate(((x_a, (OWN, NEAR)), (x_b, (FAR, ACROSS)))):
        tail = ref[half:, :].astype(F32)
        for n, rank in enumerate(ranks):
            table[0:2, at_rows(rank)] = tail[0:2, n * width : (n + 1) * width]
        table[2 + k : 3 + k, 0:half] = tail[2:3, 0:half]
    gain = table[0:1, :]
    for rel, ref in enumerate((x_a, x_b)):
        rows = ref[:half, :].astype(F32)
        scale = lax.rsqrt(jnp.mean(rows * rows, axis=-1, keepdims=True) + EPSILON)
        lowered[rel * half : (rel + 1) * half, :] = (rows * scale * gain).astype(BF16)
    leaving = [
        pltpu.make_async_copy(lowered, lowered_out, sems.at[6]),
        pltpu.make_async_copy(table, table_out, sems.at[7]),
    ]
    for copy in leaving:
        copy.start()
    for copy in copies:
        copy.wait()

    def step(n, carry):
        columns = aligned(n * 256, 256, 256)
        value = matmul(lowered[...], w[:, columns]).astype(BF16)
        put_rows(qkv, 0, columns, value[:half])
        put_rows(qkv, 1, columns, value[half:])
        return carry

    lax.fori_loop(0, w.shape[1] // 256, step, 0)
    for copy in leaving:
        copy.wait()


def first(place, x_a, x_b, w_own, w_far, w_near, w_across):
    half = x_a.shape[0] - TAIL
    wide = w_far.shape[1]
    return kernel_call(
        first_kernel,
        "first",
        [(SMEM, place), (MOVED, x_a), (MOVED, x_b), (HBM, w_own), (EITHER, w_far),
         (EITHER, w_near), (EITHER, w_across)],
        [block_shapes(2 * half, wide, True), ((2 * half, D), BF16, HBM), ((8, D), F32, HBM)],
        [pltpu.VMEM((2 * half, D), BF16), pltpu.VMEM((8, D), F32), pltpu.VMEM((D, wide), BF16),
         pltpu.SemaphoreType.DMA((8,))],
    )


def allowed_pairs(ids, position):
    size = ids.shape[1]
    frames = size // POS
    row = lax.broadcasted_iota(jnp.int32, (size, size), 0)
    column = lax.broadcasted_iota(jnp.int32, (size, size), 1)
    across = jnp.broadcast_to(ids, (size, size))
    same = (across == across.T) & (row % frames == column % frames)
    mask = same & ((column // frames) ^ position <= (row // frames) ^ position)
    return jnp.concatenate([mask, mask], 1)


def pair_of_heads(rows, low):
    return jnp.concatenate([rows * low, rows * (1 - low)], 0)


def lane_halves(value, reduce):
    size = value.shape[1] // 2
    parts = [
        jnp.broadcast_to(reduce(value[:, k * size : (k + 1) * size]), (value.shape[0], size))
        for k in range(2)
    ]
    return jnp.concatenate(parts, 1)


def pair_probs(query, key_pair, mask):
    scores = times_transposed(query, key_pair) * HEAD_DIM ** (-0.5)
    scores = jnp.where(mask, scores, -jnp.inf)
    raised = jnp.exp(scores - lane_halves(scores, lambda a: jnp.max(a, -1, keepdims=True)))
    return raised / lane_halves(raised, lambda a: jnp.sum(a, -1, keepdims=True))


def first_head_lanes():
    lane = lax.broadcasted_iota(jnp.int32, (1, 2 * HEAD_DIM), 1)
    return (lane < HEAD_DIM).astype(F32).astype(BF16)


def attend_kernel(ready, place, table, qkv, mixed):
    qkv, mixed = views(qkv, place), views(mixed, place)
    size = POS * mixed[0].shape[0] // 2
    part = mixed[0].shape[1]
    low = first_head_lanes()
    ready()
    for rel in range(2):
        mask = allowed_pairs(table[2 + rel : 3 + rel, 0:size], place[POSITION])
        for base in range(0, part, 2 * HEAD_DIM):
            query, key_rows, value_rows = (
                rows_of(qkv, rel, slice(k * part + base, k * part + base + 2 * HEAD_DIM))
                for k in range(3)
            )
            probs = pair_probs(query, pair_of_heads(key_rows, low), mask)
            value = matmul(probs.astype(BF16), pair_of_heads(value_rows, low))
            put_rows(mixed, rel, slice(base, base + 2 * HEAD_DIM), value.astype(BF16))


def attend_local(place, table, qkv):
    rows, wide = qkv[0].shape[-2:]
    return kernel_call(
        attend_kernel,
        "attend",
        [(SMEM, place), (MOVED, table), moved(*qkv)],
        [block_shapes(rows * POS, wide // 3, True)],
    )[0]


def attend_back_kernel(ready, place, table, qkv, d_mixed, d_qkv):
    qkv, d_mixed, d_qkv = (views(blocks, place) for blocks in (qkv, d_mixed, d_qkv))
    part = d_mixed[0].shape[1]
    pair = 2 * HEAD_DIM
    low = first_head_lanes()
    size = POS * d_mixed[0].shape[0] // 2
    low_full = lax.broadcasted_iota(jnp.int32, (size, pair), 1) < HEAD_DIM
    scale = HEAD_DIM ** (-0.5)
    ready()
    for rel in range(2):
        mask = allowed_pairs(table[2 + rel : 3 + rel, 0:size], place[POSITION])
        for base in range(0, part, pair):
            query, key_rows, value_rows = (
                rows_of(qkv, rel, slice(k * part + base, k * part + base + pair))
                for k in range(3)
            )
            d_rows = rows_of(d_mixed, rel, slice(base, base + pair))
            keys = pair_of_heads(key_rows, low)
            probs = pair_probs(query, keys, mask)
            d_probs = times_transposed(d_rows, pair_of_heads(value_rows, low))
            inner = lane_halves(d_probs * probs, lambda a: jnp.sum(a, -1, keepdims=True))
            d_scores = (probs * (d_probs - inner)).astype(BF16)
            d_query = matmul(d_scores, keys) * scale
            d_key = inner_rows(d_scores, query) * scale
            d_value = inner_rows(probs.astype(BF16), d_rows)
            d_key = jnp.where(low_full, d_key[:size], d_key[size:])
            d_value = jnp.where(low_full, d_value[:size], d_value[size:])
            for k, value in enumerate((d_query, d_key, d_value)):
                columns = slice(k * part + base, k * part + base + pair)
                put_rows(d_qkv, rel, columns, value.astype(BF16))


def attend_back_local(place, table, qkv, d_mixed):
    rows, wide = qkv[0].shape[-2:]
    return kernel_call(
        attend_back_kernel,
        "attend_back",
        [(SMEM, place), (MOVED, table), moved(*qkv), in_vmem(*d_mixed)],
        [block_shapes(rows * POS, wide, True)],
    )[0]


def chip_rows(place, own, near, whole, sems):
    count = own.shape[0]
    core = place[CORE]
    return [
        pltpu.make_async_copy(own, whole.at[aligned(core * count, count, 64)], sems.at[0]),
        pltpu.make_async_copy(near, whole.at[aligned((1 - core) * count, count, 64)], sems.at[1]),
    ]


def out_kernel(ready, place, w_own, w_near, mixed, term, leaving, mixed_rows, w, sems):
    mixed = views(mixed, place)
    copies = chip_rows(place, w_own, w_near, w, sems)
    for copy in copies:
        copy.start()
    ready()
    rows = jnp.concatenate([rows_of(mixed, 0), rows_of(mixed, 1)], 0)
    mixed_rows[...] = rows
    half = rows.shape[0] // 2
    for copy in copies:
        copy.wait()
    for base in range(0, D, 512):
        value = matmul(rows, w[:, base : base + 512])
        term[:, base : base + 512] = value
        lowered = value.astype(BF16)
        leaving[:half, base : base + 512] = lowered[half:]
        leaving[half:, base : base + 512] = lowered[:half]


def out_term(place, mixed, w_own, w_near):
    rows = POS * mixed[0].shape[-2]
    inner = 2 * w_own.shape[0]
    return kernel_call(
        out_kernel,
        "out_term",
        [(SMEM, place), (HBM, w_own), (HBM, w_near), in_vmem(*mixed)],
        [((rows, D), F32), ((rows, D), BF16), ((rows, inner), BF16)],
        [pltpu.VMEM((inner, D), BF16), pltpu.SemaphoreType.DMA((2,))],
    )


def d_hidden_kernel(ready, place, c_a, c_b, w_own, w_near, d_hidden, w, sems):
    copies = chip_rows(place, w_own, w_near, w, sems)
    for copy in copies:
        copy.start()
    ready()
    upstream = jnp.concatenate([c_a[...], c_b[...]], 0)
    for copy in copies:
        copy.wait()
    inner = w.shape[0]
    for base in range(0, inner, 256):
        end = min(base + 256, inner)
        d_hidden[:, base:end] = times_transposed(upstream, w[base:end, :])


def d_hidden_rows(place, c_a, c_b, w_own, w_near):
    rows, inner = 2 * c_a.shape[0], 2 * w_own.shape[0]
    return kernel_call(
        d_hidden_kernel,
        "d_hidden",
        [(SMEM, place), (MOVED, c_a), (MOVED, c_b), (HBM, w_own), (HBM, w_near)],
        [((rows, inner), F32)],
        [pltpu.VMEM((inner, D), BF16), pltpu.SemaphoreType.DMA((2,))],
    )[0]


def ffn_kernel(
    ready, place, x_a, x_b, term, far, table, d_hidden_all, *rest
):
    pieces = rest[:4]
    resid, lowered, hidden, d_gate_up, second, leaving = rest[4:10]
    w, sems = rest[10:]
    half, width, steps = term.shape[0] // 2, pieces[0].shape[0], w.shape[0]

    def begin(j, carry):
        for rank, source in enumerate(pieces):
            pltpu.make_async_copy(
                source.at[:, aligned(j * 256, 256)],
                w.at[j, aligned(place[rank] * width, width)],
                sems.at[j, rank],
            ).start()
        return carry

    lax.fori_loop(0, steps, begin, 0)
    ready()
    gain = table[1:2, :]
    for rel, x_ref in enumerate((x_a, x_b)):
        at = pl.ds(rel * half, half)
        rows = x_ref[:half, :].astype(F32) + (term[at, :] + far[at, :].astype(F32))
        resid[at, :] = rows
        scale = lax.rsqrt(jnp.mean(rows * rows, axis=-1, keepdims=True) + EPSILON)
        lowered[at, :] = (rows * scale * gain).astype(BF16)

    def step(j, carry):
        for rank in range(4):
            rows = w.at[j, pl.ds(rank * width, width)]
            pltpu.make_async_copy(rows, rows, sems.at[j, rank]).wait()
        gate_up = matmul(lowered[...], w[j])
        gate, up = gate_up[:, :128], gate_up[:, 128:]
        d_hidden = d_hidden_all[:, aligned(j * 128, 128)]
        sigmoid = jax.nn.sigmoid(gate)
        activated = gate * sigmoid
        hidden[:, aligned(j * 128, 128)] = (activated * up).astype(BF16)
        d_gate = d_hidden * up * sigmoid * (1.0 + gate * (1.0 - sigmoid))
        d_gate_up[:, aligned(j * 256, 128)] = d_gate.astype(BF16)
        d_gate_up[:, aligned(j * 256 + 128, 128)] = (d_hidden * activated).astype(BF16)
        return carry

    lax.fori_loop(0, steps, step, 0)

    def back(n, carry):
        columns = aligned(n * 256, 256)
        value = times_transposed(d_gate_up[:, 0:256], w[0, columns, :])
        for j in range(1, steps):
            value += times_transposed(d_gate_up[:, j * 256 : (j + 1) * 256], w[j, columns, :])
        second[:, columns] = value
        lower = value.astype(BF16)
        leaving[:half, columns] = lower[half:]
        leaving[half:, columns] = lower[:half]
        return carry

    lax.fori_loop(0, D // 256, back, 0)


def ffn(place, x_a, x_b, term, far, table, d_hidden, pieces):
    rows, inner = d_hidden.shape
    wide, steps = 2 * inner, inner // 128
    return kernel_call(
        ffn_kernel,
        "ffn",
        [(SMEM, place)]
        + in_stage(x_a, x_b) + in_vmem(term, far) + in_stage(table) + in_vmem(d_hidden)
        + [(EITHER if rank in (FAR, NEAR) else HBM, a) for rank, a in enumerate(pieces)],
        [((rows, D), F32), ((rows, D), BF16), ((rows, inner), BF16), ((rows, wide), BF16),
         ((rows, D), F32), ((rows, D), BF16)],
        [pltpu.VMEM((steps, D, 256), BF16), pltpu.SemaphoreType.DMA((steps, 4))],
    )


def down_kernel(ready, place, hidden, resid, w_own, w_near, kept, leaving, w, sems):
    copies = chip_rows(place, w_own, w_near, w, sems)
    for copy in copies:
        copy.start()
    half = kept.shape[0]
    ready()
    for copy in copies:
        copy.wait()

    def step(n, carry):
        columns = aligned(n * 256, 256)
        value = matmul(hidden[...], w[:, columns])
        kept[:, columns] = resid[:half, columns] + value[:half]
        leaving[:, columns] = value[half:].astype(BF16)
        return carry

    lax.fori_loop(0, D // 256, step, 0)


def down_term(place, hidden, resid, w_own, w_near):
    rows, inner = hidden.shape
    return kernel_call(
        down_kernel,
        "down_term",
        [(SMEM, place), (STAGED, hidden), (VMEM, resid), (HBM, w_own), (HBM, w_near)],
        [((rows // 2, D), F32), ((rows // 2, D), BF16)],
        [pltpu.VMEM((inner, D), BF16), pltpu.SemaphoreType.DMA((2,))],
    )


def mid_kernel(
    ready, place, second, far, resid, gains, c_a, c_b, w_own, w_near,
    d_resid_out, d_branch, gain_terms, d_mixed, d_resid, w, sums, sems,
):
    d_mixed = views(d_mixed, place)
    copies = chip_rows(place, w_own, w_near, w, sems)
    for copy in copies:
        copy.start()
    half, width = c_a.shape[0], w_own.shape[0]
    total = None
    for rel in range(2):
        at = pl.ds(rel * half, half)
        rows = resid[at, :]
        scale = lax.rsqrt(jnp.mean(rows * rows, axis=-1, keepdims=True) + EPSILON)
        d_rows = second[at, :] + far[at, :].astype(F32)
        part = jnp.sum(d_rows * (rows * scale), axis=0, keepdims=True)
        total = part if total is None else total + part
    ready()
    gain = gains[1:2, :]
    for rel, c_ref in enumerate((c_a, c_b)):
        at = pl.ds(rel * half, half)
        rows = resid[at, :]
        scale = lax.rsqrt(jnp.mean(rows * rows, axis=-1, keepdims=True) + EPSILON)
        normed = rows * scale
        scaled = (second[at, :] + far[at, :].astype(F32)) * gain
        value = c_ref[...].astype(F32) + scale * (
            scaled - normed * jnp.mean(scaled * normed, axis=-1, keepdims=True)
        )
        if rel == 0:
            d_resid[...] = value
            leaving = pltpu.make_async_copy(d_resid, d_resid_out, sems.at[2])
            leaving.start()
        d_branch[at, :] = value.astype(BF16)
    sums[...] = total
    gain_terms[0] = sums[:, aligned(place[OWN] * width, width)]
    gain_terms[1] = sums[:, aligned(place[NEAR] * width, width)]
    for copy in copies:
        copy.wait()
    for base in range(0, w.shape[0], 256):
        value = times_transposed(d_branch[...], w[base : base + 256, :]).astype(BF16)
        put_rows(d_mixed, 0, slice(base, base + 256), value[:half])
        put_rows(d_mixed, 1, slice(base, base + 256), value[half:])
    leaving.wait()


def mid(place, second, far, resid, gains, c_a, c_b, w_own, w_near):
    rows = second.shape[0]
    width = w_own.shape[0]
    return kernel_call(
        mid_kernel,
        "mid",
        [(SMEM, place), (VMEM, second), (VMEM, far), (VMEM, resid), (MOVED, gains),
         (MOVED, c_a), (MOVED, c_b), (HBM, w_own), (HBM, w_near)],
        [((rows // 2, D), F32, HBM), ((rows, D), BF16), ((2, 1, width), F32),
         block_shapes(rows, 2 * width, True)],
        [pltpu.VMEM((rows // 2, D), F32), pltpu.VMEM((2 * width, D), BF16),
         pltpu.VMEM((1, D), F32), pltpu.SemaphoreType.DMA((3,))],
    )


def back_first_kernel(
    ready, place, w_own, w_far, w_near, w_across, d_qkv, kept, leaving, rows, w, sems
):
    d_qkv = views(d_qkv, place)
    half, width = kept.shape[0], w_own.shape[0]
    part = w.shape[2] // 3
    side = place[SIDE]
    copies = [
        pltpu.make_async_copy(
            w_own.at[:, aligned((2 * k + side) * part, part)],
            w.at[0, :, pl.ds(k * part, part)],
            sems.at[k],
        )
        for k in range(3)
    ]
    copies.append(pltpu.make_async_copy(w_far, w.at[1], sems.at[3]))
    copies.append(pltpu.make_async_copy(w_near, w.at[2], sems.at[4]))
    copies.append(pltpu.make_async_copy(w_across, w.at[3], sems.at[5]))
    for copy in copies:
        copy.start()
    ready()
    rows[:half, :] = rows_of(d_qkv, 0)
    rows[half:, :] = rows_of(d_qkv, 1)
    for rank in range(4):
        for copy in copies[:3] if rank == 0 else copies[rank + 2 : rank + 3]:
            copy.wait()
        columns = aligned(place[rank] * width, width)
        value = times_transposed(rows[...], w[rank])
        kept[:, columns] = value[:half]
        leaving[:, columns] = value[half:].astype(BF16)


def back_first(place, d_qkv, w_own, w_far, w_near, w_across):
    rows, wide = POS * d_qkv[0].shape[-2], d_qkv[0].shape[-1]
    return kernel_call(
        back_first_kernel,
        "back_first",
        [(SMEM, place), (HBM, w_own), (HBM, w_far), (HBM, w_near), (HBM, w_across),
         in_vmem(*d_qkv)],
        [((rows // 2, D), F32), ((rows // 2, D), BF16), ((rows, wide), BF16)],
        [pltpu.VMEM((4, w_own.shape[0], wide), BF16), pltpu.SemaphoreType.DMA((6,))],
    )


def last_kernel(
    ready, place, kept, far, x_a, gains, d_resid, down_kept, down_far, blocks, gain_terms, sums
):
    ready()
    blocks = views(blocks, place)
    width = gain_terms.shape[2]
    rows = x_a[: kept.shape[0], :].astype(F32)
    scale = lax.rsqrt(jnp.mean(rows * rows, axis=-1, keepdims=True) + EPSILON)
    normed = rows * scale
    d_rows = kept[...] + far[...].astype(F32)
    sums[...] = jnp.sum(d_rows * normed, axis=0, keepdims=True)
    scaled = d_rows * gains[0:1, :]
    value = d_resid[...] + scale * (
        scaled - normed * jnp.mean(scaled * normed, axis=-1, keepdims=True)
    )
    put_rows(blocks, 0, slice(None), value.astype(BF16))
    put_rows(blocks, 1, slice(None), (down_kept[...] + down_far[...].astype(F32)).astype(BF16))
    for slot, rank in enumerate((OWN, NEAR, FAR, ACROSS)):
        gain_terms[slot] = sums[:, aligned(place[rank] * width, width)]


def last(place, kept, far, x_a, gains, d_resid, down_kept, down_far):
    half = kept.shape[0]
    return kernel_call(
        last_kernel,
        "last",
        [(SMEM, place)]
        + in_vmem(kept, far)
        + moved(x_a, gains, d_resid, down_kept)
        + in_vmem(down_far),
        [block_shapes(2 * half, D, True), ((4, 1, D // 4), F32)],
        [pltpu.VMEM((1, D), F32)],
    )


def both_rows(own, near, columns):
    return jnp.concatenate([own[:, columns], near[:, columns]], 0)


def leaving_kernel(
    target, ready, place, left_own, left_near, right_own, right_near, leaving
):
    ready()
    width = leaving.shape[0]
    left = both_rows(left_own, left_near, aligned(place[target] * width, width)).T

    def step(j, carry):
        columns = aligned(j * 256, 256)
        right = both_rows(right_own, right_near, columns)
        leaving[:, columns] = matmul(left, right).astype(BF16)
        return carry

    lax.fori_loop(0, leaving.shape[1] // 256, step, 0)


def leaving_gradient(place, target, left_own, left_near, right_own, right_near):
    width, wide = D // 4, right_own.shape[1]
    return kernel_call(
        functools.partial(leaving_kernel, target),
        "leaving_gradient",
        [(SMEM, place)] + moved(left_own, left_near, right_own, right_near),
        [((width, wide), BF16)],
    )[0]


def put_stripe(parts, stripes, block, value):
    if parts == 2:
        at = aligned(block * 128, 128)
        stripes[0, :, at] = value[:, :128]
        stripes[1, :, at] = value[:, 128:]
    else:
        stripes[block // 2, :, aligned((block % 2) * 256, 256)] = value


def stripe_copies(who, stripes, grad, sems):
    parts, _, part = stripes.shape
    return [
        pltpu.make_async_copy(
            stripes.at[k], grad.at[:, aligned((2 * k + who) * part, part)], sems.at[k]
        )
        for k in range(parts)
    ]


def write_stripes(who, stripes, grad, sems):
    copies = stripe_copies(who, stripes, grad, sems)
    for copy in copies:
        copy.start()
    for copy in copies:
        copy.wait()


def staying_kernel(
    ready, place, left_own, left_near, right_own, right_near, grad, stripes, sems
):
    ready()
    parts, width, _ = stripes.shape
    left = both_rows(left_own, left_near, aligned(place[OWN] * width, width)).T

    def step(j, carry):
        right = both_rows(right_own, right_near, aligned(j * 256, 256))
        put_stripe(parts, stripes, j, matmul(left, right))
        return carry

    lax.fori_loop(0, right_own.shape[1] // 256, step, 0)
    write_stripes(place[SIDE], stripes, grad, sems)


def staying_gradient(parts, place, left_own, left_near, right_own, right_near):
    width, wide = D // 4, right_own.shape[1]
    return kernel_call(
        staying_kernel,
        "staying_gradient",
        [(SMEM, place)] + in_stage(left_own, left_near, right_own, right_near),
        [((width, 2 * wide), F32, HBM)],
        [pltpu.VMEM((parts, width, wide // parts), F32), pltpu.SemaphoreType.DMA((parts,))],
    )[0]


def coming_kernel(ready, place, come, before, grad, stripes, sems):
    ready()
    parts, _, part = stripes.shape
    copies = stripe_copies(1 - place[SIDE], stripes, grad, sems)
    for k, copy in enumerate(copies):
        for j in range(come.shape[1] // 256):
            if parts == 2:
                at = j * 256 + k * 128
                stripes[k, :, j * 128 : (j + 1) * 128] = come[:, at : at + 128].astype(F32)
            elif j // 2 == k:
                at = slice((j % 2) * 256, (j % 2) * 256 + 256)
                stripes[k, :, at] = come[:, j * 256 : (j + 1) * 256].astype(F32)
        copy.start()
    for copy in copies:
        copy.wait()


def with_coming(parts, place, come, grad):
    width, wide = come.shape
    return kernel_call(
        coming_kernel,
        "coming_gradient",
        [(SMEM, place), (MOVED, come), (HBM, grad)],
        [(grad.shape, F32, HBM)],
        [pltpu.VMEM((parts, width, wide // parts), F32), pltpu.SemaphoreType.DMA((parts,))],
        aliases=((2, 0),),
    )[0]


def grad_out_kernel(ready, place, mixed_own, mixed_near, d_own, d_near, grad):
    ready()
    left = both_rows(
        mixed_own, mixed_near, aligned(place[CORE] * grad.shape[0], grad.shape[0])
    )
    for base in range(0, D, 512):
        at = slice(base, base + 512)
        grad[:, at] = inner_rows(left, jnp.concatenate([d_own[:, at], d_near[:, at]], 0))


def grad_out_rows(place, mixed_own, mixed_near, d_own, d_near):
    width = mixed_own.shape[1] // 2
    return kernel_call(
        grad_out_kernel,
        "grad_out",
        [(SMEM, place)] + in_stage(mixed_own, mixed_near, d_own, d_near),
        [((width, D), F32)],
    )[0]


def grad_down_kernel(ready, place, h_own, h_near, ca_own, cb_own, ca_near, cb_near, grad, wide):
    ready()
    count, window = grad.shape[0], wide.shape[0]
    core = place[CORE]
    skip = h_own.shape[1] - window
    left = both_rows(h_own, h_near, aligned(core * skip, window))

    def step(n, carry):
        columns = aligned(n * 256, 256)
        right = jnp.concatenate(
            [ref[:, columns] for ref in (ca_own, cb_own, ca_near, cb_near)], 0
        )
        wide[:, columns] = inner_rows(left, right)
        return carry

    lax.fori_loop(0, D // 256, step, 0)
    grad[...] = wide[aligned(core * (count - skip), count, 64), :]


def grad_down_rows(place, h_own, h_near, ca_own, cb_own, ca_near, cb_near):
    count = h_own.shape[1] // 2
    window = -(-count // 128) * 128
    return kernel_call(
        grad_down_kernel,
        "grad_down",
        [(SMEM, place)] + moved(h_own, h_near, ca_own, cb_own, ca_near, cb_near),
        [((count, D), F32)],
        [pltpu.VMEM((window, D), F32)],
    )[0]


def side_columns(weight, half, side, sems):
    part = half.shape[1] // 3
    return [
        pltpu.make_async_copy(
            weight.at[:, aligned((2 * k + side) * part, part)],
            half.at[:, pl.ds(k * part, part)],
            sems.at[k],
        )
        for k in range(3)
    ]


def kept_columns_kernel(ready, place, weight, half, sems):
    copies = side_columns(weight, half, place[SIDE], sems)
    for copy in copies:
        copy.start()
    for copy in copies:
        copy.wait()


def kept_columns(place, weight):
    count, width = weight.shape
    return kernel_call(
        kept_columns_kernel,
        "kept_columns",
        [(SMEM, place), (HBM, weight)],
        [((count, width // 2), BF16)],
        [pltpu.SemaphoreType.DMA((3,))],
    )[0]


def spread_kernel(ready, place, weight, kept, leaving, sems):
    part = weight.shape[1] // 4
    side = place[SIDE]
    copies = []
    for k in range(2):
        for j in range(part // 128):
            for who, target in ((side, kept), (1 - side, leaving)):
                copies.append(
                    pltpu.make_async_copy(
                        weight.at[:, aligned((2 * k + who) * part + j * 128, 128)],
                        target.at[:, pl.ds(j * 256 + k * 128, 128)],
                        sems.at[len(copies)],
                    )
                )
    for copy in copies:
        copy.start()
    for copy in copies:
        copy.wait()


def spread(place, weight):
    count, width = weight.shape
    return kernel_call(
        spread_kernel,
        "spread",
        [(SMEM, place), (HBM, weight)],
        [((count, width // 2), BF16)] * 2,
        [pltpu.SemaphoreType.DMA((width // 128,))],
    )


def sync(*values):
    return lax.optimization_barrier(values)


def after(value, *earlier):
    return lax.optimization_barrier((value,) + earlier)[0]


def pair_body(frames_in, segment_ids, gain_attn, w_qkv, w_out, gain_ffn, w_gate_up, w_down, cotangent):
    member = lax.axis_index("fsdp") % 4
    side, core = member >> 1, member & 1
    position = lax.axis_index("fsdp") // 4
    place = jnp.stack([member, member ^ 2, member ^ 1, member ^ 3, side, core, position])
    place = place.astype(jnp.int32)
    frames = frames_in.shape[0] // POS
    half = POS * frames

    near = lambda rows: swap(rows, 1)

    x_sent, c_sent, qkv_leaving = to_positions(place, frames_in, cotangent, w_qkv)
    qkv_across = swap(qkv_leaving, 3)
    qkv_far = near(qkv_across)
    x_came = exchange(x_sent)
    ids_own = segment_ids.reshape(frames, POS).T
    ids_own = jnp.take(ids_own, jnp.arange(POS) ^ position, axis=0).reshape(1, half)
    gains_own = jnp.stack([gain_attn, gain_ffn])
    gains_near = near(after(gains_own, qkv_leaving))
    qkv_kept = kept_columns(place, after(w_qkv, qkv_leaving))
    w_kept, w_leaving = spread(place, after(w_gate_up, qkv_leaving))
    x_came, ids_own, gains_near, qkv_kept, w_kept, w_leaving = sync(
        x_came, ids_own, gains_near, qkv_kept, w_kept, w_leaving
    )

    x_own = collect(place, x_came, ids_own, gains_own, gains_near)
    x_far = near(swap(x_own, 3))
    qkv_near = near(qkv_kept)
    c_came = exchange([after(c_sent[0], x_own)])
    x_far, qkv_far, qkv_near, w_leaving = sync(x_far, qkv_far, qkv_near, w_leaving)

    w_across = swap(w_leaving, 3)
    qkv_sent, lowered_first, table = first(
        place, x_own, x_far, w_qkv, qkv_far, qkv_near, qkv_across
    )
    qkv_sent, c_came = sync(qkv_sent, c_came)
    c_own = collect_rows(place, c_came)
    out_near, down_near = (near(after(a, lowered_first)) for a in (w_out, w_down))
    qkv, out_near, down_near, c_own = sync(exchange(qkv_sent), out_near, down_near, c_own)

    mixed_sent = attend_local(place, table, qkv)
    c_far = swap(after(c_own, mixed_sent[0]), 2)
    c_own_near, lowered_first_near = (
        near(after(a, mixed_sent[0])) for a in (c_own, lowered_first)
    )
    mixed, w_across, c_far, c_own_near, lowered_first_near = sync(
        exchange(mixed_sent), w_across, c_far, c_own_near, lowered_first_near
    )

    term, leaving, mixed = out_term(place, mixed, w_out, out_near)
    far = swap(leaving, 2)
    d_hidden = d_hidden_rows(place, c_own, after(c_far, leaving), w_down, down_near)
    w_near = near(after(w_kept, leaving))
    far, mixed_near, w_far, w_near, c_far_near, d_hidden = sync(
        far, near(mixed), near(after(w_across, leaving)), w_near, near(after(c_far, leaving)),
        d_hidden,
    )
    resid, lowered_second, hidden, d_gate_up, second, leaving = ffn(
        place, x_own, x_far, term, far, table, d_hidden, (w_kept, w_far, w_near, w_across)
    )

    second_far = swap(leaving, 2)
    hidden_near, lowered_second_near, d_gate_up_near = (
        near(after(rows, leaving)) for rows in (hidden, lowered_second, d_gate_up)
    )
    down_kept, down_leaving = down_term(place, after(hidden, leaving), resid, w_down, down_near)
    sides = (lowered_second, lowered_second_near, d_gate_up, d_gate_up_near)
    gate_up_leaving = leaving_gradient(place, ACROSS, *sides)
    second_far, down_leaving, gate_up_leaving, hidden_near, lowered_second_near = sync(
        second_far, down_leaving, gate_up_leaving, hidden_near, lowered_second_near
    )

    gate_up_come = swap(gate_up_leaving, 3)
    d_resid, d_branch, gain_ffn_terms, d_mixed = mid(
        place, second, second_far, resid, table, c_own, c_far, w_out, out_near
    )
    d_branch_near, gain_ffn_near = near(d_branch), near(gain_ffn_terms[1])
    grad_gate_up = staying_gradient(2, place, after(lowered_second, d_branch), *sides[1:])
    d_mixed, d_branch_near, gain_ffn_near, grad_gate_up = sync(
        exchange(d_mixed), d_branch_near, gain_ffn_near, grad_gate_up
    )

    d_qkv_sent = attend_back_local(place, table, qkv, d_mixed)
    grad_down = grad_down_rows(
        place, after(hidden, d_qkv_sent[0]), hidden_near, c_own, c_far, c_own_near, c_far_near
    )
    grad_out = grad_out_rows(place, mixed, mixed_near, after(d_branch, d_qkv_sent[0]), d_branch_near)
    down_far = swap(after(down_leaving, d_qkv_sent[0]), 2)
    d_qkv, gate_up_come, down_far, grad_down, grad_out = sync(
        exchange(d_qkv_sent), gate_up_come, down_far, grad_down, grad_out
    )

    kept, leaving, d_projected = back_first(
        place, d_qkv, w_qkv, qkv_far, qkv_near, qkv_across
    )
    first_far = swap(leaving, 2)
    qkv_sides = (lowered_first, lowered_first_near, d_projected, near(d_projected))
    first_far, qkv_leaving = sync(first_far, leaving_gradient(place, FAR, *qkv_sides))
    qkv_across_come = swap(qkv_leaving, 3)

    out_sent, gain_attn_terms = last(
        place, kept, first_far, x_own, table, d_resid, down_kept, down_far
    )
    grad_gate_up = with_coming(2, place, after(gate_up_come, gain_attn_terms), grad_gate_up)
    grad_qkv = staying_gradient(3, place, after(lowered_first, gain_attn_terms), *qkv_sides[1:])
    gain_sums = gain_attn_terms[:2] + swap(gain_attn_terms[2:], 2)
    gain_attn_grad = gain_sums[0] + near(gain_sums[1])
    qkv_come = near(after(qkv_across_come, grad_gate_up, grad_qkv))
    grad_qkv = with_coming(3, place, qkv_come, grad_qkv)
    out_come, grad_gate_up, grad_qkv = sync(exchange(out_sent), grad_gate_up, grad_qkv)
    grad_in, block_out = to_frames(place, out_come)
    gain_ffn_grad = (gain_ffn_terms[0] + gain_ffn_near).reshape(-1)
    return (
        block_out,
        grad_in,
        gain_attn_grad.reshape(-1),
        grad_qkv,
        grad_out,
        gain_ffn_grad,
        grad_gate_up,
        grad_down,
    )


def solution(mesh):
    in_specs = (
        P("fsdp", None),
        P("fsdp"),
        P("fsdp"),
        P("fsdp", None),
        P("fsdp", None),
        P("fsdp"),
        P("fsdp", None),
        P("fsdp", None),
        P("fsdp", None),
    )
    out_specs = (
        P("fsdp", None),
        P("fsdp", None),
        P("fsdp"),
        P("fsdp", None),
        P("fsdp", None),
        P("fsdp"),
        P("fsdp", None),
        P("fsdp", None),
    )
    chosen = pair_body if mesh.shape["fsdp"] == 4 * POS else body
    return jax.shard_map(chosen, mesh=mesh, in_specs=in_specs, out_specs=out_specs, check_vma=False)
```

```python
import functools
import math

import jax
import jax.numpy as jnp
from jax import lax
from jax.experimental import pallas as pl
from jax.experimental.pallas import tpu as pltpu
from jax.sharding import PartitionSpec as P

D = 1024
FF = 2816
HEADS = 16
HEAD_DIM = 64
POS = 8


EPSILON = 1e-05


def for_sending(array):

    def short(part):
        return part.astype(jnp.bfloat16) if part.dtype == jnp.float32 else part

    return jax.tree.map(short, array)


def swapped(block, axis, stride):
    count = lax.axis_size(axis)
    route = []
    for low in range(count):
        high = low | 1 << stride
        if high != low and high < count:
            route += [(low, high), (high, low)]
    return lax.ppermute(block, axis, route)


def positions_layout(frame_rows, groups):
    width = frame_rows.shape[-1]
    per_piece = frame_rows.shape[0] // POS // groups
    shaped = frame_rows.reshape(groups, per_piece, POS, width).transpose(2, 0, 1, 3)
    return shaped.reshape(POS * groups, per_piece, width)


def frames_layout(piece_rows, groups):
    width = piece_rows.shape[-1]
    per_piece = piece_rows.shape[1]
    shaped = piece_rows.reshape(POS, groups, per_piece, width).transpose(1, 2, 0, 3)
    return shaped.reshape(groups * per_piece * POS, width)


def inner_rows(left, right):
    return lax.dot_general(
        left, right, (((0,), (0,)), ((), ())), preferred_element_type=jnp.float32
    )


def times_transposed(left, right):
    return lax.dot_general(
        left, right, (((1,), (1,)), ((), ())), preferred_element_type=jnp.float32
    )


def join_pieces(current, partner, member, bit_level):
    upper_half = member >> bit_level & 1 == 1
    return tuple(
        (
            jnp.where(
                upper_half,
                jnp.concatenate([theirs, own_piece], 0),
                jnp.concatenate([own_piece, theirs], 0),
            )
            for own_piece, theirs in zip(current, partner)
        )
    )


def collect_forward(pieces, member, levels):
    current = pieces
    for bit_level in range(levels):
        partner = jax.tree.map(
            lambda part, own: part.astype(own.dtype),
            swapped(for_sending(current), "fsdp", bit_level),
            current,
        )
        current = join_pieces(current, partner, member, bit_level)
    return current


def collect_again(pieces, member, levels):
    current = pieces
    for bit_level in range(levels):
        partner = jax.tree.map(
            lambda part, own: part.astype(own.dtype),
            swapped(for_sending(current), "fsdp", bit_level),
            current,
        )
        current = join_pieces(current, partner, member, bit_level)
    return current


def halving_sum(terms, member, levels, sender):
    current = terms
    for bit_level in reversed(range(levels)):
        upper_half = member >> bit_level & 1 == 1
        leaving = tuple(
            (
                jnp.where(
                    upper_half,
                    term_part[: term_part.shape[0] // 2],
                    term_part[term_part.shape[0] // 2 :],
                )
                for term_part in current
            )
        )
        staying = tuple(
            (
                jnp.where(
                    upper_half,
                    term_part[term_part.shape[0] // 2 :],
                    term_part[: term_part.shape[0] // 2],
                )
                for term_part in current
            )
        )
        arrived = sender(leaving, bit_level)
        current = tuple((held_part + come_part for held_part, come_part in zip(staying, arrived)))
    return current


def send_whole(parts, bit_level):
    return jax.tree.map(
        lambda part, own: part.astype(own.dtype),
        swapped(for_sending(parts), "fsdp", bit_level),
        parts,
    )


def permitted(validity):
    row_place = lax.broadcasted_iota(jnp.int32, (POS, POS), 0)
    column_place = lax.broadcasted_iota(jnp.int32, (POS, POS), 1)
    causal = column_place <= row_place
    same_segment = validity[:, :, None] == validity[:, None, :]
    return (causal[None] & same_segment)[:, None]


def split_projections(qkv_frames):
    frames = qkv_frames.shape[0] // POS
    shaped = qkv_frames.reshape(frames, POS, 3, HEADS, HEAD_DIM)
    return (shaped[:, :, 0], shaped[:, :, 1], shaped[:, :, 2])


def masked_scores(queries, key_rows, allowed):
    scores = jnp.einsum(
        "fqhd,fkhd->fhqk", queries, key_rows, preferred_element_type=jnp.float32
    ) * HEAD_DIM ** (-0.5)
    return jnp.where(allowed, scores, -jnp.inf)


def attend(qkv_frames, validity):
    queries, key_rows, value_rows = split_projections(qkv_frames)
    scores = masked_scores(queries, key_rows, permitted(validity))
    highest = jnp.max(scores, axis=-1, keepdims=True)
    raised = jnp.exp(scores - highest)
    totals = jnp.sum(raised, axis=-1, keepdims=True)
    attn_probs = (raised / totals).astype(jnp.bfloat16)
    attended = jnp.einsum(
        "fhqk,fkhd->fqhd", attn_probs, value_rows, preferred_element_type=jnp.float32
    )
    mixed_heads = attended.reshape(qkv_frames.shape[0], D).astype(jnp.bfloat16)
    return (mixed_heads, highest + jnp.log(totals))


def attend_back(qkv_frames, validity, log_total, d_mixed):
    queries, key_rows, value_rows = split_projections(qkv_frames)
    frames = queries.shape[0]
    scores = masked_scores(queries, key_rows, permitted(validity))
    weights_full = jnp.exp(scores - log_total)
    attn_probs = weights_full.astype(jnp.bfloat16)
    d_heads = d_mixed.reshape(frames, POS, HEADS, HEAD_DIM)
    d_probs = jnp.einsum("fqhd,fkhd->fhqk", d_heads, value_rows, preferred_element_type=jnp.float32)
    d_values = jnp.einsum(
        "fhqk,fqhd->fkhd", attn_probs, d_heads, preferred_element_type=jnp.float32
    )
    d_scores = weights_full * (d_probs - jnp.sum(d_probs * weights_full, axis=-1, keepdims=True))
    d_scores = d_scores.astype(jnp.bfloat16)
    d_queries = jnp.einsum(
        "fhqk,fkhd->fqhd", d_scores, key_rows, preferred_element_type=jnp.float32
    ) * HEAD_DIM ** (-0.5)
    d_keys = jnp.einsum(
        "fhqk,fqhd->fkhd", d_scores, queries, preferred_element_type=jnp.float32
    ) * HEAD_DIM ** (-0.5)
    stacked = jnp.stack([d_queries, d_keys, d_values], axis=2)
    return stacked.reshape(frames * POS, 3 * D).astype(jnp.bfloat16)


def body(frames_in, segment_ids, gain_attn, w_qkv, w_out, gain_ffn, w_gate_up, w_down, cotangent):
    devices = lax.axis_size("fsdp")
    groups = devices // POS
    levels = groups.bit_length() - 1
    member = lax.axis_index("fsdp") % groups
    per_piece = frames_in.shape[0] // POS // groups
    validity = segment_ids.reshape(-1, POS)
    moved_input, moved_cotangent = (
        lax.all_to_all(
            positions_layout(frames_in, groups), "fsdp", split_axis=0, concat_axis=0, tiled=True
        ),
        lax.all_to_all(
            positions_layout(cotangent, groups), "fsdp", split_axis=0, concat_axis=0, tiled=True
        ),
    )
    inputs = moved_input.reshape(-1, D).astype(jnp.float32)
    upstream = moved_cotangent.reshape(-1, D)
    own_pieces = (w_qkv, w_out, w_gate_up, w_down, gain_attn, gain_ffn)
    collected = collect_forward(own_pieces, member, levels)
    whole_qkv, whole_out, whole_gate_up, whole_down, whole_gain_attn, whole_gain_ffn = collected
    gain_first = whole_gain_attn.astype(jnp.float32)
    gain_second = whole_gain_ffn.astype(jnp.float32)
    scale_first = lax.rsqrt(jnp.mean(inputs * inputs, axis=-1, keepdims=True) + EPSILON)
    normed_first = inputs * scale_first
    lowered_first = (normed_first * gain_first).astype(jnp.bfloat16)
    projected = jnp.dot(lowered_first, whole_qkv, preferred_element_type=jnp.float32).astype(
        jnp.bfloat16
    )
    qkv_frames = frames_layout(
        lax.all_to_all(
            projected.reshape(devices, per_piece, 3 * D),
            "fsdp",
            split_axis=0,
            concat_axis=0,
            tiled=True,
        ),
        groups,
    )
    mixed_frames, log_total = attend(qkv_frames, validity)
    mixed_rows = lax.all_to_all(
        positions_layout(mixed_frames, groups), "fsdp", split_axis=0, concat_axis=0, tiled=True
    ).reshape(-1, D)
    residual = inputs + jnp.dot(mixed_rows, whole_out, preferred_element_type=jnp.float32)
    scale_second = lax.rsqrt(jnp.mean(residual * residual, axis=-1, keepdims=True) + EPSILON)
    normed_second = residual * scale_second
    lowered_second = (normed_second * gain_second).astype(jnp.bfloat16)
    gate_up = jnp.dot(lowered_second, whole_gate_up, preferred_element_type=jnp.float32)
    gate_part = gate_up[:, :FF]
    up_part = gate_up[:, FF:]
    sigmoid_gate = jax.nn.sigmoid(gate_part)
    activated = gate_part * sigmoid_gate
    hidden = (activated * up_part).astype(jnp.bfloat16)
    result_rows = (
        residual + jnp.dot(hidden, whole_down, preferred_element_type=jnp.float32)
    ).astype(jnp.bfloat16)
    block_out = frames_layout(
        lax.all_to_all(
            result_rows.reshape(devices, per_piece, D),
            "fsdp",
            split_axis=0,
            concat_axis=0,
            tiled=True,
        ),
        groups,
    )
    collected = collect_again(own_pieces, member, levels)
    whole_qkv, whole_out, whole_gate_up, whole_down, whole_gain_attn, whole_gain_ffn = collected
    gain_first = whole_gain_attn.astype(jnp.float32)
    gain_second = whole_gain_ffn.astype(jnp.float32)
    grad_down_term = inner_rows(hidden, upstream)
    d_hidden = times_transposed(upstream, whole_down)
    d_gate = d_hidden * up_part * sigmoid_gate * (1.0 + gate_part * (1.0 - sigmoid_gate))
    d_up = d_hidden * activated
    d_gate_up = jnp.concatenate([d_gate, d_up], axis=1).astype(jnp.bfloat16)
    grad_gate_up_term = inner_rows(lowered_second, d_gate_up)
    d_second = times_transposed(d_gate_up, whole_gate_up)
    grad_gain_ffn_term = jnp.sum(d_second * normed_second, axis=0)
    scaled_second = d_second * gain_second
    d_residual = upstream.astype(jnp.float32) + scale_second * (
        scaled_second
        - normed_second * jnp.mean(scaled_second * normed_second, axis=-1, keepdims=True)
    )
    d_branch = d_residual.astype(jnp.bfloat16)
    grad_out_term = inner_rows(mixed_rows, d_branch)
    d_mixed = times_transposed(d_branch, whole_out).astype(jnp.bfloat16)
    d_mixed_frames = frames_layout(
        lax.all_to_all(
            d_mixed.reshape(devices, per_piece, D), "fsdp", split_axis=0, concat_axis=0, tiled=True
        ),
        groups,
    )
    d_qkv_frames = attend_back(qkv_frames, validity, log_total, d_mixed_frames)
    d_projected = lax.all_to_all(
        positions_layout(d_qkv_frames, groups), "fsdp", split_axis=0, concat_axis=0, tiled=True
    ).reshape(-1, 3 * D)
    grad_qkv_term = inner_rows(lowered_first, d_projected)
    d_first = times_transposed(d_projected, whole_qkv)
    grad_gain_attn_term = jnp.sum(d_first * normed_first, axis=0)
    scaled_first = d_first * gain_first
    d_inputs = d_residual + scale_first * (
        scaled_first - normed_first * jnp.mean(scaled_first * normed_first, axis=-1, keepdims=True)
    )
    grad_in = frames_layout(
        lax.all_to_all(
            d_inputs.reshape(devices, per_piece, D).astype(jnp.bfloat16),
            "fsdp",
            split_axis=0,
            concat_axis=0,
            tiled=True,
        ).astype(jnp.float32),
        groups,
    )
    shares = halving_sum(
        (
            grad_qkv_term,
            grad_out_term,
            grad_gate_up_term,
            grad_down_term,
            grad_gain_attn_term,
            grad_gain_ffn_term,
        ),
        member,
        levels,
        send_whole,
    )
    return (block_out, grad_in, shares[4], shares[0], shares[1], shares[5], shares[2], shares[3])

VMEM = pl.BlockSpec(memory_space=pltpu.VMEM)
SMEM = pl.BlockSpec(memory_space=pltpu.SMEM)
HBM = pl.BlockSpec(memory_space=pltpu.HBM)
STAGED = pl.BlockSpec(memory_space=pltpu.HBM)
MOVED = pl.BlockSpec(memory_space=pl.ANY)
EITHER = pl.BlockSpec(memory_space=pl.ANY)
BF16 = jnp.bfloat16
F32 = jnp.float32
OWN, FAR, NEAR, ACROSS, SIDE, CORE, POSITION = range(7)
TAIL = 16


def swap(block, mask):
    count = lax.axis_size("fsdp")
    return lax.ppermute(block, "fsdp", [(i, i ^ mask) for i in range(count)])


def exchange(blocks):
    count = lax.axis_size("fsdp")
    stride = count // POS
    if len(blocks) == POS:
        return [blocks[0]] + [swap(blocks[k], stride * k) for k in range(1, POS)]
    lanes = [[r + stride * k for k in range(POS)] for r in range(stride)]
    return [
        lax.all_to_all(
            blocks[0], "fsdp", split_axis=0, concat_axis=0, tiled=True, axis_index_groups=lanes
        )
    ]


def kernel_call(kernel, name, args, outs, scratch=(), aliases=()):
    flat = lambda items: [p for item in items for p in (item if isinstance(item, list) else [item])]
    staged = [n for n, (spec, _) in enumerate(flat(args)) if spec is STAGED or spec is MOVED]
    arrays = [
        pltpu.with_memory_space_constraint(a, pltpu.HBM) if spec is STAGED or spec is HBM else a
        for spec, a in flat(args)
    ]
    scratch = list(scratch)
    own = len(scratch)
    scratch += [pltpu.VMEM(arrays[n].shape, arrays[n].dtype) for n in staged]
    scratch += [pltpu.SemaphoreType.DMA((max(len(staged), 1),))]
    held = sum(
        math.prod(ref.shape) * jnp.dtype(ref.dtype).itemsize
        for ref in scratch
        if ref.memory_space == pltpu.VMEM
    )

    def grouped(items, values):
        return [
            [next(values) for _ in item] if isinstance(item, list) else next(values)
            for item in items
        ]

    def body_kernel(*refs):
        inputs, outputs = list(refs[: len(arrays)]), refs[len(arrays) :]
        outputs, extra = outputs[: len(flat(outs))], outputs[len(flat(outs)) :]
        extra, landing, sems = extra[:own], extra[own:-1], extra[-1]
        copies = []
        for k, n in enumerate(staged):
            copies.append(pltpu.make_async_copy(inputs[n], landing[k], sems.at[k]))
            inputs[n] = landing[k]
        for copy in copies:
            copy.start()

        def ready():
            for copy in copies:
                copy.wait()

        kernel(ready, *grouped(args, iter(inputs)), *grouped(outs, iter(outputs)), *extra)

    result = pl.pallas_call(
        body_kernel,
        name=name,
        in_specs=[spec for spec, _ in flat(args)],
        out_specs=[spec[0] if spec else VMEM for _, _, *spec in flat(outs)],
        out_shape=[
            pltpu.HBM(s, d) if spec else jax.ShapeDtypeStruct(s, d) for s, d, *spec in flat(outs)
        ],
        input_output_aliases=dict(aliases),
        scratch_shapes=scratch,
        cost_estimate=pl.CostEstimate(flops=1, bytes_accessed=1, transcendentals=0),
        compiler_params=pltpu.CompilerParams(vmem_limit_bytes=held + (8 << 20)),
    )(*arrays)
    return grouped(outs, iter(result))


def views(blocks, place):
    if len(blocks) == POS:
        return blocks
    return [blocks[0].at[place[POSITION] ^ k] for k in range(POS)]


def matmul(left, right):
    return jnp.dot(left, right, preferred_element_type=F32)


def aligned(start, size, step=128):
    return pl.ds(pl.multiple_of(start, step), size)


def rows_of(refs, rel, columns=slice(None)):
    frames = refs[0].shape[0] // 2
    return jnp.concatenate([ref[rel * frames : (rel + 1) * frames, columns] for ref in refs], 0)


def put_rows(refs, rel, columns, value):
    frames = refs[0].shape[0] // 2
    for k, ref in enumerate(refs):
        ref[rel * frames : (rel + 1) * frames, columns] = value[k * frames : (k + 1) * frames]


def block_shapes(rows, width, joined):
    if joined:
        return [((POS, rows // POS, width), BF16)]
    return [((rows // POS, width), BF16)] * POS


def in_vmem(*arrays):
    return [(VMEM, a) for a in arrays]


def in_stage(*arrays):
    return [(STAGED, a) for a in arrays]


def moved(*arrays):
    return [(MOVED, a) for a in arrays]


def place_matrix(size, to_positions, position):
    frames = size // POS
    row = lax.broadcasted_iota(jnp.int32, (size, size), 0)
    column = lax.broadcasted_iota(jnp.int32, (size, size), 1)
    if not to_positions:
        row, column = column, row
    return (column == (row % frames) * POS + ((row // frames) ^ position)).astype(F32).astype(BF16)


def to_positions_kernel(ready, place, x_rows, c_rows, weight, x_blocks, c_blocks, half, sems):
    copies = side_columns(weight, half, 1 - place[SIDE], sems)
    for copy in copies:
        copy.start()
    order = place_matrix(x_rows.shape[0], True, place[POSITION])
    ready()
    for rows, blocks in ((x_rows, x_blocks), (c_rows, c_blocks)):
        moved_rows = matmul(order, rows[...]).astype(BF16)
        count = rows.shape[0] // POS
        for k, block in enumerate(views(blocks, place)):
            block[...] = moved_rows[k * count : (k + 1) * count]
    for copy in copies:
        copy.wait()


def to_positions(place, x_rows, c_rows, weight):
    size, width = x_rows.shape
    return kernel_call(
        to_positions_kernel,
        "to_positions",
        [(SMEM, place)] + in_stage(x_rows, c_rows) + [(HBM, weight)],
        [block_shapes(size, width, True), block_shapes(size, width, True),
         ((weight.shape[0], weight.shape[1] // 2), BF16)],
        [pltpu.SemaphoreType.DMA((3,))],
    )


def joined(blocks, place):
    return jnp.concatenate([block[...] for block in views(blocks, place)], 0)


def collect_rows_kernel(ready, place, blocks, rows):
    ready()
    rows[...] = joined(blocks, place)


def collect_rows(place, blocks):
    count, width = blocks[0].shape[-2:]
    return kernel_call(
        collect_rows_kernel,
        "collect_rows",
        [(SMEM, place), in_vmem(*blocks)],
        [((count * POS, width), BF16)],
    )[0]


def collect_kernel(ready, place, blocks, ids, gains_own, gains_near, x_own):
    ready()
    half = x_own.shape[0] - TAIL
    x_own[:half, :] = joined(blocks, place)
    padded = lambda *parts: jnp.concatenate(
        parts + (jnp.zeros((1, D - sum(p.shape[1] for p in parts)), F32),), 1
    )
    row = lax.broadcasted_iota(jnp.int32, (TAIL, D), 0)
    tail = jnp.where(row == 2, padded(ids[...].astype(F32)), 0.0)
    for k in range(2):
        gain = padded(gains_own[k : k + 1, :].astype(F32), gains_near[k : k + 1, :].astype(F32))
        tail = jnp.where(row == k, gain, tail)
    x_own[half:, :] = tail.astype(BF16)


def collect(place, blocks, ids, gains_own, gains_near):
    count, width = blocks[0].shape[-2:]
    return kernel_call(
        collect_kernel,
        "collect",
        [(SMEM, place), in_vmem(*blocks)] + in_vmem(ids, gains_own, gains_near),
        [((count * POS + TAIL, width), BF16)],
    )[0]


def to_frames_kernel(ready, place, blocks, *rows):
    ready()
    blocks = views(blocks, place)
    order = place_matrix(rows[0].shape[0], False, place[POSITION])
    for rel in range(2):
        rows[rel][...] = matmul(order, rows_of(blocks, rel)).astype(rows[rel].dtype)


def to_frames(place, blocks):
    size = blocks[0].shape[-2] * POS // 2
    return kernel_call(
        to_frames_kernel,
        "to_frames",
        [(SMEM, place), in_vmem(*blocks)],
        [((size, D), F32), ((size, D), BF16)],
    )


def first_kernel(
    ready, place, x_a, x_b, w_own, w_far, w_near, w_across, qkv, lowered_out, table_out,
    lowered, table, w, sems,
):
    qkv = views(qkv, place)
    half, width = lowered.shape[0] // 2, w_own.shape[0]
    part = w.shape[1] // 3
    side = place[SIDE]
    at_rows = lambda rank: aligned(place[rank] * width, width)
    copies = [
        pltpu.make_async_copy(
            w_own.at[:, aligned((2 * k + side) * part, part)],
            w.at[at_rows(OWN), pl.ds(k * part, part)],
            sems.at[k],
        )
        for k in range(3)
    ]
    copies.append(pltpu.make_async_copy(w_far, w.at[at_rows(FAR)], sems.at[3]))
    copies.append(pltpu.make_async_copy(w_near, w.at[at_rows(NEAR)], sems.at[4]))
    copies.append(pltpu.make_async_copy(w_across, w.at[at_rows(ACROSS)], sems.at[5]))
    for copy in copies:
        copy.start()
    ready()
    table[...] = jnp.zeros_like(table)
    for k, (ref, ranks) in enumerate(((x_a, (OWN, NEAR)), (x_b, (FAR, ACROSS)))):
        tail = ref[half:, :].astype(F32)
        for n, rank in enumerate(ranks):
            table[0:2, at_rows(rank)] = tail[0:2, n * width : (n + 1) * width]
        table[2 + k : 3 + k, 0:half] = tail[2:3, 0:half]
    gain = table[0:1, :]
    for rel, ref in enumerate((x_a, x_b)):
        rows = ref[:half, :].astype(F32)
        scale = lax.rsqrt(jnp.mean(rows * rows, axis=-1, keepdims=True) + EPSILON)
        lowered[rel * half : (rel + 1) * half, :] = (rows * scale * gain).astype(BF16)
    leaving = [
        pltpu.make_async_copy(lowered, lowered_out, sems.at[6]),
        pltpu.make_async_copy(table, table_out, sems.at[7]),
    ]
    for copy in leaving:
        copy.start()
    for copy in copies:
        copy.wait()

    def step(n, carry):
        columns = aligned(n * 256, 256, 256)
        value = matmul(lowered[...], w[:, columns]).astype(BF16)
        put_rows(qkv, 0, columns, value[:half])
        put_rows(qkv, 1, columns, value[half:])
        return carry

    lax.fori_loop(0, w.shape[1] // 256, step, 0)
    for copy in leaving:
        copy.wait()


def first(place, x_a, x_b, w_own, w_far, w_near, w_across):
    half = x_a.shape[0] - TAIL
    wide = w_far.shape[1]
    return kernel_call(
        first_kernel,
        "first",
        [(SMEM, place), (MOVED, x_a), (MOVED, x_b), (HBM, w_own), (EITHER, w_far),
         (EITHER, w_near), (EITHER, w_across)],
        [block_shapes(2 * half, wide, True), ((2 * half, D), BF16, HBM), ((8, D), F32, HBM)],
        [pltpu.VMEM((2 * half, D), BF16), pltpu.VMEM((8, D), F32), pltpu.VMEM((D, wide), BF16),
         pltpu.SemaphoreType.DMA((8,))],
    )


def allowed_pairs(ids, position):
    size = ids.shape[1]
    frames = size // POS
    row = lax.broadcasted_iota(jnp.int32, (size, size), 0)
    column = lax.broadcasted_iota(jnp.int32, (size, size), 1)
    across = jnp.broadcast_to(ids, (size, size))
    same = (across == across.T) & (row % frames == column % frames)
    mask = same & ((column // frames) ^ position <= (row // frames) ^ position)
    return jnp.concatenate([mask, mask], 1)


def pair_of_heads(rows, low):
    return jnp.concatenate([rows * low, rows * (1 - low)], 0)


def lane_halves(value, reduce):
    size = value.shape[1] // 2
    parts = [
        jnp.broadcast_to(reduce(value[:, k * size : (k + 1) * size]), (value.shape[0], size))
        for k in range(2)
    ]
    return jnp.concatenate(parts, 1)


def pair_probs(query, key_pair, mask):
    scores = times_transposed(query, key_pair) * HEAD_DIM ** (-0.5)
    scores = jnp.where(mask, scores, -jnp.inf)
    raised = jnp.exp(scores - lane_halves(scores, lambda a: jnp.max(a, -1, keepdims=True)))
    return raised / lane_halves(raised, lambda a: jnp.sum(a, -1, keepdims=True))


def first_head_lanes():
    lane = lax.broadcasted_iota(jnp.int32, (1, 2 * HEAD_DIM), 1)
    return (lane < HEAD_DIM).astype(F32).astype(BF16)


def attend_kernel(ready, place, table, qkv, mixed):
    qkv, mixed = views(qkv, place), views(mixed, place)
    size = POS * mixed[0].shape[0] // 2
    part = mixed[0].shape[1]
    low = first_head_lanes()
    ready()
    for rel in range(2):
        mask = allowed_pairs(table[2 + rel : 3 + rel, 0:size], place[POSITION])
        for base in range(0, part, 2 * HEAD_DIM):
            query, key_rows, value_rows = (
                rows_of(qkv, rel, slice(k * part + base, k * part + base + 2 * HEAD_DIM))
                for k in range(3)
            )
            probs = pair_probs(query, pair_of_heads(key_rows, low), mask)
            value = matmul(probs.astype(BF16), pair_of_heads(value_rows, low))
            put_rows(mixed, rel, slice(base, base + 2 * HEAD_DIM), value.astype(BF16))


def attend_local(place, table, qkv):
    rows, wide = qkv[0].shape[-2:]
    return kernel_call(
        attend_kernel,
        "attend",
        [(SMEM, place), (MOVED, table), moved(*qkv)],
        [block_shapes(rows * POS, wide // 3, True)],
    )[0]


def attend_back_kernel(ready, place, table, qkv, d_mixed, d_qkv):
    qkv, d_mixed, d_qkv = (views(blocks, place) for blocks in (qkv, d_mixed, d_qkv))
    part = d_mixed[0].shape[1]
    pair = 2 * HEAD_DIM
    low = first_head_lanes()
    size = POS * d_mixed[0].shape[0] // 2
    low_full = lax.broadcasted_iota(jnp.int32, (size, pair), 1) < HEAD_DIM
    scale = HEAD_DIM ** (-0.5)
    ready()
    for rel in range(2):
        mask = allowed_pairs(table[2 + rel : 3 + rel, 0:size], place[POSITION])
        for base in range(0, part, pair):
            query, key_rows, value_rows = (
                rows_of(qkv, rel, slice(k * part + base, k * part + base + pair))
                for k in range(3)
            )
            d_rows = rows_of(d_mixed, rel, slice(base, base + pair))
            keys = pair_of_heads(key_rows, low)
            probs = pair_probs(query, keys, mask)
            d_probs = times_transposed(d_rows, pair_of_heads(value_rows, low))
            inner = lane_halves(d_probs * probs, lambda a: jnp.sum(a, -1, keepdims=True))
            d_scores = (probs * (d_probs - inner)).astype(BF16)
            d_query = matmul(d_scores, keys) * scale
            d_key = inner_rows(d_scores, query) * scale
            d_value = inner_rows(probs.astype(BF16), d_rows)
            d_key = jnp.where(low_full, d_key[:size], d_key[size:])
            d_value = jnp.where(low_full, d_value[:size], d_value[size:])
            for k, value in enumerate((d_query, d_key, d_value)):
                columns = slice(k * part + base, k * part + base + pair)
                put_rows(d_qkv, rel, columns, value.astype(BF16))


def attend_back_local(place, table, qkv, d_mixed):
    rows, wide = qkv[0].shape[-2:]
    return kernel_call(
        attend_back_kernel,
        "attend_back",
        [(SMEM, place), (MOVED, table), moved(*qkv), in_vmem(*d_mixed)],
        [block_shapes(rows * POS, wide, True)],
    )[0]


def chip_rows(place, own, near, whole, sems):
    count = own.shape[0]
    core = place[CORE]
    return [
        pltpu.make_async_copy(own, whole.at[aligned(core * count, count, 64)], sems.at[0]),
        pltpu.make_async_copy(near, whole.at[aligned((1 - core) * count, count, 64)], sems.at[1]),
    ]


def out_kernel(ready, place, w_own, w_near, mixed, term, leaving, mixed_rows, w, sems):
    mixed = views(mixed, place)
    copies = chip_rows(place, w_own, w_near, w, sems)
    for copy in copies:
        copy.start()
    ready()
    rows = jnp.concatenate([rows_of(mixed, 0), rows_of(mixed, 1)], 0)
    mixed_rows[...] = rows
    half = rows.shape[0] // 2
    for copy in copies:
        copy.wait()
    for base in range(0, D, 512):
        value = matmul(rows, w[:, base : base + 512])
        term[:, base : base + 512] = value
        lowered = value.astype(BF16)
        leaving[:half, base : base + 512] = lowered[half:]
        leaving[half:, base : base + 512] = lowered[:half]


def out_term(place, mixed, w_own, w_near):
    rows = POS * mixed[0].shape[-2]
    inner = 2 * w_own.shape[0]
    return kernel_call(
        out_kernel,
        "out_term",
        [(SMEM, place), (HBM, w_own), (HBM, w_near), in_vmem(*mixed)],
        [((rows, D), F32), ((rows, D), BF16), ((rows, inner), BF16)],
        [pltpu.VMEM((inner, D), BF16), pltpu.SemaphoreType.DMA((2,))],
    )


def aside_kernel(ready, place, x_a, x_b, term, c_a, c_b, w_own, w_near, base, d_hidden, w, sems):
    copies = chip_rows(place, w_own, w_near, w, sems)
    for copy in copies:
        copy.start()
    ready()
    half = c_a.shape[0]
    for rel, ref in enumerate((x_a, x_b)):
        at = pl.ds(rel * half, half)
        base[at, :] = ref[:half, :].astype(F32) + term[at, :]
    upstream = jnp.concatenate([c_a[...], c_b[...]], 0)
    for copy in copies:
        copy.wait()
    inner = w.shape[0]
    for low in range(0, inner, 256):
        high = min(low + 256, inner)
        d_hidden[:, low:high] = times_transposed(upstream, w[low:high, :])


def aside(place, x_a, x_b, term, c_a, c_b, w_own, w_near):
    rows, inner = 2 * c_a.shape[0], 2 * w_own.shape[0]
    return kernel_call(
        aside_kernel,
        "aside",
        [(SMEM, place), (MOVED, x_a), (MOVED, x_b), (VMEM, term), (MOVED, c_a), (MOVED, c_b),
         (HBM, w_own), (HBM, w_near)],
        [((rows, D), F32), ((rows, inner), F32)],
        [pltpu.VMEM((inner, D), BF16), pltpu.SemaphoreType.DMA((2,))],
    )


def ffn_kernel(
    ready, place, base, far, table, d_hidden_all, *rest
):
    kept, near, far_a, across_a, far_b, across_b = rest[:6]
    resid, lowered, hidden, d_gate_up, second, leaving = rest[6:12]
    w, sems = rest[12:]
    half, width, steps = base.shape[0] // 2, kept.shape[0], w.shape[0]
    split = far_a.shape[1] // 256

    def begin(arrived, j, carry):
        sources = ((kept, OWN, 0), (near, NEAR, 0)) + arrived
        for source, rank, before in sources:
            pltpu.make_async_copy(
                source.at[:, aligned((j - before) * 256, 256)],
                w.at[j, aligned(place[rank] * width, width)],
                sems.at[j, rank],
            ).start()
        return carry

    for low, high, far_part, across_part in (
        (0, split, far_a, across_a), (split, steps, far_b, across_b)
    ):
        arrived = ((far_part, FAR, low), (across_part, ACROSS, low))
        lax.fori_loop(low, high, functools.partial(begin, arrived), 0)
    ready()
    gain = table[1:2, :]
    for rel in range(2):
        at = pl.ds(rel * half, half)
        rows = base[at, :] + far[at, :].astype(F32)
        resid[at, :] = rows
        scale = lax.rsqrt(jnp.mean(rows * rows, axis=-1, keepdims=True) + EPSILON)
        lowered[at, :] = (rows * scale * gain).astype(BF16)

    def step(j, carry):
        for rank in range(4):
            rows = w.at[j, pl.ds(rank * width, width)]
            pltpu.make_async_copy(rows, rows, sems.at[j, rank]).wait()
        gate_up = matmul(lowered[...], w[j])
        gate, up = gate_up[:, :128], gate_up[:, 128:]
        d_hidden = d_hidden_all[:, aligned(j * 128, 128)]
        sigmoid = jax.nn.sigmoid(gate)
        activated = gate * sigmoid
        hidden[:, aligned(j * 128, 128)] = (activated * up).astype(BF16)
        d_gate = d_hidden * up * sigmoid * (1.0 + gate * (1.0 - sigmoid))
        d_gate_up[:, aligned(j * 256, 128)] = d_gate.astype(BF16)
        d_gate_up[:, aligned(j * 256 + 128, 128)] = (d_hidden * activated).astype(BF16)
        return carry

    lax.fori_loop(0, steps, step, 0)

    def back(n, carry):
        columns = aligned(n * 256, 256)
        value = times_transposed(d_gate_up[:, 0:256], w[0, columns, :])
        for j in range(1, steps):
            value += times_transposed(d_gate_up[:, j * 256 : (j + 1) * 256], w[j, columns, :])
        second[:, columns] = value
        lower = value.astype(BF16)
        leaving[:half, columns] = lower[half:]
        leaving[half:, columns] = lower[:half]
        return carry

    lax.fori_loop(0, D // 256, back, 0)


def ffn(place, base, far, table, d_hidden, pieces):
    rows, inner = d_hidden.shape
    wide, steps = 2 * inner, inner // 128
    return kernel_call(
        ffn_kernel,
        "ffn",
        [(SMEM, place)]
        + in_vmem(base, far) + moved(table) + in_vmem(d_hidden)
        + [(HBM if n in (0, 3, 5) else EITHER, a) for n, a in enumerate(pieces)],
        [((rows, D), F32), ((rows, D), BF16), ((rows, inner), BF16), ((rows, wide), BF16),
         ((rows, D), F32), ((rows, D), BF16)],
        [pltpu.VMEM((steps, D, 256), BF16), pltpu.SemaphoreType.DMA((steps, 4))],
    )


def down_kernel(ready, place, hidden, resid, w_own, w_near, kept, leaving, w, sems):
    copies = chip_rows(place, w_own, w_near, w, sems)
    for copy in copies:
        copy.start()
    half = kept.shape[0]
    ready()
    for copy in copies:
        copy.wait()

    def step(n, carry):
        columns = aligned(n * 256, 256)
        value = matmul(hidden[...], w[:, columns])
        kept[:, columns] = resid[:half, columns] + value[:half]
        leaving[:, columns] = value[half:].astype(BF16)
        return carry

    lax.fori_loop(0, D // 256, step, 0)


def down_term(place, hidden, resid, w_own, w_near):
    rows, inner = hidden.shape
    return kernel_call(
        down_kernel,
        "down_term",
        [(SMEM, place), (STAGED, hidden), (VMEM, resid), (HBM, w_own), (HBM, w_near)],
        [((rows // 2, D), F32), ((rows // 2, D), BF16)],
        [pltpu.VMEM((inner, D), BF16), pltpu.SemaphoreType.DMA((2,))],
    )


def mid_kernel(
    ready, place, second, far, resid, gains, c_a, c_b, w_own, w_near,
    d_resid_out, d_branch, gain_terms, d_mixed, d_resid, w, sums, sems,
):
    d_mixed = views(d_mixed, place)
    copies = chip_rows(place, w_own, w_near, w, sems)
    for copy in copies:
        copy.start()
    half, width = c_a.shape[0], w_own.shape[0]
    total = None
    for rel in range(2):
        at = pl.ds(rel * half, half)
        rows = resid[at, :]
        scale = lax.rsqrt(jnp.mean(rows * rows, axis=-1, keepdims=True) + EPSILON)
        d_rows = second[at, :] + far[at, :].astype(F32)
        part = jnp.sum(d_rows * (rows * scale), axis=0, keepdims=True)
        total = part if total is None else total + part
    ready()
    gain = gains[1:2, :]
    for rel, c_ref in enumerate((c_a, c_b)):
        at = pl.ds(rel * half, half)
        rows = resid[at, :]
        scale = lax.rsqrt(jnp.mean(rows * rows, axis=-1, keepdims=True) + EPSILON)
        normed = rows * scale
        scaled = (second[at, :] + far[at, :].astype(F32)) * gain
        value = c_ref[...].astype(F32) + scale * (
            scaled - normed * jnp.mean(scaled * normed, axis=-1, keepdims=True)
        )
        if rel == 0:
            d_resid[...] = value
            leaving = pltpu.make_async_copy(d_resid, d_resid_out, sems.at[2])
            leaving.start()
        d_branch[at, :] = value.astype(BF16)
    sums[...] = total
    gain_terms[0] = sums[:, aligned(place[OWN] * width, width)]
    gain_terms[1] = sums[:, aligned(place[NEAR] * width, width)]
    for copy in copies:
        copy.wait()
    for base in range(0, w.shape[0], 256):
        value = times_transposed(d_branch[...], w[base : base + 256, :]).astype(BF16)
        put_rows(d_mixed, 0, slice(base, base + 256), value[:half])
        put_rows(d_mixed, 1, slice(base, base + 256), value[half:])
    leaving.wait()


def mid(place, second, far, resid, gains, c_a, c_b, w_own, w_near):
    rows = second.shape[0]
    width = w_own.shape[0]
    return kernel_call(
        mid_kernel,
        "mid",
        [(SMEM, place), (VMEM, second), (VMEM, far), (VMEM, resid), (MOVED, gains),
         (MOVED, c_a), (MOVED, c_b), (HBM, w_own), (HBM, w_near)],
        [((rows // 2, D), F32, HBM), ((rows, D), BF16), ((2, 1, width), F32),
         block_shapes(rows, 2 * width, True)],
        [pltpu.VMEM((rows // 2, D), F32), pltpu.VMEM((2 * width, D), BF16),
         pltpu.VMEM((1, D), F32), pltpu.SemaphoreType.DMA((3,))],
    )


def back_first_kernel(
    ready, place, w_own, w_far, w_near, w_across, d_qkv, kept, leaving, rows, w, sems
):
    d_qkv = views(d_qkv, place)
    half, width = kept.shape[0], w_own.shape[0]
    part = w.shape[2] // 3
    side = place[SIDE]
    copies = [
        pltpu.make_async_copy(
            w_own.at[:, aligned((2 * k + side) * part, part)],
            w.at[0, :, pl.ds(k * part, part)],
            sems.at[k],
        )
        for k in range(3)
    ]
    copies.append(pltpu.make_async_copy(w_far, w.at[1], sems.at[3]))
    copies.append(pltpu.make_async_copy(w_near, w.at[2], sems.at[4]))
    copies.append(pltpu.make_async_copy(w_across, w.at[3], sems.at[5]))
    for copy in copies:
        copy.start()
    ready()
    rows[:half, :] = rows_of(d_qkv, 0)
    rows[half:, :] = rows_of(d_qkv, 1)
    for rank in range(4):
        for copy in copies[:3] if rank == 0 else copies[rank + 2 : rank + 3]:
            copy.wait()
        columns = aligned(place[rank] * width, width)
        value = times_transposed(rows[...], w[rank])
        kept[:, columns] = value[:half]
        leaving[:, columns] = value[half:].astype(BF16)


def back_first(place, d_qkv, w_own, w_far, w_near, w_across):
    rows, wide = POS * d_qkv[0].shape[-2], d_qkv[0].shape[-1]
    return kernel_call(
        back_first_kernel,
        "back_first",
        [(SMEM, place), (HBM, w_own), (HBM, w_far), (HBM, w_near), (HBM, w_across),
         in_vmem(*d_qkv)],
        [((rows // 2, D), F32), ((rows // 2, D), BF16), ((rows, wide), BF16)],
        [pltpu.VMEM((4, w_own.shape[0], wide), BF16), pltpu.SemaphoreType.DMA((6,))],
    )


def last_kernel(
    ready, place, kept, far, x_a, gains, d_resid, down_kept, down_far, blocks, gain_terms, sums
):
    ready()
    blocks = views(blocks, place)
    width = gain_terms.shape[2]
    rows = x_a[: kept.shape[0], :].astype(F32)
    scale = lax.rsqrt(jnp.mean(rows * rows, axis=-1, keepdims=True) + EPSILON)
    normed = rows * scale
    d_rows = kept[...] + far[...].astype(F32)
    sums[...] = jnp.sum(d_rows * normed, axis=0, keepdims=True)
    scaled = d_rows * gains[0:1, :]
    value = d_resid[...] + scale * (
        scaled - normed * jnp.mean(scaled * normed, axis=-1, keepdims=True)
    )
    put_rows(blocks, 0, slice(None), value.astype(BF16))
    put_rows(blocks, 1, slice(None), (down_kept[...] + down_far[...].astype(F32)).astype(BF16))
    for slot, rank in enumerate((OWN, NEAR, FAR, ACROSS)):
        gain_terms[slot] = sums[:, aligned(place[rank] * width, width)]


def last(place, kept, far, x_a, gains, d_resid, down_kept, down_far):
    half = kept.shape[0]
    return kernel_call(
        last_kernel,
        "last",
        [(SMEM, place)]
        + in_vmem(kept, far)
        + moved(x_a, gains, d_resid, down_kept)
        + in_vmem(down_far),
        [block_shapes(2 * half, D, True), ((4, 1, D // 4), F32)],
        [pltpu.VMEM((1, D), F32)],
    )


def both_rows(own, near, columns):
    return jnp.concatenate([own[:, columns], near[:, columns]], 0)


def leaving_kernel(
    target, ready, place, left_own, left_near, right_own, right_near, leaving
):
    ready()
    width = leaving.shape[0]
    left = both_rows(left_own, left_near, aligned(place[target] * width, width)).T

    def step(j, carry):
        columns = aligned(j * 256, 256)
        right = both_rows(right_own, right_near, columns)
        leaving[:, columns] = matmul(left, right).astype(BF16)
        return carry

    lax.fori_loop(0, leaving.shape[1] // 256, step, 0)


def leaving_gradient(place, target, left_own, left_near, right_own, right_near):
    width, wide = D // 4, right_own.shape[1]
    return kernel_call(
        functools.partial(leaving_kernel, target),
        "leaving_gradient",
        [(SMEM, place)] + moved(left_own, left_near, right_own, right_near),
        [((width, wide), BF16)],
    )[0]


def put_stripe(parts, stripes, block, value):
    if parts == 2:
        at = aligned(block * 128, 128)
        stripes[0, :, at] = value[:, :128]
        stripes[1, :, at] = value[:, 128:]
    else:
        stripes[block // 2, :, aligned((block % 2) * 256, 256)] = value


def stripe_copies(who, stripes, grad, sems):
    parts, _, part = stripes.shape
    return [
        pltpu.make_async_copy(
            stripes.at[k], grad.at[:, aligned((2 * k + who) * part, part)], sems.at[k]
        )
        for k in range(parts)
    ]


def write_stripes(who, stripes, grad, sems):
    copies = stripe_copies(who, stripes, grad, sems)
    for copy in copies:
        copy.start()
    for copy in copies:
        copy.wait()


def staying_kernel(
    ready, place, left_own, left_near, right_own, right_near, grad, stripes, sems
):
    ready()
    parts, width, _ = stripes.shape
    left = both_rows(left_own, left_near, aligned(place[OWN] * width, width)).T

    def step(j, carry):
        right = both_rows(right_own, right_near, aligned(j * 256, 256))
        put_stripe(parts, stripes, j, matmul(left, right))
        return carry

    lax.fori_loop(0, right_own.shape[1] // 256, step, 0)
    write_stripes(place[SIDE], stripes, grad, sems)


def staying_gradient(parts, place, left_own, left_near, right_own, right_near):
    width, wide = D // 4, right_own.shape[1]
    return kernel_call(
        staying_kernel,
        "staying_gradient",
        [(SMEM, place)] + in_stage(left_own, left_near, right_own, right_near),
        [((width, 2 * wide), F32, HBM)],
        [pltpu.VMEM((parts, width, wide // parts), F32), pltpu.SemaphoreType.DMA((parts,))],
    )[0]


def coming_kernel(ready, place, come, before, grad, stripes, sems):
    ready()
    parts, _, part = stripes.shape
    copies = stripe_copies(1 - place[SIDE], stripes, grad, sems)
    for k, copy in enumerate(copies):
        for j in range(come.shape[1] // 256):
            if parts == 2:
                at = j * 256 + k * 128
                stripes[k, :, j * 128 : (j + 1) * 128] = come[:, at : at + 128].astype(F32)
            elif j // 2 == k:
                at = slice((j % 2) * 256, (j % 2) * 256 + 256)
                stripes[k, :, at] = come[:, j * 256 : (j + 1) * 256].astype(F32)
        copy.start()
    for copy in copies:
        copy.wait()


def with_coming(parts, place, come, grad):
    width, wide = come.shape
    return kernel_call(
        coming_kernel,
        "coming_gradient",
        [(SMEM, place), (MOVED, come), (HBM, grad)],
        [(grad.shape, F32, HBM)],
        [pltpu.VMEM((parts, width, wide // parts), F32), pltpu.SemaphoreType.DMA((parts,))],
        aliases=((2, 0),),
    )[0]


def grad_out_kernel(ready, place, mixed_own, mixed_near, d_own, d_near, grad):
    ready()
    left = both_rows(
        mixed_own, mixed_near, aligned(place[CORE] * grad.shape[0], grad.shape[0])
    )
    for base in range(0, D, 512):
        at = slice(base, base + 512)
        grad[:, at] = inner_rows(left, jnp.concatenate([d_own[:, at], d_near[:, at]], 0))


def grad_out_rows(place, mixed_own, mixed_near, d_own, d_near):
    width = mixed_own.shape[1] // 2
    return kernel_call(
        grad_out_kernel,
        "grad_out",
        [(SMEM, place)] + in_stage(mixed_own, mixed_near, d_own, d_near),
        [((width, D), F32)],
    )[0]


def grad_down_kernel(ready, place, h_own, h_near, ca_own, cb_own, ca_near, cb_near, grad, wide):
    ready()
    count, window = grad.shape[0], wide.shape[0]
    core = place[CORE]
    skip = h_own.shape[1] - window
    left = both_rows(h_own, h_near, aligned(core * skip, window))

    def step(n, carry):
        columns = aligned(n * 256, 256)
        right = jnp.concatenate(
            [ref[:, columns] for ref in (ca_own, cb_own, ca_near, cb_near)], 0
        )
        wide[:, columns] = inner_rows(left, right)
        return carry

    lax.fori_loop(0, D // 256, step, 0)
    grad[...] = wide[aligned(core * (count - skip), count, 64), :]


def grad_down_rows(place, h_own, h_near, ca_own, cb_own, ca_near, cb_near):
    count = h_own.shape[1] // 2
    window = -(-count // 128) * 128
    return kernel_call(
        grad_down_kernel,
        "grad_down",
        [(SMEM, place)] + moved(h_own, h_near, ca_own, cb_own, ca_near, cb_near),
        [((count, D), F32)],
        [pltpu.VMEM((window, D), F32)],
    )[0]


def side_columns(weight, half, side, sems):
    part = half.shape[1] // 3
    return [
        pltpu.make_async_copy(
            weight.at[:, aligned((2 * k + side) * part, part)],
            half.at[:, pl.ds(k * part, part)],
            sems.at[k],
        )
        for k in range(3)
    ]


def kept_columns_kernel(ready, place, weight, half, sems):
    copies = side_columns(weight, half, place[SIDE], sems)
    for copy in copies:
        copy.start()
    for copy in copies:
        copy.wait()


def kept_columns(place, weight):
    count, width = weight.shape
    return kernel_call(
        kept_columns_kernel,
        "kept_columns",
        [(SMEM, place), (HBM, weight)],
        [((count, width // 2), BF16)],
        [pltpu.SemaphoreType.DMA((3,))],
    )[0]


def spread_kernel(split, ready, place, weight, kept, leaving_a, leaving_b, sems):
    part = weight.shape[1] // 4
    side = place[SIDE]
    copies = []
    for k in range(2):
        for j in range(part // 128):
            leaving, at = (leaving_a, j) if j < split else (leaving_b, j - split)
            for who, target, spot in ((side, kept, j), (1 - side, leaving, at)):
                copies.append(
                    pltpu.make_async_copy(
                        weight.at[:, aligned((2 * k + who) * part + j * 128, 128)],
                        target.at[:, pl.ds(spot * 256 + k * 128, 128)],
                        sems.at[len(copies)],
                    )
                )
    for copy in copies:
        copy.start()
    for copy in copies:
        copy.wait()


def spread(place, weight, split):
    count, width = weight.shape
    return kernel_call(
        functools.partial(spread_kernel, split),
        "spread",
        [(SMEM, place), (HBM, weight)],
        [((count, size), BF16) for size in (width // 2, 256 * split, width // 2 - 256 * split)],
        [pltpu.SemaphoreType.DMA((width // 128,))],
    )


def sync(*values):
    return lax.optimization_barrier(values)


def after(value, *earlier):
    return lax.optimization_barrier((value,) + earlier)[0]


def pair_body(frames_in, segment_ids, gain_attn, w_qkv, w_out, gain_ffn, w_gate_up, w_down, cotangent):
    member = lax.axis_index("fsdp") % 4
    side, core = member >> 1, member & 1
    position = lax.axis_index("fsdp") // 4
    place = jnp.stack([member, member ^ 2, member ^ 1, member ^ 3, side, core, position])
    place = place.astype(jnp.int32)
    frames = frames_in.shape[0] // POS
    half = POS * frames

    near = lambda rows: swap(rows, 1)

    x_sent, c_sent, qkv_leaving = to_positions(place, frames_in, cotangent, w_qkv)
    qkv_across = swap(qkv_leaving, 3)
    qkv_far = near(qkv_across)
    x_came = exchange(x_sent)
    ids_own = segment_ids.reshape(frames, POS).T
    ids_own = jnp.take(ids_own, jnp.arange(POS) ^ position, axis=0).reshape(1, half)
    gains_own = jnp.stack([gain_attn, gain_ffn])
    gains_near = near(after(gains_own, qkv_leaving))
    qkv_kept = kept_columns(place, after(w_qkv, qkv_leaving))
    w_kept, leaving_a, leaving_b = spread(place, after(w_gate_up, qkv_leaving), 3)
    x_came, ids_own, gains_near, qkv_kept, w_kept, leaving_a, leaving_b = sync(
        x_came, ids_own, gains_near, qkv_kept, w_kept, leaving_a, leaving_b
    )

    x_own = collect(place, x_came, ids_own, gains_own, gains_near)
    x_far = near(swap(x_own, 3))
    qkv_near = near(qkv_kept)
    c_came = exchange([after(c_sent[0], x_own)])
    across_a = swap(after(leaving_a, x_own), 3)
    x_far, qkv_far, qkv_near, leaving_b = sync(x_far, qkv_far, qkv_near, leaving_b)

    across_b = swap(leaving_b, 3)
    qkv_sent, lowered_first, table = first(
        place, x_own, x_far, w_qkv, qkv_far, qkv_near, qkv_across
    )
    qkv_sent, c_came, across_a = sync(qkv_sent, c_came, across_a)
    c_own = collect_rows(place, c_came)
    out_near, down_near = (near(after(a, lowered_first)) for a in (w_out, w_down))
    qkv, out_near, down_near, c_own = sync(exchange(qkv_sent), out_near, down_near, c_own)

    mixed_sent = attend_local(place, table, qkv)
    c_far = swap(after(c_own, mixed_sent[0]), 2)
    c_own_near, lowered_first_near = (
        near(after(a, mixed_sent[0])) for a in (c_own, lowered_first)
    )
    mixed, across_b, c_far, c_own_near, lowered_first_near = sync(
        exchange(mixed_sent), across_b, c_far, c_own_near, lowered_first_near
    )

    term, leaving, mixed = out_term(place, mixed, w_out, out_near)
    far = swap(leaving, 2)
    base, d_hidden = aside(
        place, x_own, x_far, term, c_own, after(c_far, leaving), w_down, down_near
    )
    mixed_near, far_a, far_b, w_near, c_far_near = (
        near(after(a, leaving)) for a in (mixed, across_a, across_b, w_kept, c_far)
    )
    far, base, d_hidden, mixed_near, far_a, far_b, w_near, c_far_near = sync(
        far, base, d_hidden, mixed_near, far_a, far_b, w_near, c_far_near
    )
    resid, lowered_second, hidden, d_gate_up, second, leaving = ffn(
        place, base, far, table, d_hidden, (w_kept, w_near, far_a, across_a, far_b, across_b)
    )

    second_far = swap(leaving, 2)
    hidden_near, lowered_second_near, d_gate_up_near = (
        near(after(rows, leaving)) for rows in (hidden, lowered_second, d_gate_up)
    )
    down_kept, down_leaving = down_term(place, after(hidden, leaving), resid, w_down, down_near)
    sides = (lowered_second, lowered_second_near, d_gate_up, d_gate_up_near)
    gate_up_leaving = leaving_gradient(place, ACROSS, *sides)
    second_far, down_leaving, gate_up_leaving, hidden_near, lowered_second_near = sync(
        second_far, down_leaving, gate_up_leaving, hidden_near, lowered_second_near
    )

    gate_up_come = swap(gate_up_leaving, 3)
    d_resid, d_branch, gain_ffn_terms, d_mixed = mid(
        place, second, second_far, resid, table, c_own, c_far, w_out, out_near
    )
    d_branch_near, gain_ffn_near = near(d_branch), near(gain_ffn_terms[1])
    grad_gate_up = staying_gradient(2, place, after(lowered_second, d_branch), *sides[1:])
    d_mixed, d_branch_near, gain_ffn_near, grad_gate_up = sync(
        exchange(d_mixed), d_branch_near, gain_ffn_near, grad_gate_up
    )

    d_qkv_sent = attend_back_local(place, table, qkv, d_mixed)
    grad_down = grad_down_rows(
        place, after(hidden, d_qkv_sent[0]), hidden_near, c_own, c_far, c_own_near, c_far_near
    )
    grad_out = grad_out_rows(place, mixed, mixed_near, after(d_branch, d_qkv_sent[0]), d_branch_near)
    down_far = swap(after(down_leaving, d_qkv_sent[0]), 2)
    d_qkv, gate_up_come, down_far, grad_down, grad_out = sync(
        exchange(d_qkv_sent), gate_up_come, down_far, grad_down, grad_out
    )

    kept, leaving, d_projected = back_first(
        place, d_qkv, w_qkv, qkv_far, qkv_near, qkv_across
    )
    first_far = swap(leaving, 2)
    qkv_sides = (lowered_first, lowered_first_near, d_projected, near(d_projected))
    first_far, qkv_leaving = sync(first_far, leaving_gradient(place, FAR, *qkv_sides))
    qkv_across_come = swap(qkv_leaving, 3)

    out_sent, gain_attn_terms = last(
        place, kept, first_far, x_own, table, d_resid, down_kept, down_far
    )
    grad_gate_up = with_coming(2, place, after(gate_up_come, gain_attn_terms), grad_gate_up)
    grad_qkv = staying_gradient(3, place, after(lowered_first, gain_attn_terms), *qkv_sides[1:])
    gain_sums = gain_attn_terms[:2] + swap(gain_attn_terms[2:], 2)
    gain_attn_grad = gain_sums[0] + near(gain_sums[1])
    qkv_come = near(after(qkv_across_come, grad_gate_up, grad_qkv))
    grad_qkv = with_coming(3, place, qkv_come, grad_qkv)
    out_come, grad_gate_up, grad_qkv = sync(exchange(out_sent), grad_gate_up, grad_qkv)
    grad_in, block_out = to_frames(place, out_come)
    gain_ffn_grad = (gain_ffn_terms[0] + gain_ffn_near).reshape(-1)
    return (
        block_out,
        grad_in,
        gain_attn_grad.reshape(-1),
        grad_qkv,
        grad_out,
        gain_ffn_grad,
        grad_gate_up,
        grad_down,
    )


def solution(mesh):
    in_specs = (
        P("fsdp", None),
        P("fsdp"),
        P("fsdp"),
        P("fsdp", None),
        P("fsdp", None),
        P("fsdp"),
        P("fsdp", None),
        P("fsdp", None),
        P("fsdp", None),
    )
    out_specs = (
        P("fsdp", None),
        P("fsdp", None),
        P("fsdp"),
        P("fsdp", None),
        P("fsdp", None),
        P("fsdp"),
        P("fsdp", None),
        P("fsdp", None),
    )
    chosen = pair_body if mesh.shape["fsdp"] == 4 * POS else body
    return jax.shard_map(chosen, mesh=mesh, in_specs=in_specs, out_specs=out_specs, check_vma=False)
```

```python
import functools
import math

import jax
import jax.numpy as jnp
from jax import lax
from jax.experimental import pallas as pl
from jax.experimental.pallas import tpu as pltpu
from jax.sharding import PartitionSpec as P

D = 1024
FF = 2816
HEADS = 16
HEAD_DIM = 64
POS = 8


EPSILON = 1e-05


def for_sending(array):

    def short(part):
        return part.astype(jnp.bfloat16) if part.dtype == jnp.float32 else part

    return jax.tree.map(short, array)


def swapped(block, axis, stride):
    count = lax.axis_size(axis)
    route = []
    for low in range(count):
        high = low | 1 << stride
        if high != low and high < count:
            route += [(low, high), (high, low)]
    return lax.ppermute(block, axis, route)


def positions_layout(frame_rows, groups):
    width = frame_rows.shape[-1]
    per_piece = frame_rows.shape[0] // POS // groups
    shaped = frame_rows.reshape(groups, per_piece, POS, width).transpose(2, 0, 1, 3)
    return shaped.reshape(POS * groups, per_piece, width)


def frames_layout(piece_rows, groups):
    width = piece_rows.shape[-1]
    per_piece = piece_rows.shape[1]
    shaped = piece_rows.reshape(POS, groups, per_piece, width).transpose(1, 2, 0, 3)
    return shaped.reshape(groups * per_piece * POS, width)


def inner_rows(left, right):
    return lax.dot_general(
        left, right, (((0,), (0,)), ((), ())), preferred_element_type=jnp.float32
    )


def times_transposed(left, right):
    return lax.dot_general(
        left, right, (((1,), (1,)), ((), ())), preferred_element_type=jnp.float32
    )


def join_pieces(current, partner, member, bit_level):
    upper_half = member >> bit_level & 1 == 1
    return tuple(
        (
            jnp.where(
                upper_half,
                jnp.concatenate([theirs, own_piece], 0),
                jnp.concatenate([own_piece, theirs], 0),
            )
            for own_piece, theirs in zip(current, partner)
        )
    )


def collect_forward(pieces, member, levels):
    current = pieces
    for bit_level in range(levels):
        partner = jax.tree.map(
            lambda part, own: part.astype(own.dtype),
            swapped(for_sending(current), "fsdp", bit_level),
            current,
        )
        current = join_pieces(current, partner, member, bit_level)
    return current


def collect_again(pieces, member, levels):
    current = pieces
    for bit_level in range(levels):
        partner = jax.tree.map(
            lambda part, own: part.astype(own.dtype),
            swapped(for_sending(current), "fsdp", bit_level),
            current,
        )
        current = join_pieces(current, partner, member, bit_level)
    return current


def halving_sum(terms, member, levels, sender):
    current = terms
    for bit_level in reversed(range(levels)):
        upper_half = member >> bit_level & 1 == 1
        leaving = tuple(
            (
                jnp.where(
                    upper_half,
                    term_part[: term_part.shape[0] // 2],
                    term_part[term_part.shape[0] // 2 :],
                )
                for term_part in current
            )
        )
        staying = tuple(
            (
                jnp.where(
                    upper_half,
                    term_part[term_part.shape[0] // 2 :],
                    term_part[: term_part.shape[0] // 2],
                )
                for term_part in current
            )
        )
        arrived = sender(leaving, bit_level)
        current = tuple((held_part + come_part for held_part, come_part in zip(staying, arrived)))
    return current


def send_whole(parts, bit_level):
    return jax.tree.map(
        lambda part, own: part.astype(own.dtype),
        swapped(for_sending(parts), "fsdp", bit_level),
        parts,
    )


def permitted(validity):
    row_place = lax.broadcasted_iota(jnp.int32, (POS, POS), 0)
    column_place = lax.broadcasted_iota(jnp.int32, (POS, POS), 1)
    causal = column_place <= row_place
    same_segment = validity[:, :, None] == validity[:, None, :]
    return (causal[None] & same_segment)[:, None]


def split_projections(qkv_frames):
    frames = qkv_frames.shape[0] // POS
    shaped = qkv_frames.reshape(frames, POS, 3, HEADS, HEAD_DIM)
    return (shaped[:, :, 0], shaped[:, :, 1], shaped[:, :, 2])


def masked_scores(queries, key_rows, allowed):
    scores = jnp.einsum(
        "fqhd,fkhd->fhqk", queries, key_rows, preferred_element_type=jnp.float32
    ) * HEAD_DIM ** (-0.5)
    return jnp.where(allowed, scores, -jnp.inf)


def attend(qkv_frames, validity):
    queries, key_rows, value_rows = split_projections(qkv_frames)
    scores = masked_scores(queries, key_rows, permitted(validity))
    highest = jnp.max(scores, axis=-1, keepdims=True)
    raised = jnp.exp(scores - highest)
    totals = jnp.sum(raised, axis=-1, keepdims=True)
    attn_probs = (raised / totals).astype(jnp.bfloat16)
    attended = jnp.einsum(
        "fhqk,fkhd->fqhd", attn_probs, value_rows, preferred_element_type=jnp.float32
    )
    mixed_heads = attended.reshape(qkv_frames.shape[0], D).astype(jnp.bfloat16)
    return (mixed_heads, highest + jnp.log(totals))


def attend_back(qkv_frames, validity, log_total, d_mixed):
    queries, key_rows, value_rows = split_projections(qkv_frames)
    frames = queries.shape[0]
    scores = masked_scores(queries, key_rows, permitted(validity))
    weights_full = jnp.exp(scores - log_total)
    attn_probs = weights_full.astype(jnp.bfloat16)
    d_heads = d_mixed.reshape(frames, POS, HEADS, HEAD_DIM)
    d_probs = jnp.einsum("fqhd,fkhd->fhqk", d_heads, value_rows, preferred_element_type=jnp.float32)
    d_values = jnp.einsum(
        "fhqk,fqhd->fkhd", attn_probs, d_heads, preferred_element_type=jnp.float32
    )
    d_scores = weights_full * (d_probs - jnp.sum(d_probs * weights_full, axis=-1, keepdims=True))
    d_scores = d_scores.astype(jnp.bfloat16)
    d_queries = jnp.einsum(
        "fhqk,fkhd->fqhd", d_scores, key_rows, preferred_element_type=jnp.float32
    ) * HEAD_DIM ** (-0.5)
    d_keys = jnp.einsum(
        "fhqk,fqhd->fkhd", d_scores, queries, preferred_element_type=jnp.float32
    ) * HEAD_DIM ** (-0.5)
    stacked = jnp.stack([d_queries, d_keys, d_values], axis=2)
    return stacked.reshape(frames * POS, 3 * D).astype(jnp.bfloat16)


def body(frames_in, segment_ids, gain_attn, w_qkv, w_out, gain_ffn, w_gate_up, w_down, cotangent):
    devices = lax.axis_size("fsdp")
    groups = devices // POS
    levels = groups.bit_length() - 1
    member = lax.axis_index("fsdp") % groups
    per_piece = frames_in.shape[0] // POS // groups
    validity = segment_ids.reshape(-1, POS)
    moved_input, moved_cotangent = (
        lax.all_to_all(
            positions_layout(frames_in, groups), "fsdp", split_axis=0, concat_axis=0, tiled=True
        ),
        lax.all_to_all(
            positions_layout(cotangent, groups), "fsdp", split_axis=0, concat_axis=0, tiled=True
        ),
    )
    inputs = moved_input.reshape(-1, D).astype(jnp.float32)
    upstream = moved_cotangent.reshape(-1, D)
    own_pieces = (w_qkv, w_out, w_gate_up, w_down, gain_attn, gain_ffn)
    collected = collect_forward(own_pieces, member, levels)
    whole_qkv, whole_out, whole_gate_up, whole_down, whole_gain_attn, whole_gain_ffn = collected
    gain_first = whole_gain_attn.astype(jnp.float32)
    gain_second = whole_gain_ffn.astype(jnp.float32)
    scale_first = lax.rsqrt(jnp.mean(inputs * inputs, axis=-1, keepdims=True) + EPSILON)
    normed_first = inputs * scale_first
    lowered_first = (normed_first * gain_first).astype(jnp.bfloat16)
    projected = jnp.dot(lowered_first, whole_qkv, preferred_element_type=jnp.float32).astype(
        jnp.bfloat16
    )
    qkv_frames = frames_layout(
        lax.all_to_all(
            projected.reshape(devices, per_piece, 3 * D),
            "fsdp",
            split_axis=0,
            concat_axis=0,
            tiled=True,
        ),
        groups,
    )
    mixed_frames, log_total = attend(qkv_frames, validity)
    mixed_rows = lax.all_to_all(
        positions_layout(mixed_frames, groups), "fsdp", split_axis=0, concat_axis=0, tiled=True
    ).reshape(-1, D)
    residual = inputs + jnp.dot(mixed_rows, whole_out, preferred_element_type=jnp.float32)
    scale_second = lax.rsqrt(jnp.mean(residual * residual, axis=-1, keepdims=True) + EPSILON)
    normed_second = residual * scale_second
    lowered_second = (normed_second * gain_second).astype(jnp.bfloat16)
    gate_up = jnp.dot(lowered_second, whole_gate_up, preferred_element_type=jnp.float32)
    gate_part = gate_up[:, :FF]
    up_part = gate_up[:, FF:]
    sigmoid_gate = jax.nn.sigmoid(gate_part)
    activated = gate_part * sigmoid_gate
    hidden = (activated * up_part).astype(jnp.bfloat16)
    result_rows = (
        residual + jnp.dot(hidden, whole_down, preferred_element_type=jnp.float32)
    ).astype(jnp.bfloat16)
    block_out = frames_layout(
        lax.all_to_all(
            result_rows.reshape(devices, per_piece, D),
            "fsdp",
            split_axis=0,
            concat_axis=0,
            tiled=True,
        ),
        groups,
    )
    collected = collect_again(own_pieces, member, levels)
    whole_qkv, whole_out, whole_gate_up, whole_down, whole_gain_attn, whole_gain_ffn = collected
    gain_first = whole_gain_attn.astype(jnp.float32)
    gain_second = whole_gain_ffn.astype(jnp.float32)
    grad_down_term = inner_rows(hidden, upstream)
    d_hidden = times_transposed(upstream, whole_down)
    d_gate = d_hidden * up_part * sigmoid_gate * (1.0 + gate_part * (1.0 - sigmoid_gate))
    d_up = d_hidden * activated
    d_gate_up = jnp.concatenate([d_gate, d_up], axis=1).astype(jnp.bfloat16)
    grad_gate_up_term = inner_rows(lowered_second, d_gate_up)
    d_second = times_transposed(d_gate_up, whole_gate_up)
    grad_gain_ffn_term = jnp.sum(d_second * normed_second, axis=0)
    scaled_second = d_second * gain_second
    d_residual = upstream.astype(jnp.float32) + scale_second * (
        scaled_second
        - normed_second * jnp.mean(scaled_second * normed_second, axis=-1, keepdims=True)
    )
    d_branch = d_residual.astype(jnp.bfloat16)
    grad_out_term = inner_rows(mixed_rows, d_branch)
    d_mixed = times_transposed(d_branch, whole_out).astype(jnp.bfloat16)
    d_mixed_frames = frames_layout(
        lax.all_to_all(
            d_mixed.reshape(devices, per_piece, D), "fsdp", split_axis=0, concat_axis=0, tiled=True
        ),
        groups,
    )
    d_qkv_frames = attend_back(qkv_frames, validity, log_total, d_mixed_frames)
    d_projected = lax.all_to_all(
        positions_layout(d_qkv_frames, groups), "fsdp", split_axis=0, concat_axis=0, tiled=True
    ).reshape(-1, 3 * D)
    grad_qkv_term = inner_rows(lowered_first, d_projected)
    d_first = times_transposed(d_projected, whole_qkv)
    grad_gain_attn_term = jnp.sum(d_first * normed_first, axis=0)
    scaled_first = d_first * gain_first
    d_inputs = d_residual + scale_first * (
        scaled_first - normed_first * jnp.mean(scaled_first * normed_first, axis=-1, keepdims=True)
    )
    grad_in = frames_layout(
        lax.all_to_all(
            d_inputs.reshape(devices, per_piece, D).astype(jnp.bfloat16),
            "fsdp",
            split_axis=0,
            concat_axis=0,
            tiled=True,
        ).astype(jnp.float32),
        groups,
    )
    shares = halving_sum(
        (
            grad_qkv_term,
            grad_out_term,
            grad_gate_up_term,
            grad_down_term,
            grad_gain_attn_term,
            grad_gain_ffn_term,
        ),
        member,
        levels,
        send_whole,
    )
    return (block_out, grad_in, shares[4], shares[0], shares[1], shares[5], shares[2], shares[3])

VMEM = pl.BlockSpec(memory_space=pltpu.VMEM)
SMEM = pl.BlockSpec(memory_space=pltpu.SMEM)
HBM = pl.BlockSpec(memory_space=pltpu.HBM)
STAGED = pl.BlockSpec(memory_space=pltpu.HBM)
MOVED = pl.BlockSpec(memory_space=pl.ANY)
EITHER = pl.BlockSpec(memory_space=pl.ANY)
BF16 = jnp.bfloat16
F32 = jnp.float32
OWN, FAR, NEAR, ACROSS, SIDE, CORE, POSITION = range(7)
TAIL = 16


def swap(block, mask):
    count = lax.axis_size("fsdp")
    return lax.ppermute(block, "fsdp", [(i, i ^ mask) for i in range(count)])


def exchange(blocks):
    count = lax.axis_size("fsdp")
    stride = count // POS
    if len(blocks) == POS:
        return [blocks[0]] + [swap(blocks[k], stride * k) for k in range(1, POS)]
    lanes = [[r + stride * k for k in range(POS)] for r in range(stride)]
    return [
        lax.all_to_all(
            blocks[0], "fsdp", split_axis=0, concat_axis=0, tiled=True, axis_index_groups=lanes
        )
    ]


def kernel_call(kernel, name, args, outs, scratch=(), aliases=()):
    flat = lambda items: [p for item in items for p in (item if isinstance(item, list) else [item])]
    staged = [n for n, (spec, _) in enumerate(flat(args)) if spec is STAGED or spec is MOVED]
    arrays = [
        pltpu.with_memory_space_constraint(a, pltpu.HBM) if spec is STAGED or spec is HBM else a
        for spec, a in flat(args)
    ]
    scratch = list(scratch)
    own = len(scratch)
    scratch += [pltpu.VMEM(arrays[n].shape, arrays[n].dtype) for n in staged]
    scratch += [pltpu.SemaphoreType.DMA((max(len(staged), 1),))]
    held = sum(
        math.prod(ref.shape) * jnp.dtype(ref.dtype).itemsize
        for ref in scratch
        if ref.memory_space == pltpu.VMEM
    )

    def grouped(items, values):
        return [
            [next(values) for _ in item] if isinstance(item, list) else next(values)
            for item in items
        ]

    def body_kernel(*refs):
        inputs, outputs = list(refs[: len(arrays)]), refs[len(arrays) :]
        outputs, extra = outputs[: len(flat(outs))], outputs[len(flat(outs)) :]
        extra, landing, sems = extra[:own], extra[own:-1], extra[-1]
        copies = []
        for k, n in enumerate(staged):
            copies.append(pltpu.make_async_copy(inputs[n], landing[k], sems.at[k]))
            inputs[n] = landing[k]
        for copy in copies:
            copy.start()

        def ready():
            for copy in copies:
                copy.wait()

        kernel(ready, *grouped(args, iter(inputs)), *grouped(outs, iter(outputs)), *extra)

    result = pl.pallas_call(
        body_kernel,
        name=name,
        in_specs=[spec for spec, _ in flat(args)],
        out_specs=[spec[0] if spec else VMEM for _, _, *spec in flat(outs)],
        out_shape=[
            pltpu.HBM(s, d) if spec else jax.ShapeDtypeStruct(s, d) for s, d, *spec in flat(outs)
        ],
        input_output_aliases=dict(aliases),
        scratch_shapes=scratch,
        cost_estimate=pl.CostEstimate(flops=1, bytes_accessed=1, transcendentals=0),
        compiler_params=pltpu.CompilerParams(vmem_limit_bytes=held + (8 << 20)),
    )(*arrays)
    return grouped(outs, iter(result))


def views(blocks, place):
    if len(blocks) == POS:
        return blocks
    return [blocks[0].at[place[POSITION] ^ k] for k in range(POS)]


def matmul(left, right):
    return jnp.dot(left, right, preferred_element_type=F32)


def aligned(start, size, step=128):
    return pl.ds(pl.multiple_of(start, step), size)


def rows_of(refs, rel, columns=slice(None)):
    frames = refs[0].shape[0] // 2
    return jnp.concatenate([ref[rel * frames : (rel + 1) * frames, columns] for ref in refs], 0)


def put_rows(refs, rel, columns, value):
    frames = refs[0].shape[0] // 2
    for k, ref in enumerate(refs):
        ref[rel * frames : (rel + 1) * frames, columns] = value[k * frames : (k + 1) * frames]


def block_shapes(rows, width, joined):
    if joined:
        return [((POS, rows // POS, width), BF16)]
    return [((rows // POS, width), BF16)] * POS


def in_vmem(*arrays):
    return [(VMEM, a) for a in arrays]


def in_stage(*arrays):
    return [(STAGED, a) for a in arrays]


def moved(*arrays):
    return [(MOVED, a) for a in arrays]


def place_matrix(size, to_positions, position):
    frames = size // POS
    row = lax.broadcasted_iota(jnp.int32, (size, size), 0)
    column = lax.broadcasted_iota(jnp.int32, (size, size), 1)
    if not to_positions:
        row, column = column, row
    return (column == (row % frames) * POS + ((row // frames) ^ position)).astype(F32).astype(BF16)


def to_positions_kernel(ready, place, x_rows, c_rows, weight, x_blocks, c_blocks, half, sems):
    copies = side_columns(weight, half, 1 - place[SIDE], sems)
    for copy in copies:
        copy.start()
    order = place_matrix(x_rows.shape[0], True, place[POSITION])
    ready()
    for rows, blocks in ((x_rows, x_blocks), (c_rows, c_blocks)):
        moved_rows = matmul(order, rows[...]).astype(BF16)
        count = rows.shape[0] // POS
        for k, block in enumerate(views(blocks, place)):
            block[...] = moved_rows[k * count : (k + 1) * count]
    for copy in copies:
        copy.wait()


def to_positions(place, x_rows, c_rows, weight):
    size, width = x_rows.shape
    return kernel_call(
        to_positions_kernel,
        "to_positions",
        [(SMEM, place)] + in_stage(x_rows, c_rows) + [(HBM, weight)],
        [block_shapes(size, width, True), block_shapes(size, width, True),
         ((weight.shape[0], weight.shape[1] // 2), BF16)],
        [pltpu.SemaphoreType.DMA((3,))],
    )


def joined(blocks, place):
    return jnp.concatenate([block[...] for block in views(blocks, place)], 0)


def collect_rows_kernel(ready, place, blocks, rows):
    ready()
    rows[...] = joined(blocks, place)


def collect_rows(place, blocks):
    count, width = blocks[0].shape[-2:]
    return kernel_call(
        collect_rows_kernel,
        "collect_rows",
        [(SMEM, place), in_vmem(*blocks)],
        [((count * POS, width), BF16)],
    )[0]


def collect_kernel(ready, place, blocks, ids, gains_own, gains_near, x_own):
    ready()
    half = x_own.shape[0] - TAIL
    x_own[:half, :] = joined(blocks, place)
    padded = lambda *parts: jnp.concatenate(
        parts + (jnp.zeros((1, D - sum(p.shape[1] for p in parts)), F32),), 1
    )
    row = lax.broadcasted_iota(jnp.int32, (TAIL, D), 0)
    tail = jnp.where(row == 2, padded(ids[...].astype(F32)), 0.0)
    for k in range(2):
        gain = padded(gains_own[k : k + 1, :].astype(F32), gains_near[k : k + 1, :].astype(F32))
        tail = jnp.where(row == k, gain, tail)
    x_own[half:, :] = tail.astype(BF16)


def collect(place, blocks, ids, gains_own, gains_near):
    count, width = blocks[0].shape[-2:]
    return kernel_call(
        collect_kernel,
        "collect",
        [(SMEM, place), in_vmem(*blocks)] + in_vmem(ids, gains_own, gains_near),
        [((count * POS + TAIL, width), BF16)],
    )[0]


def to_frames_kernel(ready, place, blocks, *rows):
    ready()
    blocks = views(blocks, place)
    order = place_matrix(rows[0].shape[0], False, place[POSITION])
    for rel in range(2):
        rows[rel][...] = matmul(order, rows_of(blocks, rel)).astype(rows[rel].dtype)


def to_frames(place, blocks):
    size = blocks[0].shape[-2] * POS // 2
    return kernel_call(
        to_frames_kernel,
        "to_frames",
        [(SMEM, place), in_vmem(*blocks)],
        [((size, D), F32), ((size, D), BF16)],
    )


def first_kernel(
    ready, place, x_a, x_b, w_own, w_far, w_near, w_across, qkv, lowered_out, table_out,
    lowered, table, w, sems,
):
    qkv = views(qkv, place)
    half, width = lowered.shape[0] // 2, w_own.shape[0]
    part = w.shape[1] // 3
    side = place[SIDE]
    at_rows = lambda rank: aligned(place[rank] * width, width)
    copies = [
        pltpu.make_async_copy(
            w_own.at[:, aligned((2 * k + side) * part, part)],
            w.at[at_rows(OWN), pl.ds(k * part, part)],
            sems.at[k],
        )
        for k in range(3)
    ]
    copies.append(pltpu.make_async_copy(w_far, w.at[at_rows(FAR)], sems.at[3]))
    copies.append(pltpu.make_async_copy(w_near, w.at[at_rows(NEAR)], sems.at[4]))
    copies.append(pltpu.make_async_copy(w_across, w.at[at_rows(ACROSS)], sems.at[5]))
    for copy in copies:
        copy.start()
    ready()
    table[...] = jnp.zeros_like(table)
    for k, (ref, ranks) in enumerate(((x_a, (OWN, NEAR)), (x_b, (FAR, ACROSS)))):
        tail = ref[half:, :].astype(F32)
        for n, rank in enumerate(ranks):
            table[0:2, at_rows(rank)] = tail[0:2, n * width : (n + 1) * width]
        table[2 + k : 3 + k, 0:half] = tail[2:3, 0:half]
    gain = table[0:1, :]
    for rel, ref in enumerate((x_a, x_b)):
        rows = ref[:half, :].astype(F32)
        scale = lax.rsqrt(jnp.mean(rows * rows, axis=-1, keepdims=True) + EPSILON)
        lowered[rel * half : (rel + 1) * half, :] = (rows * scale * gain).astype(BF16)
    leaving = [
        pltpu.make_async_copy(lowered, lowered_out, sems.at[6]),
        pltpu.make_async_copy(table, table_out, sems.at[7]),
    ]
    for copy in leaving:
        copy.start()
    for copy in copies:
        copy.wait()

    def step(n, carry):
        columns = aligned(n * 256, 256, 256)
        value = matmul(lowered[...], w[:, columns]).astype(BF16)
        put_rows(qkv, 0, columns, value[:half])
        put_rows(qkv, 1, columns, value[half:])
        return carry

    lax.fori_loop(0, w.shape[1] // 256, step, 0)
    for copy in leaving:
        copy.wait()


def first(place, x_a, x_b, w_own, w_far, w_near, w_across):
    half = x_a.shape[0] - TAIL
    wide = w_far.shape[1]
    return kernel_call(
        first_kernel,
        "first",
        [(SMEM, place), (MOVED, x_a), (MOVED, x_b), (HBM, w_own), (EITHER, w_far),
         (EITHER, w_near), (EITHER, w_across)],
        [block_shapes(2 * half, wide, True), ((2 * half, D), BF16, HBM), ((8, D), F32, HBM)],
        [pltpu.VMEM((2 * half, D), BF16), pltpu.VMEM((8, D), F32), pltpu.VMEM((D, wide), BF16),
         pltpu.SemaphoreType.DMA((8,))],
    )


def allowed_pairs(ids, position):
    size = ids.shape[1]
    frames = size // POS
    row = lax.broadcasted_iota(jnp.int32, (size, size), 0)
    column = lax.broadcasted_iota(jnp.int32, (size, size), 1)
    across = jnp.broadcast_to(ids, (size, size))
    same = (across == across.T) & (row % frames == column % frames)
    mask = same & ((column // frames) ^ position <= (row // frames) ^ position)
    return jnp.concatenate([mask, mask], 1)


def pair_of_heads(rows, low):
    return jnp.concatenate([rows * low, rows * (1 - low)], 0)


def lane_halves(value, reduce):
    size = value.shape[1] // 2
    parts = [
        jnp.broadcast_to(reduce(value[:, k * size : (k + 1) * size]), (value.shape[0], size))
        for k in range(2)
    ]
    return jnp.concatenate(parts, 1)


def pair_probs(query, key_pair, mask):
    scores = times_transposed(query, key_pair) * HEAD_DIM ** (-0.5)
    scores = jnp.where(mask, scores, -jnp.inf)
    raised = jnp.exp(scores - lane_halves(scores, lambda a: jnp.max(a, -1, keepdims=True)))
    return raised / lane_halves(raised, lambda a: jnp.sum(a, -1, keepdims=True))


def first_head_lanes():
    lane = lax.broadcasted_iota(jnp.int32, (1, 2 * HEAD_DIM), 1)
    return (lane < HEAD_DIM).astype(F32).astype(BF16)


def attend_kernel(ready, place, table, qkv, mixed):
    qkv, mixed = views(qkv, place), views(mixed, place)
    size = POS * mixed[0].shape[0] // 2
    part = mixed[0].shape[1]
    low = first_head_lanes()
    ready()
    for rel in range(2):
        mask = allowed_pairs(table[2 + rel : 3 + rel, 0:size], place[POSITION])
        for base in range(0, part, 2 * HEAD_DIM):
            query, key_rows, value_rows = (
                rows_of(qkv, rel, slice(k * part + base, k * part + base + 2 * HEAD_DIM))
                for k in range(3)
            )
            probs = pair_probs(query, pair_of_heads(key_rows, low), mask)
            value = matmul(probs.astype(BF16), pair_of_heads(value_rows, low))
            put_rows(mixed, rel, slice(base, base + 2 * HEAD_DIM), value.astype(BF16))


def attend_local(place, table, qkv):
    rows, wide = qkv[0].shape[-2:]
    return kernel_call(
        attend_kernel,
        "attend",
        [(SMEM, place), (MOVED, table), moved(*qkv)],
        [block_shapes(rows * POS, wide // 3, True)],
    )[0]


def attend_back_kernel(ready, place, table, qkv, d_mixed, d_qkv):
    qkv, d_mixed, d_qkv = (views(blocks, place) for blocks in (qkv, d_mixed, d_qkv))
    part = d_mixed[0].shape[1]
    pair = 2 * HEAD_DIM
    low = first_head_lanes()
    size = POS * d_mixed[0].shape[0] // 2
    low_full = lax.broadcasted_iota(jnp.int32, (size, pair), 1) < HEAD_DIM
    scale = HEAD_DIM ** (-0.5)
    ready()
    for rel in range(2):
        mask = allowed_pairs(table[2 + rel : 3 + rel, 0:size], place[POSITION])
        for base in range(0, part, pair):
            query, key_rows, value_rows = (
                rows_of(qkv, rel, slice(k * part + base, k * part + base + pair))
                for k in range(3)
            )
            d_rows = rows_of(d_mixed, rel, slice(base, base + pair))
            keys = pair_of_heads(key_rows, low)
            probs = pair_probs(query, keys, mask)
            d_probs = times_transposed(d_rows, pair_of_heads(value_rows, low))
            inner = lane_halves(d_probs * probs, lambda a: jnp.sum(a, -1, keepdims=True))
            d_scores = (probs * (d_probs - inner)).astype(BF16)
            d_query = matmul(d_scores, keys) * scale
            d_key = inner_rows(d_scores, query) * scale
            d_value = inner_rows(probs.astype(BF16), d_rows)
            d_key = jnp.where(low_full, d_key[:size], d_key[size:])
            d_value = jnp.where(low_full, d_value[:size], d_value[size:])
            for k, value in enumerate((d_query, d_key, d_value)):
                columns = slice(k * part + base, k * part + base + pair)
                put_rows(d_qkv, rel, columns, value.astype(BF16))


def attend_back_local(place, table, qkv, d_mixed):
    rows, wide = qkv[0].shape[-2:]
    return kernel_call(
        attend_back_kernel,
        "attend_back",
        [(SMEM, place), (MOVED, table), moved(*qkv), in_vmem(*d_mixed)],
        [block_shapes(rows * POS, wide, True)],
    )[0]


def chip_rows(place, own, near, whole, sems):
    count = own.shape[0]
    core = place[CORE]
    return [
        pltpu.make_async_copy(own, whole.at[aligned(core * count, count, 64)], sems.at[0]),
        pltpu.make_async_copy(near, whole.at[aligned((1 - core) * count, count, 64)], sems.at[1]),
    ]


def out_kernel(ready, place, w_own, w_near, mixed, term, leaving, mixed_rows, w, sems):
    mixed = views(mixed, place)
    copies = chip_rows(place, w_own, w_near, w, sems)
    for copy in copies:
        copy.start()
    ready()
    rows = jnp.concatenate([rows_of(mixed, 0), rows_of(mixed, 1)], 0)
    mixed_rows[...] = rows
    half = rows.shape[0] // 2
    for copy in copies:
        copy.wait()
    for base in range(0, D, 512):
        value = matmul(rows, w[:, base : base + 512])
        term[:, base : base + 512] = value
        lowered = value.astype(BF16)
        leaving[:half, base : base + 512] = lowered[half:]
        leaving[half:, base : base + 512] = lowered[:half]


def out_term(place, mixed, w_own, w_near):
    rows = POS * mixed[0].shape[-2]
    inner = 2 * w_own.shape[0]
    return kernel_call(
        out_kernel,
        "out_term",
        [(SMEM, place), (EITHER, w_own), (EITHER, w_near), in_vmem(*mixed)],
        [((rows, D), F32), ((rows, D), BF16), ((rows, inner), BF16)],
        [pltpu.VMEM((inner, D), BF16), pltpu.SemaphoreType.DMA((2,))],
    )


def aside_kernel(ready, place, x_a, x_b, term, c_a, c_b, w_own, w_near, base, d_hidden, w, sems):
    copies = chip_rows(place, w_own, w_near, w, sems)
    for copy in copies:
        copy.start()
    ready()
    half = c_a.shape[0]
    for rel, ref in enumerate((x_a, x_b)):
        at = pl.ds(rel * half, half)
        base[at, :] = ref[:half, :].astype(F32) + term[at, :]
    upstream = jnp.concatenate([c_a[...], c_b[...]], 0)
    for copy in copies:
        copy.wait()
    inner = w.shape[0]
    for low in range(0, inner, 256):
        high = min(low + 256, inner)
        d_hidden[:, low:high] = times_transposed(upstream, w[low:high, :])


def aside(place, x_a, x_b, term, c_a, c_b, w_own, w_near):
    rows, inner = 2 * c_a.shape[0], 2 * w_own.shape[0]
    return kernel_call(
        aside_kernel,
        "aside",
        [(SMEM, place), (MOVED, x_a), (MOVED, x_b), (VMEM, term), (MOVED, c_a), (MOVED, c_b),
         (HBM, w_own), (HBM, w_near)],
        [((rows, D), F32), ((rows, inner), F32)],
        [pltpu.VMEM((inner, D), BF16), pltpu.SemaphoreType.DMA((2,))],
    )


def ffn_kernel(
    ready, place, base, far, table, d_hidden_all, *rest
):
    kept, near, far_a, across_a, far_b, across_b = rest[:6]
    resid, lowered, hidden, d_gate_up, second, leaving = rest[6:12]
    w, sems = rest[12:]
    half, width, steps = base.shape[0] // 2, kept.shape[0], w.shape[0]
    split = far_a.shape[1] // 256

    def begin(arrived, j, carry):
        sources = ((kept, OWN, 0), (near, NEAR, 0)) + arrived
        for source, rank, before in sources:
            pltpu.make_async_copy(
                source.at[:, aligned((j - before) * 256, 256)],
                w.at[j, aligned(place[rank] * width, width)],
                sems.at[j, rank],
            ).start()
        return carry

    for low, high, far_part, across_part in (
        (0, split, far_a, across_a), (split, steps, far_b, across_b)
    ):
        arrived = ((far_part, FAR, low), (across_part, ACROSS, low))
        lax.fori_loop(low, high, functools.partial(begin, arrived), 0)
    ready()
    gain = table[1:2, :]
    for rel in range(2):
        at = pl.ds(rel * half, half)
        rows = base[at, :] + far[at, :].astype(F32)
        resid[at, :] = rows
        scale = lax.rsqrt(jnp.mean(rows * rows, axis=-1, keepdims=True) + EPSILON)
        lowered[at, :] = (rows * scale * gain).astype(BF16)

    def step(j, carry):
        for rank in range(4):
            rows = w.at[j, pl.ds(rank * width, width)]
            pltpu.make_async_copy(rows, rows, sems.at[j, rank]).wait()
        gate_up = matmul(lowered[...], w[j])
        gate, up = gate_up[:, :128], gate_up[:, 128:]
        d_hidden = d_hidden_all[:, aligned(j * 128, 128)]
        sigmoid = jax.nn.sigmoid(gate)
        activated = gate * sigmoid
        hidden[:, aligned(j * 128, 128)] = (activated * up).astype(BF16)
        d_gate = d_hidden * up * sigmoid * (1.0 + gate * (1.0 - sigmoid))
        d_gate_up[:, aligned(j * 256, 128)] = d_gate.astype(BF16)
        d_gate_up[:, aligned(j * 256 + 128, 128)] = (d_hidden * activated).astype(BF16)
        return carry

    lax.fori_loop(0, steps, step, 0)

    def back(n, carry):
        columns = aligned(n * 256, 256)
        value = times_transposed(d_gate_up[:, 0:256], w[0, columns, :])
        for j in range(1, steps):
            value += times_transposed(d_gate_up[:, j * 256 : (j + 1) * 256], w[j, columns, :])
        second[:, columns] = value
        lower = value.astype(BF16)
        leaving[:half, columns] = lower[half:]
        leaving[half:, columns] = lower[:half]
        return carry

    lax.fori_loop(0, D // 256, back, 0)


def ffn(place, base, far, table, d_hidden, pieces):
    rows, inner = d_hidden.shape
    wide, steps = 2 * inner, inner // 128
    return kernel_call(
        ffn_kernel,
        "ffn",
        [(SMEM, place)]
        + in_vmem(base, far) + moved(table) + in_vmem(d_hidden)
        + [(HBM if n in (0, 3, 5) else EITHER, a) for n, a in enumerate(pieces)],
        [((rows, D), F32), ((rows, D), BF16), ((rows, inner), BF16), ((rows, wide), BF16),
         ((rows, D), F32), ((rows, D), BF16)],
        [pltpu.VMEM((steps, D, 256), BF16), pltpu.SemaphoreType.DMA((steps, 4))],
    )


def down_kernel(ready, place, hidden, resid, w_own, w_near, kept, leaving, w, sems):
    copies = chip_rows(place, w_own, w_near, w, sems)
    for copy in copies:
        copy.start()
    half = kept.shape[0]
    ready()
    for copy in copies:
        copy.wait()

    def step(n, carry):
        columns = aligned(n * 256, 256)
        value = matmul(hidden[...], w[:, columns])
        kept[:, columns] = resid[:half, columns] + value[:half]
        leaving[:, columns] = value[half:].astype(BF16)
        return carry

    lax.fori_loop(0, D // 256, step, 0)


def down_term(place, hidden, resid, w_own, w_near):
    rows, inner = hidden.shape
    return kernel_call(
        down_kernel,
        "down_term",
        [(SMEM, place), (MOVED, hidden), (VMEM, resid), (EITHER, w_own), (EITHER, w_near)],
        [((rows // 2, D), F32), ((rows // 2, D), BF16)],
        [pltpu.VMEM((inner, D), BF16), pltpu.SemaphoreType.DMA((2,))],
    )


def mid_kernel(
    ready, place, second, far, resid, gains, c_a, c_b, w_own, w_near,
    d_resid_out, d_branch, gain_terms, d_mixed, d_resid, w, sums, sems,
):
    d_mixed = views(d_mixed, place)
    copies = chip_rows(place, w_own, w_near, w, sems)
    for copy in copies:
        copy.start()
    half, width = c_a.shape[0], w_own.shape[0]
    total = None
    for rel in range(2):
        at = pl.ds(rel * half, half)
        rows = resid[at, :]
        scale = lax.rsqrt(jnp.mean(rows * rows, axis=-1, keepdims=True) + EPSILON)
        d_rows = second[at, :] + far[at, :].astype(F32)
        part = jnp.sum(d_rows * (rows * scale), axis=0, keepdims=True)
        total = part if total is None else total + part
    ready()
    gain = gains[1:2, :]
    for rel, c_ref in enumerate((c_a, c_b)):
        at = pl.ds(rel * half, half)
        rows = resid[at, :]
        scale = lax.rsqrt(jnp.mean(rows * rows, axis=-1, keepdims=True) + EPSILON)
        normed = rows * scale
        scaled = (second[at, :] + far[at, :].astype(F32)) * gain
        value = c_ref[...].astype(F32) + scale * (
            scaled - normed * jnp.mean(scaled * normed, axis=-1, keepdims=True)
        )
        if rel == 0:
            d_resid[...] = value
            leaving = pltpu.make_async_copy(d_resid, d_resid_out, sems.at[2])
            leaving.start()
        d_branch[at, :] = value.astype(BF16)
    sums[...] = total
    gain_terms[0] = sums[:, aligned(place[OWN] * width, width)]
    gain_terms[1] = sums[:, aligned(place[NEAR] * width, width)]
    for copy in copies:
        copy.wait()
    for base in range(0, w.shape[0], 256):
        value = times_transposed(d_branch[...], w[base : base + 256, :]).astype(BF16)
        put_rows(d_mixed, 0, slice(base, base + 256), value[:half])
        put_rows(d_mixed, 1, slice(base, base + 256), value[half:])
    leaving.wait()


def mid(place, second, far, resid, gains, c_a, c_b, w_own, w_near):
    rows = second.shape[0]
    width = w_own.shape[0]
    return kernel_call(
        mid_kernel,
        "mid",
        [(SMEM, place), (VMEM, second), (VMEM, far), (VMEM, resid), (MOVED, gains),
         (MOVED, c_a), (MOVED, c_b), (EITHER, w_own), (EITHER, w_near)],
        [((rows // 2, D), F32, HBM), ((rows, D), BF16), ((2, 1, width), F32),
         block_shapes(rows, 2 * width, True)],
        [pltpu.VMEM((rows // 2, D), F32), pltpu.VMEM((2 * width, D), BF16),
         pltpu.VMEM((1, D), F32), pltpu.SemaphoreType.DMA((3,))],
    )


def back_first_kernel(
    ready, place, w_own, w_far, w_near, w_across, d_qkv, kept, leaving, rows, w, sems
):
    d_qkv = views(d_qkv, place)
    half, width = kept.shape[0], w_own.shape[0]
    part = w.shape[2] // 3
    side = place[SIDE]
    copies = [
        pltpu.make_async_copy(
            w_own.at[:, aligned((2 * k + side) * part, part)],
            w.at[0, :, pl.ds(k * part, part)],
            sems.at[k],
        )
        for k in range(3)
    ]
    copies.append(pltpu.make_async_copy(w_far, w.at[1], sems.at[3]))
    copies.append(pltpu.make_async_copy(w_near, w.at[2], sems.at[4]))
    copies.append(pltpu.make_async_copy(w_across, w.at[3], sems.at[5]))
    for copy in copies:
        copy.start()
    ready()
    rows[:half, :] = rows_of(d_qkv, 0)
    rows[half:, :] = rows_of(d_qkv, 1)
    for rank in range(4):
        for copy in copies[:3] if rank == 0 else copies[rank + 2 : rank + 3]:
            copy.wait()
        columns = aligned(place[rank] * width, width)
        value = times_transposed(rows[...], w[rank])
        kept[:, columns] = value[:half]
        leaving[:, columns] = value[half:].astype(BF16)


def back_first(place, d_qkv, w_own, w_far, w_near, w_across):
    rows, wide = POS * d_qkv[0].shape[-2], d_qkv[0].shape[-1]
    return kernel_call(
        back_first_kernel,
        "back_first",
        [(SMEM, place), (HBM, w_own), (HBM, w_far), (HBM, w_near), (HBM, w_across),
         in_vmem(*d_qkv)],
        [((rows // 2, D), F32), ((rows // 2, D), BF16), ((rows, wide), BF16)],
        [pltpu.VMEM((4, w_own.shape[0], wide), BF16), pltpu.SemaphoreType.DMA((6,))],
    )


def last_kernel(
    ready, place, kept, far, x_a, gains, d_resid, down_kept, down_far, blocks, gain_terms, sums
):
    ready()
    blocks = views(blocks, place)
    width = gain_terms.shape[2]
    rows = x_a[: kept.shape[0], :].astype(F32)
    scale = lax.rsqrt(jnp.mean(rows * rows, axis=-1, keepdims=True) + EPSILON)
    normed = rows * scale
    d_rows = kept[...] + far[...].astype(F32)
    sums[...] = jnp.sum(d_rows * normed, axis=0, keepdims=True)
    scaled = d_rows * gains[0:1, :]
    value = d_resid[...] + scale * (
        scaled - normed * jnp.mean(scaled * normed, axis=-1, keepdims=True)
    )
    put_rows(blocks, 0, slice(None), value.astype(BF16))
    put_rows(blocks, 1, slice(None), (down_kept[...] + down_far[...].astype(F32)).astype(BF16))
    for slot, rank in enumerate((OWN, NEAR, FAR, ACROSS)):
        gain_terms[slot] = sums[:, aligned(place[rank] * width, width)]


def last(place, kept, far, x_a, gains, d_resid, down_kept, down_far):
    half = kept.shape[0]
    return kernel_call(
        last_kernel,
        "last",
        [(SMEM, place)]
        + in_vmem(kept, far)
        + moved(x_a, gains, d_resid, down_kept)
        + in_vmem(down_far),
        [block_shapes(2 * half, D, True), ((4, 1, D // 4), F32)],
        [pltpu.VMEM((1, D), F32)],
    )


def both_rows(own, near, columns):
    return jnp.concatenate([own[:, columns], near[:, columns]], 0)


def leaving_kernel(
    target, ready, place, left_own, left_near, right_own, right_near, leaving
):
    ready()
    width = leaving.shape[0]
    left = both_rows(left_own, left_near, aligned(place[target] * width, width)).T

    def step(j, carry):
        columns = aligned(j * 256, 256)
        right = both_rows(right_own, right_near, columns)
        leaving[:, columns] = matmul(left, right).astype(BF16)
        return carry

    lax.fori_loop(0, leaving.shape[1] // 256, step, 0)


def leaving_gradient(place, target, left_own, left_near, right_own, right_near):
    width, wide = D // 4, right_own.shape[1]
    return kernel_call(
        functools.partial(leaving_kernel, target),
        "leaving_gradient",
        [(SMEM, place)] + moved(left_own, left_near, right_own, right_near),
        [((width, wide), BF16)],
    )[0]


def put_stripe(parts, stripes, block, value):
    if parts == 2:
        at = aligned(block * 128, 128)
        stripes[0, :, at] = value[:, :128]
        stripes[1, :, at] = value[:, 128:]
    else:
        stripes[block // 2, :, aligned((block % 2) * 256, 256)] = value


def stripe_copies(who, stripes, grad, sems):
    parts, _, part = stripes.shape
    return [
        pltpu.make_async_copy(
            stripes.at[k], grad.at[:, aligned((2 * k + who) * part, part)], sems.at[k]
        )
        for k in range(parts)
    ]


def write_stripes(who, stripes, grad, sems):
    copies = stripe_copies(who, stripes, grad, sems)
    for copy in copies:
        copy.start()
    for copy in copies:
        copy.wait()


def staying_kernel(
    ready, place, left_own, left_near, right_own, right_near, grad, stripes, sems
):
    ready()
    parts, width, _ = stripes.shape
    left = both_rows(left_own, left_near, aligned(place[OWN] * width, width)).T

    def step(j, carry):
        right = both_rows(right_own, right_near, aligned(j * 256, 256))
        put_stripe(parts, stripes, j, matmul(left, right))
        return carry

    lax.fori_loop(0, right_own.shape[1] // 256, step, 0)
    write_stripes(place[SIDE], stripes, grad, sems)


def staying_gradient(parts, place, left_own, left_near, right_own, right_near):
    width, wide = D // 4, right_own.shape[1]
    return kernel_call(
        staying_kernel,
        "staying_gradient",
        [(SMEM, place)] + in_stage(left_own, left_near, right_own, right_near),
        [((width, 2 * wide), F32, HBM)],
        [pltpu.VMEM((parts, width, wide // parts), F32), pltpu.SemaphoreType.DMA((parts,))],
    )[0]


def coming_kernel(ready, place, come, before, grad, stripes, sems):
    ready()
    parts, _, part = stripes.shape
    copies = stripe_copies(1 - place[SIDE], stripes, grad, sems)
    for k, copy in enumerate(copies):
        for j in range(come.shape[1] // 256):
            if parts == 2:
                at = j * 256 + k * 128
                stripes[k, :, j * 128 : (j + 1) * 128] = come[:, at : at + 128].astype(F32)
            elif j // 2 == k:
                at = slice((j % 2) * 256, (j % 2) * 256 + 256)
                stripes[k, :, at] = come[:, j * 256 : (j + 1) * 256].astype(F32)
        copy.start()
    for copy in copies:
        copy.wait()


def with_coming(parts, place, come, grad):
    width, wide = come.shape
    return kernel_call(
        coming_kernel,
        "coming_gradient",
        [(SMEM, place), (MOVED, come), (HBM, grad)],
        [(grad.shape, F32, HBM)],
        [pltpu.VMEM((parts, width, wide // parts), F32), pltpu.SemaphoreType.DMA((parts,))],
        aliases=((2, 0),),
    )[0]


def grad_out_kernel(ready, place, mixed_own, mixed_near, d_own, d_near, grad):
    ready()
    left = both_rows(
        mixed_own, mixed_near, aligned(place[CORE] * grad.shape[0], grad.shape[0])
    )
    for base in range(0, D, 512):
        at = slice(base, base + 512)
        grad[:, at] = inner_rows(left, jnp.concatenate([d_own[:, at], d_near[:, at]], 0))


def grad_out_rows(place, mixed_own, mixed_near, d_own, d_near):
    width = mixed_own.shape[1] // 2
    return kernel_call(
        grad_out_kernel,
        "grad_out",
        [(SMEM, place)] + in_stage(mixed_own, mixed_near, d_own, d_near),
        [((width, D), F32)],
    )[0]


def grad_down_kernel(ready, place, h_own, h_near, ca_own, cb_own, ca_near, cb_near, grad, wide):
    ready()
    count, window = grad.shape[0], wide.shape[0]
    core = place[CORE]
    skip = h_own.shape[1] - window
    left = both_rows(h_own, h_near, aligned(core * skip, window))

    def step(n, carry):
        columns = aligned(n * 256, 256)
        right = jnp.concatenate(
            [ref[:, columns] for ref in (ca_own, cb_own, ca_near, cb_near)], 0
        )
        wide[:, columns] = inner_rows(left, right)
        return carry

    lax.fori_loop(0, D // 256, step, 0)
    grad[...] = wide[aligned(core * (count - skip), count, 64), :]


def grad_down_rows(place, h_own, h_near, ca_own, cb_own, ca_near, cb_near):
    count = h_own.shape[1] // 2
    window = -(-count // 128) * 128
    return kernel_call(
        grad_down_kernel,
        "grad_down",
        [(SMEM, place)] + moved(h_own, h_near, ca_own, cb_own, ca_near, cb_near),
        [((count, D), F32)],
        [pltpu.VMEM((window, D), F32)],
    )[0]


def side_columns(weight, half, side, sems):
    part = half.shape[1] // 3
    return [
        pltpu.make_async_copy(
            weight.at[:, aligned((2 * k + side) * part, part)],
            half.at[:, pl.ds(k * part, part)],
            sems.at[k],
        )
        for k in range(3)
    ]


def kept_columns_kernel(ready, place, weight, half, sems):
    copies = side_columns(weight, half, place[SIDE], sems)
    for copy in copies:
        copy.start()
    for copy in copies:
        copy.wait()


def kept_columns(place, weight):
    count, width = weight.shape
    return kernel_call(
        kept_columns_kernel,
        "kept_columns",
        [(SMEM, place), (HBM, weight)],
        [((count, width // 2), BF16)],
        [pltpu.SemaphoreType.DMA((3,))],
    )[0]


def spread_kernel(split, ready, place, weight, kept, leaving_a, leaving_b, sems):
    part = weight.shape[1] // 4
    side = place[SIDE]
    copies = []
    for k in range(2):
        for j in range(part // 128):
            leaving, at = (leaving_a, j) if j < split else (leaving_b, j - split)
            for who, target, spot in ((side, kept, j), (1 - side, leaving, at)):
                copies.append(
                    pltpu.make_async_copy(
                        weight.at[:, aligned((2 * k + who) * part + j * 128, 128)],
                        target.at[:, pl.ds(spot * 256 + k * 128, 128)],
                        sems.at[len(copies)],
                    )
                )
    for copy in copies:
        copy.start()
    for copy in copies:
        copy.wait()


def spread(place, weight, split):
    count, width = weight.shape
    return kernel_call(
        functools.partial(spread_kernel, split),
        "spread",
        [(SMEM, place), (HBM, weight)],
        [((count, size), BF16) for size in (width // 2, 256 * split, width // 2 - 256 * split)],
        [pltpu.SemaphoreType.DMA((width // 128,))],
    )


def sync(*values):
    return lax.optimization_barrier(values)


def after(value, *earlier):
    return lax.optimization_barrier((value,) + earlier)[0]


def pair_body(frames_in, segment_ids, gain_attn, w_qkv, w_out, gain_ffn, w_gate_up, w_down, cotangent):
    member = lax.axis_index("fsdp") % 4
    side, core = member >> 1, member & 1
    position = lax.axis_index("fsdp") // 4
    place = jnp.stack([member, member ^ 2, member ^ 1, member ^ 3, side, core, position])
    place = place.astype(jnp.int32)
    frames = frames_in.shape[0] // POS
    half = POS * frames

    near = lambda rows: swap(rows, 1)

    x_sent, c_sent, qkv_leaving = to_positions(place, frames_in, cotangent, w_qkv)
    qkv_across = swap(qkv_leaving, 3)
    qkv_far = near(qkv_across)
    x_came = exchange(x_sent)
    ids_own = segment_ids.reshape(frames, POS).T
    ids_own = jnp.take(ids_own, jnp.arange(POS) ^ position, axis=0).reshape(1, half)
    gains_own = jnp.stack([gain_attn, gain_ffn])
    gains_near = near(after(gains_own, qkv_leaving))
    qkv_kept = kept_columns(place, after(w_qkv, qkv_leaving))
    w_kept, leaving_a, leaving_b = spread(place, after(w_gate_up, qkv_leaving), 3)
    x_came, ids_own, gains_near, qkv_kept, w_kept, leaving_a, leaving_b = sync(
        x_came, ids_own, gains_near, qkv_kept, w_kept, leaving_a, leaving_b
    )

    x_own = collect(place, x_came, ids_own, gains_own, gains_near)
    x_far = near(swap(x_own, 3))
    qkv_near = near(qkv_kept)
    c_came = exchange([after(c_sent[0], x_own)])
    across_a = swap(after(leaving_a, x_own), 3)
    x_far, qkv_far, qkv_near, leaving_b = sync(x_far, qkv_far, qkv_near, leaving_b)

    across_b = swap(leaving_b, 3)
    qkv_sent, lowered_first, table = first(
        place, x_own, x_far, w_qkv, qkv_far, qkv_near, qkv_across
    )
    qkv_sent, c_came, across_a = sync(qkv_sent, c_came, across_a)
    c_own = collect_rows(place, c_came)
    out_near, down_near = (near(after(a, lowered_first)) for a in (w_out, w_down))
    qkv, out_near, down_near, c_own = sync(exchange(qkv_sent), out_near, down_near, c_own)

    mixed_sent = attend_local(place, table, qkv)
    c_far = swap(after(c_own, mixed_sent[0]), 2)
    c_own_near, lowered_first_near = (
        near(after(a, mixed_sent[0])) for a in (c_own, lowered_first)
    )
    mixed, across_b, c_far, c_own_near, lowered_first_near = sync(
        exchange(mixed_sent), across_b, c_far, c_own_near, lowered_first_near
    )

    term, leaving, mixed = out_term(place, mixed, w_out, out_near)
    far = swap(leaving, 2)
    base, d_hidden = aside(
        place, x_own, x_far, term, c_own, after(c_far, leaving), w_down, down_near
    )
    mixed_near, far_a, far_b, w_near, c_far_near = (
        near(after(a, leaving)) for a in (mixed, across_a, across_b, w_kept, c_far)
    )
    far, base, d_hidden, mixed_near, far_a, far_b, w_near, c_far_near = sync(
        far, base, d_hidden, mixed_near, far_a, far_b, w_near, c_far_near
    )
    resid, lowered_second, hidden, d_gate_up, second, leaving = ffn(
        place, base, far, table, d_hidden, (w_kept, w_near, far_a, across_a, far_b, across_b)
    )

    second_far = swap(leaving, 2)
    hidden_near, lowered_second_near, d_gate_up_near = (
        near(after(rows, leaving)) for rows in (hidden, lowered_second, d_gate_up)
    )
    down_kept, down_leaving = down_term(place, after(hidden, leaving), resid, w_down, down_near)
    sides = (lowered_second, lowered_second_near, d_gate_up, d_gate_up_near)
    gate_up_leaving = leaving_gradient(place, ACROSS, *sides)
    second_far, down_leaving, gate_up_leaving, hidden_near, lowered_second_near = sync(
        second_far, down_leaving, gate_up_leaving, hidden_near, lowered_second_near
    )

    gate_up_come = swap(gate_up_leaving, 3)
    d_resid, d_branch, gain_ffn_terms, d_mixed = mid(
        place, second, second_far, resid, table, c_own, c_far, w_out, out_near
    )
    d_branch_near, gain_ffn_near = near(d_branch), near(gain_ffn_terms[1])
    grad_gate_up = staying_gradient(2, place, after(lowered_second, d_branch), *sides[1:])
    d_mixed, d_branch_near, gain_ffn_near, grad_gate_up = sync(
        exchange(d_mixed), d_branch_near, gain_ffn_near, grad_gate_up
    )

    d_qkv_sent = attend_back_local(place, table, qkv, d_mixed)
    grad_down = grad_down_rows(
        place, after(hidden, d_qkv_sent[0]), hidden_near, c_own, c_far, c_own_near, c_far_near
    )
    grad_out = grad_out_rows(place, mixed, mixed_near, after(d_branch, d_qkv_sent[0]), d_branch_near)
    down_far = swap(after(down_leaving, d_qkv_sent[0]), 2)
    d_qkv, gate_up_come, down_far, grad_down, grad_out = sync(
        exchange(d_qkv_sent), gate_up_come, down_far, grad_down, grad_out
    )

    kept, leaving, d_projected = back_first(
        place, d_qkv, w_qkv, qkv_far, qkv_near, qkv_across
    )
    first_far = swap(leaving, 2)
    qkv_sides = (lowered_first, lowered_first_near, d_projected, near(d_projected))
    first_far, qkv_leaving = sync(first_far, leaving_gradient(place, FAR, *qkv_sides))
    qkv_across_come = swap(qkv_leaving, 3)

    out_sent, gain_attn_terms = last(
        place, kept, first_far, x_own, table, d_resid, down_kept, down_far
    )
    grad_gate_up = with_coming(2, place, after(gate_up_come, gain_attn_terms), grad_gate_up)
    grad_qkv = staying_gradient(3, place, after(lowered_first, gain_attn_terms), *qkv_sides[1:])
    gain_sums = gain_attn_terms[:2] + swap(gain_attn_terms[2:], 2)
    gain_attn_grad = gain_sums[0] + near(gain_sums[1])
    qkv_come = near(after(qkv_across_come, grad_gate_up, grad_qkv))
    grad_qkv = with_coming(3, place, qkv_come, grad_qkv)
    out_come, grad_gate_up, grad_qkv = sync(exchange(out_sent), grad_gate_up, grad_qkv)
    grad_in, block_out = to_frames(place, out_come)
    gain_ffn_grad = (gain_ffn_terms[0] + gain_ffn_near).reshape(-1)
    return (
        block_out,
        grad_in,
        gain_attn_grad.reshape(-1),
        grad_qkv,
        grad_out,
        gain_ffn_grad,
        grad_gate_up,
        grad_down,
    )


def solution(mesh):
    in_specs = (
        P("fsdp", None),
        P("fsdp"),
        P("fsdp"),
        P("fsdp", None),
        P("fsdp", None),
        P("fsdp"),
        P("fsdp", None),
        P("fsdp", None),
        P("fsdp", None),
    )
    out_specs = (
        P("fsdp", None),
        P("fsdp", None),
        P("fsdp"),
        P("fsdp", None),
        P("fsdp", None),
        P("fsdp"),
        P("fsdp", None),
        P("fsdp", None),
    )
    chosen = pair_body if mesh.shape["fsdp"] == 4 * POS else body
    return jax.shard_map(chosen, mesh=mesh, in_specs=in_specs, out_specs=out_specs, check_vma=False)
```
